512 devices in a mesh: spk: 16 (over y_lo, x, core), pts: 32 (over y_hi, z).
Axes of the slice: x: 4, y: 4 (y_hi: 2, y_lo: 2; y = y_hi * 2 + y_lo), z: 16, core: 2. Of those that a mesh axis runs over, the one named last changes fastest.
Arguments:
- desired: float32 [2, 8, 8192], P(None, None, 'pts'), may hold values from -6 to 6
- spk_cells: int32 [4096], replicated, may hold values from 0 to 4095, each once
- pt_cells: float32 [3, 8192], P(None, 'pts'), may hold values from 0 to 1
- eval_cells: float32 [3, 65536], P(None, ('spk', 'pts')), may hold values from 0 to 1
- wavenumber: float32 [1], replicated, may hold values from 15 to 25
Outputs:
- drives: float32 [2, 8, 4096], P(None, None, 'spk')
- residual: float32 [2, 8, 8192], P(None, None, 'pts')
- field: float32 [2, 8, 65536], P(None, None, ('spk', 'pts'))
The draws below stay inside these ranges and needn't reach their ends.
Inputs may be any that keep to these rules, and one draw needn't show every extreme that they name: `spk_cells`: each cell of the 64 x 64 wall holds exactly one loudspeaker.
All inputs are finite; a program needn't handle non-finite values.
Results may differ from the reference program's by a relative error of at most 0.0003.
Values sent between devices are 32-bit elements; how exact they have to be, the bound alone decides.
No kernel may reach another device: no remote copies, remote signals or barrier semaphores. Data moves between devices by JAX's collectives and lax.ppermute only.
A program may use at most 64 MiB of HBM per device.

```python
import jax
import jax.numpy as jnp
from jax import lax

WALL = 64
SPEAKERS = 4096
FIELDS = 8
PTS_DEV = 256
ITERS = 2
POINTS = 8192
EVALS = 65536


def draw_pt_cells(key, part):
    first = jax.random.fold_in(key, 11)
    second = jax.random.fold_in(key, 12)
    index = jnp.arange(POINTS)
    shard = (index // PTS_DEV).astype(jnp.float32)
    within = (index % PTS_DEV).astype(jnp.float32)
    jitter = jax.random.uniform(first, (2, POINTS), jnp.float32)
    sides = jax.random.uniform(second, (2, POINTS), jnp.float32)
    depth = 0.5 * (shard + jitter[0]) / (POINTS // PTS_DEV) + 0.5 * (within + jitter[1]) / PTS_DEV
    depth = jnp.clip(depth, 0.0, 1.0)
    sides = jnp.clip(sides, 0.0, 1.0)
    return jnp.concatenate([depth[None, :], sides], axis=0).astype(jnp.float32)


def steps_of(rng, extent, split, smallest, high):
    def one(axis_at, parts):
        draws = jax.random.uniform(jax.random.fold_in(jax.random.fold_in(rng, 6), axis_at), (parts,), jnp.float32, smallest / len(split), high / len(split))
        return jnp.repeat(jnp.exp(draws), extent[axis_at] // parts).reshape((-1,) + (1,) * (len(extent) - axis_at - 1))

    level = one(*split[0])
    for cut in split[1:]:
        level = level * one(*cut)
    return level


def bell_draw(key, dims, scale, bound, cuts=(), dtype=jnp.bfloat16):
    drawn = scale * jax.random.normal(key, dims, jnp.float32)
    if cuts:
        drawn = drawn * steps_of(key, dims, cuts, -0.22, 0.18)
    return jnp.clip(drawn, -bound, bound).astype(dtype)


def setup_inputs(seed: int = 0) -> dict:
    key_of = jax.random.split(jax.random.key(seed), 6)
    return {
        "desired": bell_draw(key_of[0], (2, FIELDS, POINTS), 1.0, 6.0, ((2, 32),), jnp.float32),
        "spk_cells": jax.random.permutation(key_of[1], SPEAKERS).astype(jnp.int32),
        "pt_cells": draw_pt_cells(jax.random.fold_in(key_of[5], 71), 0),
        "eval_cells": jnp.clip(1.0 * jax.random.uniform(key_of[3], (3, EVALS), jnp.float32) ** steps_of(key_of[3], (3, EVALS), ((1, 512),), -0.2, 0.2), 0.0, 1.0),
        "wavenumber": jnp.clip(jax.random.uniform(key_of[4], (1,), jnp.float32, 15.0, 25.0), 15.0, 25.0),
    }


wall_pitch = 0.05
front_gap = 0.5
depth_span = 3.15
side_span = 3.2
tikhonov = 0.1

def green_tile(wall_cells, point_cells, wavenumber):
    centre = (WALL - 1) * 0.5
    wall_row = (wall_cells // WALL).astype(jnp.float32)
    wall_col = (wall_cells % WALL).astype(jnp.float32)
    wall_y = (wall_row - centre) * wall_pitch
    wall_z = (wall_col - centre) * wall_pitch
    coords = point_cells
    offset_x = front_gap + coords[0] * depth_span
    offset_y = coords[1] * side_span - 0.5 * side_span
    offset_z = coords[2] * side_span - 0.5 * side_span
    delta_y = offset_y[:, None] - wall_y[None, :]
    delta_z = offset_z[:, None] - wall_z[None, :]
    distance = jnp.sqrt(offset_x[:, None] * offset_x[:, None] + delta_y * delta_y + delta_z * delta_z)
    magnitude = 1.0 / (WALL * distance)
    phases = wavenumber[0] * distance
    return (magnitude * jnp.cos(phases), -magnitude * jnp.sin(phases))

def contract_last(left, right):
    return lax.dot_general(left, right, (((1,), (1,)), ((), ())), precision=lax.Precision.HIGHEST)

def forward_tile(drives, green_real, green_imag):
    real_part = contract_last(drives[0], green_real) - contract_last(drives[1], green_imag)
    imag_part = contract_last(drives[0], green_imag) + contract_last(drives[1], green_real)
    return jnp.stack([real_part, imag_part])

def adjoint_tile(values, green_real, green_imag):
    highest = lax.Precision.HIGHEST
    real_part = jnp.dot(values[0], green_real, precision=highest) + jnp.dot(values[1], green_imag, precision=highest)
    imag_part = jnp.dot(values[1], green_real, precision=highest) - jnp.dot(values[0], green_imag, precision=highest)
    return jnp.stack([real_part, imag_part])

def pressure_all(drives, wall_cells, point_cells, wavenumber, block):
    count = point_cells.shape[1] // block
    grouped = point_cells.reshape(3, count, block).transpose(1, 0, 2)

    def single(cells):
        green_real, green_imag = green_tile(wall_cells, cells, wavenumber)
        return forward_tile(drives, green_real, green_imag)
    blocks = lax.map(single, grouped)
    return blocks.transpose(1, 2, 0, 3).reshape(2, drives.shape[1], count * block)

def gradient_all(values, wall_cells, point_cells, wavenumber, block):
    count = point_cells.shape[1] // block
    grouped = point_cells.reshape(3, count, block).transpose(1, 0, 2)
    pieces = values.reshape(2, values.shape[1], count, block).transpose(2, 0, 1, 3)

    def accumulate(total, item):
        cells, piece = item
        green_real, green_imag = green_tile(wall_cells, cells, wavenumber)
        return (total + adjoint_tile(piece, green_real, green_imag), None)
    start = jnp.zeros((2, values.shape[1], wall_cells.shape[0]), jnp.float32)
    total, unused = lax.scan(accumulate, start, (grouped, pieces))
    return total

def reference(desired, spk_cells, pt_cells, eval_cells, wavenumber):
    drives = jnp.zeros((2, desired.shape[1], spk_cells.shape[0]), jnp.float32)
    residual = desired
    gradient = gradient_all(residual, spk_cells, pt_cells, wavenumber, PTS_DEV)
    direction = gradient
    gamma_now = lax.optimization_barrier(jnp.sum(gradient * gradient, axis=(0, 2)))
    for iteration in range(ITERS):
        image = pressure_all(direction, spk_cells, pt_cells, wavenumber, PTS_DEV)
        delta = lax.optimization_barrier(jnp.sum(image * image, axis=(0, 2))) + tikhonov * lax.optimization_barrier(jnp.sum(direction * direction, axis=(0, 2)))
        alpha = (gamma_now / delta)[None, :, None]
        drives = drives + alpha * direction
        residual = residual - alpha * image
        if iteration + 1 < ITERS:
            gradient = gradient_all(residual, spk_cells, pt_cells, wavenumber, PTS_DEV) - tikhonov * drives
            gamma_next = lax.optimization_barrier(jnp.sum(gradient * gradient, axis=(0, 2)))
            direction = gradient + (gamma_next / gamma_now)[None, :, None] * direction
            gamma_now = gamma_next
    field = pressure_all(drives, spk_cells, eval_cells, wavenumber, PTS_DEV)
    return (drives, residual, field)
```

```python
import functools
import math

import jax
import jax.numpy as jnp
from jax import lax
from jax.experimental import pallas as pl
from jax.experimental.pallas import tpu as pltpu
from jax.sharding import Mesh
from jax.sharding import PartitionSpec as P

WALL = 64
SPK = ("ylo", "x", "core")
PTS = ("yhi", "za", "zb", "zc")
FLD = ("za", "zb")
NEAR = ("yhi", "zc")

wall_pitch = 0.05
front_gap = 0.5
depth_span = 3.15
side_span = 3.2
tikhonov = 0.1

SIN = (4.442883014678955, -7.308245658874512, 3.606354236602783, -0.8461116552352905, 0.1098245158791542)
COS = (-1.4142135381698608, 6.978850841522217, -5.739460468292236, 1.883557915687561, -0.3106880187988281)
ROUNDER = 12582912.0

f32 = jnp.float32
bf16 = jnp.bfloat16


def spec(space=pltpu.VMEM):
    return pl.BlockSpec(memory_space=space)


def call(kernel, out_shapes, scratch, limit_mib, n_smem, n_in, name, flops, trans=0):
    return pl.pallas_call(
        kernel,
        out_shape=out_shapes,
        in_specs=[spec(pltpu.SMEM)] * n_smem + [spec()] * (n_in - n_smem),
        out_specs=jax.tree.map(lambda _: spec(), out_shapes),
        scratch_shapes=scratch,
        compiler_params=pltpu.CompilerParams(vmem_limit_bytes=limit_mib << 20),
        cost_estimate=pl.CostEstimate(flops=flops, bytes_accessed=1 << 20, transcendentals=trans),
        name=name,
    )


def poly(coeffs, u):
    out = coeffs[-1]
    for c in coeffs[-2::-1]:
        out = out * u + c
    return out


def green(scaled, strength):
    inverse = lax.rsqrt(scaled)
    turns = scaled * inverse
    magnitude = inverse * strength
    whole = (turns + ROUNDER) - ROUNDER
    frac = turns - whole
    u = frac * frac
    s = poly(SIN, u) * frac
    c = poly(COS, u)
    ms = magnitude * s
    return magnitude - ms * s, ms * c


def wall_rows(cells, kappa):
    centre = (WALL - 1) * 0.5
    row = jnp.right_shift(cells, 6).astype(f32)
    col = jnp.bitwise_and(cells, WALL - 1).astype(f32)
    return (row - centre) * (wall_pitch * kappa), (col - centre) * (wall_pitch * kappa)


def column(row):
    return jnp.broadcast_to(row, (128, 128)).T


def total(x):
    return jnp.broadcast_to(jnp.sum(x, keepdims=True), (1, 128))


def add_up(ref):
    out = ref[0]
    for i in range(1, ref.shape[0]):
        out = out + ref[i]
    return out


def split_bf16(x):
    high = x.astype(bf16)
    return high, (x - high.astype(f32)).astype(bf16)


def eval_green_kernel(wave_ref, cells_ref, eval_ref, high_ref, low_ref):
    kappa = wave_ref[0] * (0.5 / math.pi)
    strength = kappa * (1.0 / WALL)
    ex = column((front_gap + eval_ref[0:1, :] * depth_span) * kappa)
    ey = column((eval_ref[1:2, :] * side_span - 0.5 * side_span) * kappa)
    ez = column((eval_ref[2:3, :] * side_span - 0.5 * side_span) * kappa)
    ex2 = ex * ex

    def step(i, carry):
        wy, wz = wall_rows(cells_ref[pl.ds(i, 1), :], kappa)
        lanes = pl.ds(pl.multiple_of(i * 128, 128), 128)
        for part in range(2):
            rows = slice(part * 64, part * 64 + 64)
            dy = ey[rows] - wy
            dz = ez[rows] - wz
            real, imag = green(ex2[rows] + dy * dy + dz * dz, strength)
            rh, rl = split_bf16(real)
            ih, il = split_bf16(imag)
            high_ref[part * 64 : part * 64 + 64, lanes] = rh
            low_ref[part * 64 : part * 64 + 64, lanes] = rl
            high_ref[128 + part * 64 : 128 + part * 64 + 64, lanes] = ih
            low_ref[128 + part * 64 : 128 + part * 64 + 64, lanes] = il
        return carry

    lax.fori_loop(0, cells_ref.shape[0], step, 0)


def first_kernel(own_ref, wave_ref, cells_ref, got_ref, g_ref, send_ref, wall_ref, acc_ref):
    kappa = wave_ref[0] * (0.5 / math.pi)
    strength = kappa * (1.0 / WALL)
    for blk in range(2):
        wy, wz = wall_rows(cells_ref[pl.ds(own_ref[0] * 2 + blk, 1), :], kappa)
        wall_ref[0, blk * 128 : blk * 128 + 128, :] = column(wy)
        wall_ref[1, blk * 128 : blk * 128 + 128, :] = column(wz)
    size = 32

    def chunk(k, carry):
        rows = pl.ds(pl.multiple_of(k * size, size), size)
        wy = wall_ref[0, rows, :]
        wz = wall_ref[1, rows, :]

        def source(j, sums):
            real_sum, imag_sum = sums
            for half in range(2):
                lanes = slice(half * 128, half * 128 + 128)
                px = (front_gap + got_ref[j, 2:3, lanes] * depth_span) * kappa
                py = (got_ref[j, 3:4, lanes] * side_span - 0.5 * side_span) * kappa
                pz = (got_ref[j, 4:5, lanes] * side_span - 0.5 * side_span) * kappa
                vr = got_ref[j, 0:1, lanes]
                vi = got_ref[j, 1:2, lanes]
                dy = py - wy
                dz = pz - wz
                real, imag = green(px * px + dy * dy + dz * dz, strength)
                g_ref[j * 2 + half, 0, rows, :] = real
                g_ref[j * 2 + half, 1, rows, :] = imag
                real_sum = real_sum + (real * vr + imag * vi)
                imag_sum = imag_sum + (real * vi - imag * vr)
            return real_sum, imag_sum

        zero = jnp.zeros((size, 128), f32)
        real_sum, imag_sum = lax.fori_loop(0, got_ref.shape[0], source, (zero, zero))
        acc_ref[0, rows, :] = real_sum
        acc_ref[1, rows, :] = imag_sum
        return carry

    lax.fori_loop(0, 256 // size, chunk, 0)
    rows = rows_of(acc_ref)
    for i in range(send_ref.shape[0]):
        send_ref[i, 0:4, :] = rows


def rows_of(acc_ref):
    rows = []
    for part in range(2):
        for blk in range(2):
            block = acc_ref[part, blk * 128 : blk * 128 + 128, :]
            rows.append(jnp.sum(block.T, axis=0, keepdims=True))
    return jnp.concatenate(rows, axis=0)


def forward(g_ref, rows, col_ref, out_ref):
    for part in range(2):
        for blk in range(2):
            i = part * 2 + blk
            col_ref[part, blk * 128 : blk * 128 + 128, :] = column(rows[i : i + 1, :])
    size = 64

    def step(t, carry):
        real_sum = jnp.zeros((8, 128), f32)
        imag_sum = jnp.zeros((8, 128), f32)
        for k in range(256 // size):
            rows = slice(k * size, k * size + size)
            gr = g_ref[t, 0, rows, :]
            gi = g_ref[t, 1, rows, :]
            qr = col_ref[0, rows, :]
            qi = col_ref[1, rows, :]
            real_sum = real_sum + (gr * qr - gi * qi).reshape(size // 8, 8, 128).sum(axis=0)
            imag_sum = imag_sum + (gi * qr + gr * qi).reshape(size // 8, 8, 128).sum(axis=0)
        out_ref[pl.ds(t, 1), :] = jnp.sum(real_sum, axis=0, keepdims=True)
        out_ref[pl.ds(t + 16, 1), :] = jnp.sum(imag_sum, axis=0, keepdims=True)
        return carry

    lax.fori_loop(0, 16, step, 0)


def adjoint(g_ref, im_ref, acc_ref):
    size = 64

    def chunk(k, carry):
        rows = pl.ds(pl.multiple_of(k * size, size), size)
        real_sum = jnp.zeros((size, 128), f32)
        imag_sum = jnp.zeros((size, 128), f32)
        for t in range(16):
            vr = im_ref[t : t + 1, :]
            vi = im_ref[16 + t : 17 + t, :]
            gr = g_ref[t, 0, rows, :]
            gi = g_ref[t, 1, rows, :]
            real_sum = real_sum + (gr * vr + gi * vi)
            imag_sum = imag_sum + (gr * vi - gi * vr)
        acc_ref[0, rows, :] = real_sum
        acc_ref[1, rows, :] = imag_sum
        return carry

    lax.fori_loop(0, 256 // size, chunk, 0)
    return rows_of(acc_ref)


def image_kernel(g_ref, got_ref, send_ref, own_ref, col_ref, im_ref):
    g0 = add_up(got_ref)
    own_ref[...] = g0
    forward(g_ref, g0, col_ref, im_ref)
    message = jnp.concatenate([im_ref[...], g0, total(g0 * g0), jnp.zeros((3, 128), f32)], axis=0)
    for i in range(send_ref.shape[0]):
        send_ref[i] = message


def adjoint_kernel(g_ref, got_ref, send_ref, im_ref, acc_ref):
    whole = add_up(got_ref)
    im_ref[...] = whole
    rows = adjoint(g_ref, im_ref, acc_ref)
    im = whole[0:32, :]
    message = jnp.concatenate([rows, total(im * im), jnp.zeros((3, 128), f32)], axis=0)
    for i in range(send_ref.shape[0]):
        send_ref[i] = message


def second_image_kernel(g_ref, got_ref, g0_ref, im0_ref, send_ref, alpha_ref, col_ref, im_ref):
    whole = add_up(got_ref)
    g0 = g0_ref[...]
    gamma = im0_ref[36:37, :]
    alpha = gamma / (whole[4:5, :] + tikhonov * gamma)
    alpha_ref[...] = alpha
    g1 = g0 - alpha * (whole[0:4, :] + tikhonov * g0)
    forward(g_ref, g1, col_ref, im_ref)
    message = jnp.concatenate([im_ref[...], g1, total(g1 * g1), total(g1 * g0), jnp.zeros((2, 128), f32)], axis=0)
    for i in range(send_ref.shape[0]):
        send_ref[i] = message


def norm_kernel(got_ref, im0_ref, send_ref, im1_ref):
    whole = add_up(got_ref)
    gamma0 = im0_ref[36:37, :]
    gamma1 = whole[36:37, :]
    cross = whole[37:38, :]
    beta = gamma1 / gamma0
    im1 = whole[0:32, :] + beta * im0_ref[0:32, :]
    im1_ref[0:32, :] = im1
    im1_ref[32:33, :] = beta
    im1_ref[33:34, :] = gamma1
    im1_ref[34:35, :] = gamma1 + (2.0 * cross + beta * gamma0) * beta
    square = total(im1 * im1)
    for i in range(send_ref.shape[0]):
        send_ref[i] = square


def drive_kernel(got_ref, alpha_ref, im0_ref, im1_ref, first_ref, second_ref, send_ref):
    alpha0 = alpha_ref[...]
    beta = im1_ref[32:33, :]
    alpha1 = im1_ref[33:34, :] / (add_up(got_ref) + tikhonov * im1_ref[34:35, :])
    change = alpha0 * im0_ref[0:32, :] + alpha1 * im1_ref[0:32, :]
    from_first = alpha0 + alpha1 * beta
    for s in range(16):
        rows = from_first * first_ref[s, 32:36, :] + alpha1 * second_ref[s, 32:36, :]
        for i in range(send_ref.shape[0]):
            send_ref[i, 4 * s : 4 * s + 4, :] = rows
    for i in range(send_ref.shape[0]):
        send_ref[i, 64:66, :] = change[2 * i : 2 * i + 2, :]
        send_ref[i, 66:68, :] = change[16 + 2 * i : 18 + 2 * i, :]


def field_kernel(own_ref, got_ref, high_ref, low_ref, desired_ref, drives_ref, residual_ref, field_ref):
    own = own_ref[0]
    for part in range(2):
        for blk in range(2):
            lanes = slice(blk * 128, blk * 128 + 128)
            drives_ref[part, :, lanes] = got_ref[:, own * 4 + part * 2 + blk, :]
            residual_ref[part, :, lanes] = desired_ref[part, :, lanes] - got_ref[:, 64 + part * 2 + blk, :]
    out = jnp.zeros((32, 256), f32)
    fine = jnp.zeros((16, 256), f32)
    for s in range(16):
        lanes = slice(s * 256, s * 256 + 256)
        parts = [
            jnp.concatenate([got_ref[:, 4 * s + 2 * part + blk, :] for blk in range(2)], axis=1)
            for part in range(2)
        ]
        high, low = split_bf16(jnp.concatenate(parts, axis=0))
        both = jnp.concatenate([high, low], axis=0)
        dims = (((1,), (1,)), ((), ()))
        out = out + lax.dot_general(both, high_ref[:, lanes], dims, preferred_element_type=f32)
        fine = fine + lax.dot_general(high, low_ref[:, lanes], dims, preferred_element_type=f32)
    out = out[0:16, :] + out[16:32, :] + fine
    field_ref[0] = out[0:8, 0:128] - out[8:16, 128:256]
    field_ref[1] = out[0:8, 128:256] + out[8:16, 0:128]


def exchange(array, axes):
    return lax.all_to_all(array, axes, split_axis=0, concat_axis=0, tiled=True)


def shape(*dims, dtype=f32):
    return jax.ShapeDtypeStruct(dims, dtype)


def local(desired, spk_cells, pt_cells, eval_cells, wavenumber):
    cells = spk_cells.reshape(32, 128)
    own = lax.axis_index(SPK).astype(jnp.int32).reshape(1)
    vmem = pltpu.VMEM

    outgoing = jnp.concatenate(
        [desired.transpose(1, 0, 2), jnp.broadcast_to(pt_cells, (8, 3, 256))], axis=1
    )
    got0 = exchange(outgoing, FLD)
    high, low = call(
        eval_green_kernel,
        (shape(256, 4096, dtype=bf16), shape(256, 4096, dtype=bf16)),
        [], 12, 1, 3, "eval_green", 524288 * 40, 524288,
    )(wavenumber, cells, eval_cells)
    g, send1 = call(
        first_kernel,
        (shape(16, 2, 256, 128), shape(4, 4, 128)),
        [vmem((2, 256, 128), f32), vmem((2, 256, 128), f32)], 12, 2, 4, "first", 524288 * 48, 524288,
    )(own, wavenumber, cells, got0)
    got1 = exchange(send1, NEAR)
    send2, g0 = call(
        image_kernel,
        (shape(16, 40, 128), shape(4, 128)),
        [vmem((2, 256, 128), f32), vmem((32, 128), f32)], 12, 0, 2, "image", 524288 * 8,
    )(g, got1)
    got2 = exchange(send2, SPK)
    send3, im0 = call(
        adjoint_kernel,
        (shape(4, 8, 128), shape(40, 128)),
        [vmem((2, 256, 128), f32)], 12, 0, 2, "adjoint", 524288 * 8,
    )(g, got2)
    got3 = exchange(send3, NEAR)
    send4, alpha = call(
        second_image_kernel,
        (shape(16, 40, 128), shape(1, 128)),
        [vmem((2, 256, 128), f32), vmem((32, 128), f32)], 12, 0, 4, "second_image", 524288 * 8,
    )(g, got3, g0, im0)
    got4 = exchange(send4, SPK)
    send5, im1 = call(
        norm_kernel,
        (shape(4, 1, 128), shape(40, 128)),
        [], 8, 0, 2, "norm", 81920,
    )(got4, im0)
    got5 = exchange(send5, NEAR)
    send6 = call(
        drive_kernel,
        shape(8, 72, 128),
        [], 8, 0, 6, "drive", 81920,
    )(got5, alpha, im0, im1, got2, got4)
    got6 = exchange(send6, FLD)
    return call(
        field_kernel,
        (shape(2, 8, 256), shape(2, 8, 256), shape(2, 8, 128)),
        [], 12, 1, 5, "field", 524288 * 96,
    )(own, got6, high, low, desired)


def solution(mesh):
    split = Mesh(
        mesh.devices.reshape(2, 4, 2, 2, 4, 2, 2), ("ylo", "x", "core", "yhi", "za", "zb", "zc")
    )
    in_specs = (P(None, None, PTS), P(), P(None, PTS), P(None, SPK + PTS), P())
    out_specs = (P(None, None, SPK), P(None, None, PTS), P(None, None, SPK + PTS))
    return jax.shard_map(local, mesh=split, in_specs=in_specs, out_specs=out_specs, check_vma=False)
```

```python
import math

import jax
import jax.numpy as jnp
from jax import lax
from jax.experimental import pallas as pl
from jax.experimental.pallas import tpu as pltpu
from jax.sharding import Mesh
from jax.sharding import PartitionSpec as P

WALL = 64
SPK = ("ylo", "x", "core")
PTS = ("yhi", "za", "zb", "zc")
FLD = ("za", "zb")
BANKS = ("x", "core")
NEAR = ("ylo", "yhi", "zc")

wall_pitch = 0.05
front_gap = 0.5
depth_span = 3.15
side_span = 3.2
tikhonov = 0.1
centre = (WALL - 1) * 0.5

SIN = (4.442879676818848, -7.307816505432129, 3.5977742671966553, -0.7911993861198425)
COS = (-1.4142040014266968, 6.97763729095459, -5.715188026428223, 1.728213906288147)
ROUNDER = 12582912.0

f32 = jnp.float32
bf16 = jnp.bfloat16
vmem = pltpu.VMEM


def spec(space=pltpu.VMEM):
    return pl.BlockSpec(memory_space=space)


def shape(*dims, dtype=f32):
    return jax.ShapeDtypeStruct(dims, dtype)


WHOLE = 64
SPACES = {"s": pltpu.SMEM, "v": pltpu.VMEM, "a": pl.ANY}


def call(kernel, out_shapes, scratch, limit_mib, spaces, name, flops, trans=0):
    return pl.pallas_call(
        kernel,
        out_shape=out_shapes,
        in_specs=[spec(SPACES[c]) for c in spaces],
        out_specs=jax.tree.map(lambda _: spec(), out_shapes),
        scratch_shapes=scratch,
        compiler_params=pltpu.CompilerParams(vmem_limit_bytes=min(limit_mib << 20, 67043328)),
        cost_estimate=pl.CostEstimate(flops=flops, bytes_accessed=1 << 20, transcendentals=trans),
        name=name,
    )


def poly(coeffs, u):
    out = coeffs[-1]
    for c in coeffs[-2::-1]:
        out = out * u + c
    return out


def green(scaled, strength):
    inverse = lax.rsqrt(scaled)
    turns = scaled * inverse
    magnitude = inverse * strength
    whole = (turns + ROUNDER) - ROUNDER
    frac = turns - whole
    u = frac * frac
    s = poly(SIN, u) * frac
    c = poly(COS, u)
    ms = magnitude * s
    return magnitude - ms * s, ms * c


def column(row):
    return jnp.broadcast_to(row, (128, 128)).T


def total(x):
    return jnp.broadcast_to(jnp.sum(x, keepdims=True), (1, 128))


def fold(x):
    out = x[0]
    for i in range(1, x.shape[0]):
        out = out + x[i]
    return out


def split_bf16(x):
    high = x.astype(bf16)
    return high, (x - high.astype(f32)).astype(bf16)


def iota(dims, dim):
    return lax.broadcasted_iota(jnp.int32, dims, dim)


def prepare_kernel(desired_hbm, points_hbm, send_ref, desired_ref, points_ref, sems):
    copies = [
        pltpu.make_async_copy(desired_hbm, desired_ref, sems.at[0]),
        pltpu.make_async_copy(points_hbm, points_ref, sems.at[1]),
    ]
    for copy in copies:
        copy.start()
    lanes = pl.ds(pl.multiple_of(lax.axis_index("ylo") * 128, 128), 128)
    for copy in copies:
        copy.wait()
    points = points_ref[:, lanes]
    for f in range(8):
        send_ref[f, 0:1, :] = desired_ref[0, f : f + 1, lanes]
        send_ref[f, 1:2, :] = desired_ref[1, f : f + 1, lanes]
        send_ref[f, 2:5, :] = points


def eval_green_kernel(wave_ref, eval_ref, high_ref, low_ref, token_ref):
    kappa = wave_ref[0] * (0.5 / math.pi)
    strength = kappa * (1.0 / WALL)
    token_ref[...] = jnp.zeros_like(token_ref)
    ex = column((front_gap + eval_ref[0:1, :] * depth_span) * kappa)
    ey = column((eval_ref[1:2, :] * side_span - 0.5 * side_span) * kappa)
    ez = column((eval_ref[2:3, :] * side_span - 0.5 * side_span) * kappa)
    lane = iota((1, 128), 1)
    dz = ez - (jnp.bitwise_and(lane, WALL - 1).astype(f32) - centre) * (wall_pitch * kappa)
    base = ex * ex + dz * dz

    def step(i, carry):
        wall_row = i * 2 + jnp.right_shift(lane, 6)
        wy = (wall_row.astype(f32) - centre) * (wall_pitch * kappa)
        lanes = pl.ds(pl.multiple_of(i * 128, 128), 128)
        for start in range(0, 128, 64):
            rows = slice(start, start + 64)
            dy = ey[rows] - wy
            real, imag = green(base[rows] + dy * dy, strength)
            rh, rl = split_bf16(real)
            ih, il = split_bf16(imag)
            high_ref[start : start + 64, lanes] = rh
            low_ref[start : start + 64, lanes] = rl
            high_ref[128 + start : 192 + start, lanes] = ih
            low_ref[128 + start : 192 + start, lanes] = il
        return carry

    lax.fori_loop(0, 32, step, 0)


def first_kernel(wave_ref, got_ref, token_ref, g_ref, send_ref, dz2_ref, rest_ref, acc_ref):
    kappa = wave_ref[0] * (0.5 / math.pi)
    strength = kappa * (1.0 / WALL)
    wz = (iota((WALL, 128), 0).astype(f32) - centre) * (wall_pitch * kappa)
    wy = ((iota((8, 128), 0) + lax.axis_index(BANKS) * 8).astype(f32) - centre) * (wall_pitch * kappa)
    for j in range(8):
        px = (front_gap + got_ref[j, 2:3, :] * depth_span) * kappa
        py = (got_ref[j, 3:4, :] * side_span - 0.5 * side_span) * kappa
        pz = (got_ref[j, 4:5, :] * side_span - 0.5 * side_span) * kappa
        dz = pz - wz
        dz2_ref[j] = dz * dz
        dy = py - wy
        rest_ref[j] = px * px + dy * dy
    size = 32

    def wall_row(r, carry):
        for start in range(0, WALL, size):
            rows = pl.ds(pl.multiple_of(r * WALL + start, size), size)

            def block(j, sums):
                real_sum, imag_sum = sums
                vr = got_ref[j, 0:1, :]
                vi = got_ref[j, 1:2, :]
                real, imag = green(
                    dz2_ref[j, start : start + size, :] + rest_ref[j, pl.ds(r, 1), :], strength
                )
                g_ref[j, 0, rows, :] = real
                g_ref[j, 1, rows, :] = imag
                real_sum = real_sum + (real * vr + imag * vi)
                imag_sum = imag_sum + (real * vi - imag * vr)
                return real_sum, imag_sum

            zero = jnp.zeros((size, 128), f32)
            real_sum, imag_sum = lax.fori_loop(0, 8, block, (zero, zero), unroll=2)
            acc_ref[0, rows, :] = real_sum
            acc_ref[1, rows, :] = imag_sum
        return carry

    lax.fori_loop(0, 8, wall_row, 0)
    rows = rows_of(acc_ref)
    for i in range(8):
        send_ref[i] = rows


def rows_of(acc_ref):
    rows = []
    for part in range(2):
        for blk in range(4):
            block = acc_ref[part, blk * 128 : blk * 128 + 128, :]
            rows.append(jnp.sum(block.T, axis=0, keepdims=True))
    return jnp.concatenate(rows, axis=0)


def forward(g_ref, rows, col_ref, out_ref):
    for part in range(2):
        for blk in range(4):
            i = part * 4 + blk
            col_ref[part, blk * 128 : blk * 128 + 128, :] = column(rows[i : i + 1, :])
    size = 64

    def step(t, carry):
        real_sum = jnp.zeros((8, 128), f32)
        imag_sum = jnp.zeros((8, 128), f32)
        for k in range(512 // size):
            at = slice(k * size, k * size + size)
            gr = g_ref[t, 0, at, :]
            gi = g_ref[t, 1, at, :]
            qr = col_ref[0, at, :]
            qi = col_ref[1, at, :]
            real_sum = real_sum + (gr * qr - gi * qi).reshape(size // 8, 8, 128).sum(axis=0)
            imag_sum = imag_sum + (gi * qr + gr * qi).reshape(size // 8, 8, 128).sum(axis=0)
        out_ref[pl.ds(t, 1), :] = jnp.sum(real_sum, axis=0, keepdims=True)
        out_ref[pl.ds(t + 8, 1), :] = jnp.sum(imag_sum, axis=0, keepdims=True)
        return carry

    lax.fori_loop(0, 8, step, 0)


def adjoint(g_ref, im, acc_ref):
    size = 64

    def chunk(k, carry):
        rows = pl.ds(pl.multiple_of(k * size, size), size)
        real_sum = jnp.zeros((size, 128), f32)
        imag_sum = jnp.zeros((size, 128), f32)
        for t in range(8):
            vr = im[t : t + 1, :]
            vi = im[8 + t : 9 + t, :]
            gr = g_ref[t, 0, rows, :]
            gi = g_ref[t, 1, rows, :]
            real_sum = real_sum + (gr * vr + gi * vi)
            imag_sum = imag_sum + (gr * vi - gi * vr)
        acc_ref[0, rows, :] = real_sum
        acc_ref[1, rows, :] = imag_sum
        return carry

    lax.fori_loop(0, 512 // size, chunk, 0)
    return rows_of(acc_ref)


def image_kernel(g_ref, got_ref, send_ref, own_ref, col_ref, im_ref):
    g0 = fold(got_ref)
    own_ref[...] = g0
    forward(g_ref, g0, col_ref, im_ref)
    im = im_ref[...]
    for i in range(8):
        send_ref[i, 0:16, :] = im
        send_ref[i, 16:24, :] = g0


def adjoint_kernel(g_ref, got_ref, send_ref, acc_ref):
    im = fold(got_ref[:, 0:16, :])
    rows = adjoint(g_ref, im, acc_ref)
    norm = jnp.broadcast_to(total(im * im), (8, 128))
    for i in range(8):
        send_ref[i, 0:8, :] = rows
        send_ref[i, 8:24, :] = im
        send_ref[i, 24:32, :] = norm


def gathered_total(a, b):
    return total(fold(a * b))


def second_image_kernel(g_ref, got3_ref, got2_ref, g0_ref, send_ref, alpha_ref, col_ref, im_ref):
    all_g0 = got2_ref[:, 16:24, :]
    gamma = gathered_total(all_g0, all_g0)
    g0 = g0_ref[...]
    back = fold(got3_ref[:, 0:8, :])
    norm = fold(got3_ref[:, 24:25, :])
    alpha = gamma / (norm + tikhonov * gamma)
    alpha_ref[0:1, :] = alpha
    alpha_ref[1:2, :] = gamma
    g1 = g0 - alpha * (back + tikhonov * g0)
    forward(g_ref, g1, col_ref, im_ref)
    im = im_ref[...]
    for i in range(8):
        send_ref[i, 0:16, :] = im
        send_ref[i, 16:24, :] = g1


def norm_kernel(got4_ref, got2_ref, alpha_ref, send_ref, scalar_ref):
    all_g0 = got2_ref[:, 16:24, :]
    all_g1 = got4_ref[:, 16:24, :]
    gamma0 = alpha_ref[1:2, :]
    gamma1 = gathered_total(all_g1, all_g1)
    cross = gathered_total(all_g1, all_g0)
    beta = gamma1 / gamma0
    im1 = fold(got4_ref[:, 0:16, :]) + beta * fold(got2_ref[:, 0:16, :])
    scalar_ref[0:1, :] = beta
    scalar_ref[1:2, :] = gamma1
    scalar_ref[2:3, :] = gamma1 + (2.0 * cross + beta * gamma0) * beta
    square = jnp.broadcast_to(total(im1 * im1), (8, 128))
    for i in range(8):
        send_ref[i, 0:16, :] = im1
        send_ref[i, 16:24, :] = square


def drive_kernel(got5_ref, got3_ref, got2_ref, got4_ref, alpha_ref, scalar_ref, send_ref):
    alpha0 = alpha_ref[0:1, :]
    beta = scalar_ref[0:1, :]
    norm = fold(got5_ref[:, 16:17, :])
    alpha1 = scalar_ref[1:2, :] / (norm + tikhonov * scalar_ref[2:3, :])
    from_first = alpha0 + alpha1 * beta
    for u in range(8):
        rows = from_first * got2_ref[u, 16:24, :] + alpha1 * got4_ref[u, 16:24, :]
        for i in range(8):
            send_ref[i, 8 * u : 8 * u + 8, :] = rows
    for half in range(2):
        member = half * 4 + lax.axis_index(("yhi", "zc"))
        change = alpha0 * got3_ref[member, 8:24, :] + alpha1 * got5_ref[member, 0:16, :]
        for i in range(8):
            send_ref[i, 64 + half : 65 + half, :] = change[i : i + 1, :]
            send_ref[i, 66 + half : 67 + half, :] = change[8 + i : 9 + i, :]


def field_kernel(got_ref, high_ref, low_ref, desired_ref, cells_ref, drives_ref, residual_ref, field_ref):
    for part in range(2):
        for half in range(2):
            lanes = slice(half * 128, half * 128 + 128)
            residual_ref[part, :, lanes] = desired_ref[part, :, lanes] - got_ref[:, 64 + part * 2 + half, :]
    drives = got_ref[:, 0:64, :].reshape(512, 128)
    for blk in range(2):
        lanes = slice(blk * 128, blk * 128 + 128)
        cells = cells_ref[pl.ds(lax.axis_index(SPK) * 2 + blk, 1), :]
        pick = (iota((128, 128), 0) == jnp.bitwise_and(cells, 127)).astype(f32)
        picked = jnp.dot(drives, pick, precision=lax.Precision.HIGHEST, preferred_element_type=f32)
        line = iota((64, 128), 0)
        place = jnp.right_shift(line, 3) * 4 + jnp.bitwise_and(line, 3)
        right = place == jnp.right_shift(cells, 7)
        real = jnp.bitwise_and(line, 4) == 0
        for part in range(2):
            mask = jnp.where(right & (real if part == 0 else ~real), 1.0, 0.0)
            for f in range(8):
                rows = picked[f * 64 : f * 64 + 64, :] * mask
                drives_ref[part, f : f + 1, lanes] = jnp.sum(rows, axis=0, keepdims=True)
    out = jnp.zeros((32, 256), f32)
    fine = jnp.zeros((16, 256), f32)
    dims = (((1,), (1,)), ((), ()))
    for u in range(8):
        for pair in range(2):
            parts = [
                jnp.concatenate(
                    [got_ref[:, u * 8 + part * 4 + pair * 2 + k, :] for k in range(2)], axis=1
                )
                for part in range(2)
            ]
            high, low = split_bf16(jnp.concatenate(parts, axis=0))
            both = jnp.concatenate([high, low], axis=0)
            at = (u * 2 + pair) * 256
            lanes = slice(at, at + 256)
            out = out + lax.dot_general(both, high_ref[:, lanes], dims, preferred_element_type=f32)
            fine = fine + lax.dot_general(high, low_ref[:, lanes], dims, preferred_element_type=f32)
    out = out[0:16, :] + out[16:32, :] + fine
    field_ref[0] = out[0:8, 0:128] - out[8:16, 128:256]
    field_ref[1] = out[0:8, 128:256] + out[8:16, 0:128]


def exchange(array, axes):
    return lax.all_to_all(array, axes, split_axis=0, concat_axis=0, tiled=True)


def local(desired, spk_cells, pt_cells, eval_cells, wavenumber):
    send0 = call(
        prepare_kernel,
        shape(8, 8, 128),
        [vmem((2, 8, 256), f32), vmem((3, 256), f32), pltpu.SemaphoreType.DMA((2,))],
        WHOLE, "aa", "prepare", 1024,
    )(desired, pt_cells)
    got0 = exchange(send0, FLD)
    high, low, token = call(
        eval_green_kernel,
        (shape(256, 4096, dtype=bf16), shape(256, 4096, dtype=bf16), shape(8, 128)),
        [], 8, "sv", "eval_green", 524288 * 40, 524288,
    )(wavenumber, eval_cells)
    g, send1 = call(
        first_kernel,
        (shape(8, 2, 512, 128), shape(8, 8, 128)),
        [vmem((8, 64, 128), f32), vmem((8, 8, 128), f32), vmem((2, 512, 128), f32)],
        8, "svv", "first", 524288 * 48, 524288,
    )(wavenumber, got0, token)
    got1 = exchange(send1, NEAR)
    send2, g0 = call(
        image_kernel,
        (shape(8, 24, 128), shape(8, 128)),
        [vmem((2, 512, 128), f32), vmem((16, 128), f32)], 8, "vv", "image", 524288 * 8,
    )(g, got1)
    got2 = exchange(send2, BANKS)
    send3 = call(
        adjoint_kernel, shape(8, 32, 128), [vmem((2, 512, 128), f32)], 8, "vv", "adjoint", 524288 * 8,
    )(g, got2)
    got3 = exchange(send3, NEAR)
    send4, alpha = call(
        second_image_kernel,
        (shape(8, 24, 128), shape(2, 128)),
        [vmem((2, 512, 128), f32), vmem((16, 128), f32)], 8, "vvvv", "second_image", 524288 * 8,
    )(g, got3, got2, g0)
    got4 = exchange(send4, BANKS)
    send5, scalars = call(
        norm_kernel, (shape(8, 24, 128), shape(3, 128)), [], 8, "vvv", "norm", 81920,
    )(got4, got2, alpha)
    got5 = exchange(send5, NEAR)
    send6 = call(
        drive_kernel, shape(8, 72, 128), [], 8, "vvvvvv", "drive", 81920,
    )(got5, got3, got2, got4, alpha, scalars)
    got6 = exchange(send6, FLD)
    return call(
        field_kernel,
        (shape(2, 8, 256), shape(2, 8, 256), shape(2, 8, 128)),
        [], 12, "vvvvv", "field", 524288 * 96,
    )(got6, high, low, desired, spk_cells.reshape(32, 128))


def solution(mesh):
    split = Mesh(
        mesh.devices.reshape(2, 4, 2, 2, 4, 2, 2), ("ylo", "x", "core", "yhi", "za", "zb", "zc")
    )
    in_specs = (P(None, None, PTS), P(), P(None, PTS), P(None, SPK + PTS), P())
    out_specs = (P(None, None, SPK), P(None, None, PTS), P(None, None, SPK + PTS))
    return jax.shard_map(local, mesh=split, in_specs=in_specs, out_specs=out_specs, check_vma=False)
```

```python
import math

import jax
import jax.numpy as jnp
from jax import lax
from jax.experimental import pallas as pl
from jax.experimental.pallas import tpu as pltpu
from jax.sharding import Mesh
from jax.sharding import PartitionSpec as P

WALL = 64
SPK = ("ylo", "x", "core")
PTS = ("yhi", "za", "zb", "zc")
FLD = ("za", "zb")
BANKS = ("x", "core")
NEAR = ("ylo", "yhi", "zc")

wall_pitch = 0.05
front_gap = 0.5
depth_span = 3.15
side_span = 3.2
tikhonov = 0.1
centre = (WALL - 1) * 0.5

SIN = (4.442879676818848, -7.307816505432129, 3.5977742671966553, -0.7911993861198425)
COS = (-1.4142040014266968, 6.97763729095459, -5.715188026428223, 1.728213906288147)
ROUNDER = 12582912.0

f32 = jnp.float32
bf16 = jnp.bfloat16
vmem = pltpu.VMEM


def spec(space=pltpu.VMEM):
    return pl.BlockSpec(memory_space=space)


def shape(*dims, dtype=f32):
    return jax.ShapeDtypeStruct(dims, dtype)


WHOLE = 64
SPACES = {"s": pltpu.SMEM, "v": pltpu.VMEM, "a": pl.ANY, "h": pltpu.HBM}


def call(kernel, out_shapes, scratch, limit_mib, spaces, name, flops, trans=0, out_spaces=None):
    return pl.pallas_call(
        kernel,
        out_shape=out_shapes,
        in_specs=[spec(SPACES[c]) for c in spaces],
        out_specs=tuple(spec(SPACES[c]) for c in out_spaces)
        if out_spaces
        else jax.tree.map(lambda _: spec(), out_shapes),
        scratch_shapes=scratch,
        compiler_params=pltpu.CompilerParams(vmem_limit_bytes=min(limit_mib << 20, 67043328)),
        cost_estimate=pl.CostEstimate(flops=flops, bytes_accessed=1 << 20, transcendentals=trans),
        name=name,
    )


def poly(coeffs, u):
    out = coeffs[-1]
    for c in coeffs[-2::-1]:
        out = out * u + c
    return out


def green(scaled, strength):
    inverse = lax.rsqrt(scaled)
    turns = scaled * inverse
    magnitude = inverse * strength
    whole = (turns + ROUNDER) - ROUNDER
    frac = turns - whole
    u = frac * frac
    s = poly(SIN, u) * frac
    c = poly(COS, u)
    ms = magnitude * s
    return magnitude - ms * s, ms * c


def column(row):
    return jnp.broadcast_to(row, (128, 128)).T


def total(x):
    return jnp.broadcast_to(jnp.sum(x, keepdims=True), (1, 128))


def fold(x):
    out = x[0]
    for i in range(1, x.shape[0]):
        out = out + x[i]
    return out


def split_bf16(x):
    high = x.astype(bf16)
    return high, (x - high.astype(f32)).astype(bf16)


def iota(dims, dim):
    return lax.broadcasted_iota(jnp.int32, dims, dim)


def prepare_kernel(desired_hbm, points_hbm, send_hbm, sems):
    lanes = pl.ds(pl.multiple_of(lax.axis_index("ylo") * 128, 128), 128)
    copies = []
    for part in range(2):
        copies.append(
            pltpu.make_async_copy(
                desired_hbm.at[part, :, lanes], send_hbm.at[:, part, :], sems.at[part]
            )
        )
    for f in range(8):
        copies.append(
            pltpu.make_async_copy(points_hbm.at[:, lanes], send_hbm.at[f, 2:5, :], sems.at[2 + f])
        )
    for copy in copies:
        copy.start()
    for copy in copies:
        copy.wait()


def eval_green_kernel(wave_ref, eval_ref, high_hbm, low_hbm, high_ref, low_ref, sems):
    kappa = wave_ref[0] * (0.5 / math.pi)
    strength = kappa * (1.0 / WALL)
    ex = column((front_gap + eval_ref[0:1, :] * depth_span) * kappa)
    ey = column((eval_ref[1:2, :] * side_span - 0.5 * side_span) * kappa)
    ez = column((eval_ref[2:3, :] * side_span - 0.5 * side_span) * kappa)
    lane = iota((1, 128), 1)
    dz = ez - (jnp.bitwise_and(lane, WALL - 1).astype(f32) - centre) * (wall_pitch * kappa)
    base = ex * ex + dz * dz

    def step(i, carry):
        wall_row = i * 2 + jnp.right_shift(lane, 6)
        wy = (wall_row.astype(f32) - centre) * (wall_pitch * kappa)
        lanes = pl.ds(pl.multiple_of(i * 128, 128), 128)
        for start in range(0, 128, 64):
            rows = slice(start, start + 64)
            dy = ey[rows] - wy
            real, imag = green(base[rows] + dy * dy, strength)
            rh, rl = split_bf16(real)
            ih, il = split_bf16(imag)
            high_ref[start : start + 64, lanes] = rh
            low_ref[start : start + 64, lanes] = rl
            high_ref[128 + start : 192 + start, lanes] = ih
            low_ref[128 + start : 192 + start, lanes] = il
        return carry

    copies = []
    for quarter in range(4):
        lax.fori_loop(quarter * 8, quarter * 8 + 8, step, 0)
        lanes = slice(quarter * 1024, quarter * 1024 + 1024)
        for k, (ref, hbm) in enumerate(((high_ref, high_hbm), (low_ref, low_hbm))):
            copies.append(
                pltpu.make_async_copy(ref.at[:, lanes], hbm.at[:, lanes], sems.at[k, quarter])
            )
            copies[-1].start()
    for copy in copies:
        copy.wait()


def first_kernel(wave_ref, got_ref, g_ref, send_ref, dz2_ref, rest_ref, acc_ref):
    kappa = wave_ref[0] * (0.5 / math.pi)
    strength = kappa * (1.0 / WALL)
    wz = (iota((WALL, 128), 0).astype(f32) - centre) * (wall_pitch * kappa)
    wy = ((iota((8, 128), 0) + lax.axis_index(BANKS) * 8).astype(f32) - centre) * (wall_pitch * kappa)
    for j in range(8):
        px = (front_gap + got_ref[j, 2:3, :] * depth_span) * kappa
        py = (got_ref[j, 3:4, :] * side_span - 0.5 * side_span) * kappa
        pz = (got_ref[j, 4:5, :] * side_span - 0.5 * side_span) * kappa
        dz = pz - wz
        dz2_ref[j] = dz * dz
        dy = py - wy
        rest_ref[j] = px * px + dy * dy
    size = 32

    def wall_row(r, carry):
        for start in range(0, WALL, size):
            rows = pl.ds(pl.multiple_of(r * WALL + start, size), size)

            def block(j, sums):
                real_sum, imag_sum = sums
                vr = got_ref[j, 0:1, :]
                vi = got_ref[j, 1:2, :]
                real, imag = green(
                    dz2_ref[j, start : start + size, :] + rest_ref[j, pl.ds(r, 1), :], strength
                )
                g_ref[j, 0, rows, :] = real
                g_ref[j, 1, rows, :] = imag
                real_sum = real_sum + (real * vr + imag * vi)
                imag_sum = imag_sum + (real * vi - imag * vr)
                return real_sum, imag_sum

            zero = jnp.zeros((size, 128), f32)
            real_sum, imag_sum = lax.fori_loop(0, 8, block, (zero, zero), unroll=2)
            acc_ref[0, rows, :] = real_sum
            acc_ref[1, rows, :] = imag_sum
        return carry

    lax.fori_loop(0, 8, wall_row, 0)
    rows = rows_of(acc_ref)
    for i in range(8):
        send_ref[i] = rows


def rows_of(acc_ref):
    rows = []
    for part in range(2):
        for blk in range(4):
            block = acc_ref[part, blk * 128 : blk * 128 + 128, :]
            rows.append(jnp.sum(block.T, axis=0, keepdims=True))
    return jnp.concatenate(rows, axis=0)


def forward(g_ref, rows, col_ref, out_ref):
    for part in range(2):
        for blk in range(4):
            i = part * 4 + blk
            col_ref[part, blk * 128 : blk * 128 + 128, :] = column(rows[i : i + 1, :])
    size = 64

    def step(t, carry):
        real_sum = jnp.zeros((8, 128), f32)
        imag_sum = jnp.zeros((8, 128), f32)
        for k in range(512 // size):
            at = slice(k * size, k * size + size)
            gr = g_ref[t, 0, at, :]
            gi = g_ref[t, 1, at, :]
            qr = col_ref[0, at, :]
            qi = col_ref[1, at, :]
            real_sum = real_sum + (gr * qr - gi * qi).reshape(size // 8, 8, 128).sum(axis=0)
            imag_sum = imag_sum + (gi * qr + gr * qi).reshape(size // 8, 8, 128).sum(axis=0)
        out_ref[pl.ds(t, 1), :] = jnp.sum(real_sum, axis=0, keepdims=True)
        out_ref[pl.ds(t + 8, 1), :] = jnp.sum(imag_sum, axis=0, keepdims=True)
        return carry

    lax.fori_loop(0, 8, step, 0)


def adjoint(g_ref, im, acc_ref):
    size = 64

    def chunk(k, carry):
        rows = pl.ds(pl.multiple_of(k * size, size), size)
        real_sum = jnp.zeros((size, 128), f32)
        imag_sum = jnp.zeros((size, 128), f32)
        for t in range(8):
            vr = im[t : t + 1, :]
            vi = im[8 + t : 9 + t, :]
            gr = g_ref[t, 0, rows, :]
            gi = g_ref[t, 1, rows, :]
            real_sum = real_sum + (gr * vr + gi * vi)
            imag_sum = imag_sum + (gr * vi - gi * vr)
        acc_ref[0, rows, :] = real_sum
        acc_ref[1, rows, :] = imag_sum
        return carry

    lax.fori_loop(0, 512 // size, chunk, 0)
    return rows_of(acc_ref)


def image_kernel(g_ref, got_ref, send_ref, own_ref, col_ref, im_ref):
    g0 = fold(got_ref)
    own_ref[...] = g0
    forward(g_ref, g0, col_ref, im_ref)
    im = im_ref[...]
    for i in range(8):
        send_ref[i, 0:16, :] = im
        send_ref[i, 16:24, :] = g0


def adjoint_kernel(g_ref, got_ref, send_ref, acc_ref):
    im = fold(got_ref[:, 0:16, :])
    rows = adjoint(g_ref, im, acc_ref)
    norm = jnp.broadcast_to(total(im * im), (8, 128))
    for i in range(8):
        send_ref[i, 0:8, :] = rows
        send_ref[i, 8:24, :] = im
        send_ref[i, 24:32, :] = norm


def gathered_total(a, b):
    return total(fold(a * b))


def second_image_kernel(g_ref, got3_ref, got2_ref, g0_ref, send_ref, alpha_ref, col_ref, im_ref):
    all_g0 = got2_ref[:, 16:24, :]
    gamma = gathered_total(all_g0, all_g0)
    g0 = g0_ref[...]
    back = fold(got3_ref[:, 0:8, :])
    norm = fold(got3_ref[:, 24:25, :])
    alpha = gamma / (norm + tikhonov * gamma)
    alpha_ref[0:1, :] = alpha
    alpha_ref[1:2, :] = gamma
    g1 = g0 - alpha * (back + tikhonov * g0)
    forward(g_ref, g1, col_ref, im_ref)
    im = im_ref[...]
    for i in range(8):
        send_ref[i, 0:16, :] = im
        send_ref[i, 16:24, :] = g1


def norm_kernel(got4_ref, got2_ref, alpha_ref, send_ref, scalar_ref):
    all_g0 = got2_ref[:, 16:24, :]
    all_g1 = got4_ref[:, 16:24, :]
    gamma0 = alpha_ref[1:2, :]
    gamma1 = gathered_total(all_g1, all_g1)
    cross = gathered_total(all_g1, all_g0)
    beta = gamma1 / gamma0
    im1 = fold(got4_ref[:, 0:16, :]) + beta * fold(got2_ref[:, 0:16, :])
    scalar_ref[0:1, :] = beta
    scalar_ref[1:2, :] = gamma1
    scalar_ref[2:3, :] = gamma1 + (2.0 * cross + beta * gamma0) * beta
    square = jnp.broadcast_to(total(im1 * im1), (8, 128))
    for i in range(8):
        send_ref[i, 0:16, :] = im1
        send_ref[i, 16:24, :] = square


def drive_kernel(got5_ref, got3_ref, got2_ref, got4_ref, alpha_ref, scalar_ref, send_ref):
    alpha0 = alpha_ref[0:1, :]
    beta = scalar_ref[0:1, :]
    norm = fold(got5_ref[:, 16:17, :])
    alpha1 = scalar_ref[1:2, :] / (norm + tikhonov * scalar_ref[2:3, :])
    from_first = alpha0 + alpha1 * beta
    for u in range(8):
        rows = from_first * got2_ref[u, 16:24, :] + alpha1 * got4_ref[u, 16:24, :]
        for i in range(8):
            send_ref[i, 8 * u : 8 * u + 8, :] = rows
    for half in range(2):
        member = half * 4 + lax.axis_index(("yhi", "zc"))
        change = alpha0 * got3_ref[member, 8:24, :] + alpha1 * got5_ref[member, 0:16, :]
        for i in range(8):
            send_ref[i, 64 + half : 65 + half, :] = change[i : i + 1, :]
            send_ref[i, 66 + half : 67 + half, :] = change[8 + i : 9 + i, :]


ROWS = 72


def of_fields(got_ref, row):
    return got_ref[pl.ds(row, 8, stride=ROWS), :]


def field_kernel(got_ref, high_ref, low_ref, desired_ref, cells_ref, drives_ref, residual_ref, field_ref):
    for part in range(2):
        for half in range(2):
            lanes = slice(half * 128, half * 128 + 128)
            residual_ref[part, :, lanes] = desired_ref[part, :, lanes] - of_fields(
                got_ref, 64 + part * 2 + half
            )
    first_cell = lax.axis_index(SPK) * 2
    cells = jnp.concatenate([cells_ref[pl.ds(first_cell + blk, 1), :] for blk in range(2)], axis=1)
    pick = jnp.where(iota((128, 256), 0) == jnp.bitwise_and(cells, 127), 1.0, 0.0).astype(bf16)
    line = iota((64, 256), 0)
    place = jnp.right_shift(line, 3) * 4 + jnp.bitwise_and(line, 3)
    right = place == jnp.right_shift(cells, 7)
    is_real = jnp.bitwise_and(line, 4) == 0
    real_mask = jnp.where(right & is_real, 1.0, 0.0)
    imag_mask = jnp.where(right & ~is_real, 1.0, 0.0)
    for f in range(8):
        x = got_ref[f * ROWS : f * ROWS + 64, :]
        high = x.astype(bf16)
        left = x - high.astype(f32)
        middle, low = split_bf16(left)
        three = jnp.concatenate([high, middle, low], axis=0)
        picked = jnp.dot(three, pick, preferred_element_type=f32)
        picked = picked[0:64] + picked[64:128] + picked[128:192]
        drives_ref[0, f : f + 1, :] = jnp.sum(picked * real_mask, axis=0, keepdims=True)
        drives_ref[1, f : f + 1, :] = jnp.sum(picked * imag_mask, axis=0, keepdims=True)
    out = jnp.zeros((32, 256), f32)
    fine = jnp.zeros((16, 256), f32)
    dims = (((1,), (1,)), ((), ()))
    for u in range(8):
        for pair in range(2):
            parts = [
                jnp.concatenate(
                    [of_fields(got_ref, u * 8 + part * 4 + pair * 2 + k) for k in range(2)], axis=1
                )
                for part in range(2)
            ]
            high, low = split_bf16(jnp.concatenate(parts, axis=0))
            both = jnp.concatenate([high, low], axis=0)
            at = (u * 2 + pair) * 256
            lanes = slice(at, at + 256)
            out = out + lax.dot_general(both, high_ref[:, lanes], dims, preferred_element_type=f32)
            fine = fine + lax.dot_general(high, low_ref[:, lanes], dims, preferred_element_type=f32)
    out = out[0:16, :] + out[16:32, :] + fine
    field_ref[0] = out[0:8, 0:128] - out[8:16, 128:256]
    field_ref[1] = out[0:8, 128:256] + out[8:16, 0:128]


def exchange(array, axes):
    return lax.all_to_all(array, axes, split_axis=0, concat_axis=0, tiled=True)


def local(desired, spk_cells, pt_cells, eval_cells, wavenumber):
    (send0,) = call(
        prepare_kernel, (shape(8, 8, 128),), [pltpu.SemaphoreType.DMA((10,))],
        WHOLE, "aa", "prepare", 1024, out_spaces="h",
    )(desired, pt_cells)
    got0 = exchange(send0, FLD)
    high, low = call(
        eval_green_kernel,
        (shape(256, 4096, dtype=bf16), shape(256, 4096, dtype=bf16)),
        [vmem((256, 4096), bf16), vmem((256, 4096), bf16), pltpu.SemaphoreType.DMA((2, 4))],
        63, "sv", "eval_green", 524288 * 40, 524288, out_spaces="hh",
    )(wavenumber, eval_cells)
    got0, high, low = lax.optimization_barrier((got0, high, low))
    g, send1 = call(
        first_kernel,
        (shape(8, 2, 512, 128), shape(8, 8, 128)),
        [vmem((8, 64, 128), f32), vmem((8, 8, 128), f32), vmem((2, 512, 128), f32)],
        8, "sv", "first", 524288 * 48, 524288,
    )(wavenumber, got0)
    got1 = exchange(send1, NEAR)
    send2, g0 = call(
        image_kernel,
        (shape(8, 24, 128), shape(8, 128)),
        [vmem((2, 512, 128), f32), vmem((16, 128), f32)], 8, "vv", "image", 524288 * 8,
    )(g, got1)
    got2 = exchange(send2, BANKS)
    send3 = call(
        adjoint_kernel, shape(8, 32, 128), [vmem((2, 512, 128), f32)], 8, "vv", "adjoint", 524288 * 8,
    )(g, got2)
    got3 = exchange(send3, NEAR)
    send4, alpha = call(
        second_image_kernel,
        (shape(8, 24, 128), shape(2, 128)),
        [vmem((2, 512, 128), f32), vmem((16, 128), f32)], 8, "vvvv", "second_image", 524288 * 8,
    )(g, got3, got2, g0)
    got4 = exchange(send4, BANKS)
    send5, scalars = call(
        norm_kernel, (shape(8, 24, 128), shape(3, 128)), [], 8, "vvv", "norm", 81920,
    )(got4, got2, alpha)
    got5 = exchange(send5, NEAR)
    send6 = call(
        drive_kernel, shape(8, ROWS, 128), [], 8, "vvvvvv", "drive", 81920,
    )(got5, got3, got2, got4, alpha, scalars)
    got6 = exchange(send6, FLD)
    return call(
        field_kernel,
        (shape(2, 8, 256), shape(2, 8, 256), shape(2, 8, 128)),
        [], 12, "vvvvv", "field", 524288 * 96,
    )(got6.reshape(8 * ROWS, 128), high, low, desired, spk_cells.reshape(32, 128))


def solution(mesh):
    split = Mesh(
        mesh.devices.reshape(2, 4, 2, 2, 4, 2, 2), ("ylo", "x", "core", "yhi", "za", "zb", "zc")
    )
    in_specs = (P(None, None, PTS), P(), P(None, PTS), P(None, SPK + PTS), P())
    out_specs = (P(None, None, SPK), P(None, None, PTS), P(None, None, SPK + PTS))
    return jax.shard_map(local, mesh=split, in_specs=in_specs, out_specs=out_specs, check_vma=False)
```

```python
import math

import jax
import jax.numpy as jnp
from jax import lax
from jax.experimental import pallas as pl
from jax.experimental.pallas import tpu as pltpu
from jax.sharding import Mesh
from jax.sharding import PartitionSpec as P

WALL = 64
SPK = ("ylo", "x", "core")
PTS = ("yhi", "za", "zb", "zc")
FLD = ("za", "zb")
BANKS = ("x", "core")
NEAR = ("ylo", "yhi", "zc")

wall_pitch = 0.05
front_gap = 0.5
depth_span = 3.15
side_span = 3.2
tikhonov = 0.1
centre = (WALL - 1) * 0.5

SIN = (4.442879676818848, -7.307816505432129, 3.5977742671966553, -0.7911993861198425)
COS = (-1.4142040014266968, 6.97763729095459, -5.715188026428223, 1.728213906288147)
ROUNDER = 12582912.0
LOW_SCALE = 4194304.0

f32 = jnp.float32
f8 = jnp.float8_e4m3fn
bf16 = jnp.bfloat16
vmem = pltpu.VMEM


def spec(space=pltpu.VMEM):
    return pl.BlockSpec(memory_space=space)


def shape(*dims, dtype=f32):
    return jax.ShapeDtypeStruct(dims, dtype)


WHOLE = 64
SPACES = {"s": pltpu.SMEM, "v": pltpu.VMEM, "a": pl.ANY, "h": pltpu.HBM}


def call(kernel, out_shapes, scratch, limit_mib, spaces, name, flops, trans=0, out_spaces=None):
    return pl.pallas_call(
        kernel,
        out_shape=out_shapes,
        in_specs=[spec(SPACES[c]) for c in spaces],
        out_specs=tuple(spec(SPACES[c]) for c in out_spaces)
        if out_spaces
        else jax.tree.map(lambda _: spec(), out_shapes),
        scratch_shapes=scratch,
        compiler_params=pltpu.CompilerParams(vmem_limit_bytes=min(int(limit_mib * (1 << 20)), 67043328)),
        cost_estimate=pl.CostEstimate(flops=flops, bytes_accessed=1 << 20, transcendentals=trans),
        name=name,
    )


def poly(coeffs, u):
    out = coeffs[-1]
    for c in coeffs[-2::-1]:
        out = out * u + c
    return out


def green(scaled, strength):
    inverse = lax.rsqrt(scaled)
    turns = scaled * inverse
    magnitude = inverse * strength
    whole = (turns + ROUNDER) - ROUNDER
    frac = turns - whole
    u = frac * frac
    s = poly(SIN, u) * frac
    c = poly(COS, u)
    ms = magnitude * s
    return magnitude - ms * s, ms * c


def column(row):
    return jnp.broadcast_to(row, (128, 128)).T


def total(x):
    return jnp.broadcast_to(jnp.sum(x, keepdims=True), (1, 128))


def fold(x):
    out = x[0]
    for i in range(1, x.shape[0]):
        out = out + x[i]
    return out


def split_bf16(x):
    high = x.astype(bf16)
    return high, (x - high.astype(f32)).astype(bf16)


def iota(dims, dim):
    return lax.broadcasted_iota(jnp.int32, dims, dim)


def prepare_kernel(desired_hbm, points_hbm, send_ref, desired_ref, points_ref, sems):
    copies = [
        pltpu.make_async_copy(desired_hbm, desired_ref, sems.at[0]),
        pltpu.make_async_copy(points_hbm, points_ref, sems.at[1]),
    ]
    for copy in copies:
        copy.start()
    lanes = pl.ds(pl.multiple_of(lax.axis_index("ylo") * 128, 128), 128)
    for copy in copies:
        copy.wait()
    points = points_ref[:, lanes]
    for f in range(8):
        send_ref[f, 0:1, :] = desired_ref[0, f : f + 1, lanes]
        send_ref[f, 1:2, :] = desired_ref[1, f : f + 1, lanes]
        send_ref[f, 2:5, :] = points


def eval_green_kernel(wave_ref, eval_ref, high_ref, low_ref):
    kappa = wave_ref[0] * (0.5 / math.pi)
    strength = kappa * (1.0 / WALL)
    ex = column((front_gap + eval_ref[0:1, :] * depth_span) * kappa)
    ey = column((eval_ref[1:2, :] * side_span - 0.5 * side_span) * kappa)
    ez = column((eval_ref[2:3, :] * side_span - 0.5 * side_span) * kappa)
    lane = iota((1, 128), 1)
    dz = ez - (jnp.bitwise_and(lane, WALL - 1).astype(f32) - centre) * (wall_pitch * kappa)
    base = ex * ex + dz * dz

    def step(i, carry):
        wall_row = i * 2 + jnp.right_shift(lane, 6)
        wy = (wall_row.astype(f32) - centre) * (wall_pitch * kappa)
        lanes = pl.ds(pl.multiple_of(i * 128, 128), 128)
        for start in range(0, 128, 64):
            rows = slice(start, start + 64)
            dy = ey[rows] - wy
            real, imag = green(base[rows] + dy * dy, strength)
            for first, value in ((start, real), (128 + start, imag)):
                high = value.astype(bf16)
                high_ref[first : first + 64, lanes] = high
                low_ref[first : first + 64, lanes] = ((value - high.astype(f32)) * LOW_SCALE).astype(f8)
        return carry

    lax.fori_loop(0, 32, step, 0)


def first_kernel(wave_ref, got_ref, g_ref, send_ref, dz2_ref, rest_ref, acc_ref):
    kappa = wave_ref[0] * (0.5 / math.pi)
    strength = kappa * (1.0 / WALL)
    wz = (iota((WALL, 128), 0).astype(f32) - centre) * (wall_pitch * kappa)
    wy = ((iota((8, 128), 0) + lax.axis_index(BANKS) * 8).astype(f32) - centre) * (wall_pitch * kappa)
    for j in range(8):
        px = (front_gap + got_ref[j, 2:3, :] * depth_span) * kappa
        py = (got_ref[j, 3:4, :] * side_span - 0.5 * side_span) * kappa
        pz = (got_ref[j, 4:5, :] * side_span - 0.5 * side_span) * kappa
        dz = pz - wz
        dz2_ref[j] = dz * dz
        dy = py - wy
        rest_ref[j] = px * px + dy * dy
    size = 32

    def wall_row(r, carry):
        for start in range(0, WALL, size):
            rows = pl.ds(pl.multiple_of(r * WALL + start, size), size)

            def block(j, sums):
                real_sum, imag_sum = sums
                vr = got_ref[j, 0:1, :]
                vi = got_ref[j, 1:2, :]
                real, imag = green(
                    dz2_ref[j, start : start + size, :] + rest_ref[j, pl.ds(r, 1), :], strength
                )
                g_ref[j, 0, rows, :] = real
                g_ref[j, 1, rows, :] = imag
                real_sum = real_sum + (real * vr + imag * vi)
                imag_sum = imag_sum + (real * vi - imag * vr)
                return real_sum, imag_sum

            zero = jnp.zeros((size, 128), f32)
            real_sum, imag_sum = lax.fori_loop(0, 8, block, (zero, zero), unroll=2)
            acc_ref[0, rows, :] = real_sum
            acc_ref[1, rows, :] = imag_sum
        return carry

    lax.fori_loop(0, 8, wall_row, 0)
    rows = rows_of(acc_ref)
    for i in range(8):
        send_ref[i] = rows


def rows_of(acc_ref):
    rows = []
    for part in range(2):
        for blk in range(4):
            block = acc_ref[part, blk * 128 : blk * 128 + 128, :]
            rows.append(jnp.sum(block.T, axis=0, keepdims=True))
    return jnp.concatenate(rows, axis=0)


def forward(g_ref, rows, col_ref, out_ref):
    for part in range(2):
        for blk in range(4):
            i = part * 4 + blk
            col_ref[part, blk * 128 : blk * 128 + 128, :] = column(rows[i : i + 1, :])
    size = 64

    def step(t, carry):
        real_sum = jnp.zeros((8, 128), f32)
        imag_sum = jnp.zeros((8, 128), f32)
        for k in range(512 // size):
            at = slice(k * size, k * size + size)
            gr = g_ref[t, 0, at, :]
            gi = g_ref[t, 1, at, :]
            qr = col_ref[0, at, :]
            qi = col_ref[1, at, :]
            real_sum = real_sum + (gr * qr - gi * qi).reshape(size // 8, 8, 128).sum(axis=0)
            imag_sum = imag_sum + (gi * qr + gr * qi).reshape(size // 8, 8, 128).sum(axis=0)
        out_ref[pl.ds(t, 1), :] = jnp.sum(real_sum, axis=0, keepdims=True)
        out_ref[pl.ds(t + 8, 1), :] = jnp.sum(imag_sum, axis=0, keepdims=True)
        return carry

    lax.fori_loop(0, 8, step, 0)


def adjoint(g_ref, im, acc_ref):
    size = 64

    def chunk(k, carry):
        rows = pl.ds(pl.multiple_of(k * size, size), size)
        real_sum = jnp.zeros((size, 128), f32)
        imag_sum = jnp.zeros((size, 128), f32)
        for t in range(8):
            vr = im[t : t + 1, :]
            vi = im[8 + t : 9 + t, :]
            gr = g_ref[t, 0, rows, :]
            gi = g_ref[t, 1, rows, :]
            real_sum = real_sum + (gr * vr + gi * vi)
            imag_sum = imag_sum + (gr * vi - gi * vr)
        acc_ref[0, rows, :] = real_sum
        acc_ref[1, rows, :] = imag_sum
        return carry

    lax.fori_loop(0, 512 // size, chunk, 0)
    return rows_of(acc_ref)


def image_kernel(g_ref, got_ref, send_ref, own_ref, col_ref, im_ref):
    g0 = fold(got_ref)
    own_ref[...] = g0
    forward(g_ref, g0, col_ref, im_ref)
    im = im_ref[...]
    for i in range(8):
        send_ref[i, 0:16, :] = im
        send_ref[i, 16:24, :] = g0


def adjoint_kernel(g_ref, got_ref, send_ref, acc_ref):
    im = fold(got_ref[:, 0:16, :])
    rows = adjoint(g_ref, im, acc_ref)
    norm = jnp.broadcast_to(total(im * im), (8, 128))
    for i in range(8):
        send_ref[i, 0:8, :] = rows
        send_ref[i, 8:24, :] = im
        send_ref[i, 24:32, :] = norm


def gathered_total(a, b):
    return total(fold(a * b))


def second_image_kernel(g_ref, got3_ref, got2_ref, g0_ref, send_ref, alpha_ref, col_ref, im_ref):
    all_g0 = got2_ref[:, 16:24, :]
    gamma = gathered_total(all_g0, all_g0)
    g0 = g0_ref[...]
    back = fold(got3_ref[:, 0:8, :])
    norm = fold(got3_ref[:, 24:25, :])
    alpha = gamma / (norm + tikhonov * gamma)
    alpha_ref[0:1, :] = alpha
    alpha_ref[1:2, :] = gamma
    g1 = g0 - alpha * (back + tikhonov * g0)
    forward(g_ref, g1, col_ref, im_ref)
    im = im_ref[...]
    for i in range(8):
        send_ref[i, 0:16, :] = im
        send_ref[i, 16:24, :] = g1


def norm_kernel(got4_ref, got2_ref, alpha_ref, send_ref, scalar_ref):
    all_g0 = got2_ref[:, 16:24, :]
    all_g1 = got4_ref[:, 16:24, :]
    gamma0 = alpha_ref[1:2, :]
    gamma1 = gathered_total(all_g1, all_g1)
    cross = gathered_total(all_g1, all_g0)
    beta = gamma1 / gamma0
    im1 = fold(got4_ref[:, 0:16, :]) + beta * fold(got2_ref[:, 0:16, :])
    scalar_ref[0:1, :] = beta
    scalar_ref[1:2, :] = gamma1
    scalar_ref[2:3, :] = gamma1 + (2.0 * cross + beta * gamma0) * beta
    square = jnp.broadcast_to(total(im1 * im1), (8, 128))
    for i in range(8):
        send_ref[i, 0:16, :] = im1
        send_ref[i, 16:24, :] = square


def drive_kernel(got5_ref, got3_ref, got2_ref, got4_ref, alpha_ref, scalar_ref, send_ref):
    alpha0 = alpha_ref[0:1, :]
    beta = scalar_ref[0:1, :]
    norm = fold(got5_ref[:, 16:17, :])
    alpha1 = scalar_ref[1:2, :] / (norm + tikhonov * scalar_ref[2:3, :])
    from_first = alpha0 + alpha1 * beta
    for u in range(8):
        rows = from_first * got2_ref[u, 16:24, :] + alpha1 * got4_ref[u, 16:24, :]
        for i in range(8):
            send_ref[i, 8 * u : 8 * u + 8, :] = rows
    for half in range(2):
        member = half * 4 + lax.axis_index(("yhi", "zc"))
        change = alpha0 * got3_ref[member, 8:24, :] + alpha1 * got5_ref[member, 0:16, :]
        for i in range(8):
            send_ref[i, 64 + half : 65 + half, :] = change[i : i + 1, :]
            send_ref[i, 66 + half : 67 + half, :] = change[8 + i : 9 + i, :]


ROWS = 72


def of_fields(got_ref, row):
    return got_ref[pl.ds(row, 8, stride=ROWS), :]


def field_kernel(
    got_ref, high_ref, low_ref, desired_ref, cells_ref, drives_ref, residual_ref, field_ref
):
    for part in range(2):
        for half in range(2):
            lanes = slice(half * 128, half * 128 + 128)
            residual_ref[part, :, lanes] = desired_ref[part, :, lanes] - of_fields(
                got_ref, 64 + part * 2 + half
            )
    first_cell = lax.axis_index(SPK) * 2
    cells = jnp.concatenate([cells_ref[pl.ds(first_cell + blk, 1), :] for blk in range(2)], axis=1)
    pick = jnp.where(iota((128, 256), 0) == jnp.bitwise_and(cells, 127), 1.0, 0.0).astype(bf16)
    line = iota((64, 256), 0)
    place = jnp.right_shift(line, 3) * 4 + jnp.bitwise_and(line, 3)
    right = place == jnp.right_shift(cells, 7)
    is_real = jnp.bitwise_and(line, 4) == 0
    real_mask = jnp.where(right & is_real, 1.0, 0.0)
    imag_mask = jnp.where(right & ~is_real, 1.0, 0.0)
    for f in range(8):
        x = got_ref[f * ROWS : f * ROWS + 64, :]
        high = x.astype(bf16)
        left = x - high.astype(f32)
        middle, low = split_bf16(left)
        three = jnp.concatenate([high, middle, low], axis=0)
        picked = jnp.dot(three, pick, preferred_element_type=f32)
        picked = picked[0:64] + picked[64:128] + picked[128:192]
        drives_ref[0, f : f + 1, :] = jnp.sum(picked * real_mask, axis=0, keepdims=True)
        drives_ref[1, f : f + 1, :] = jnp.sum(picked * imag_mask, axis=0, keepdims=True)
    out = jnp.zeros((32, 256), f32)
    fine = jnp.zeros((16, 256), f32)
    dims = (((1,), (1,)), ((), ()))
    for u in range(8):
        for pair in range(2):
            parts = [
                jnp.concatenate(
                    [of_fields(got_ref, u * 8 + part * 4 + pair * 2 + k) for k in range(2)], axis=1
                )
                for part in range(2)
            ]
            high, low = split_bf16(jnp.concatenate(parts, axis=0))
            both = jnp.concatenate([high, low], axis=0)
            at = (u * 2 + pair) * 256
            lanes = slice(at, at + 256)
            out = out + lax.dot_general(both, high_ref[:, lanes], dims, preferred_element_type=f32)
            rest = low_ref[:, lanes].astype(bf16)
            fine = fine + lax.dot_general(high, rest, dims, preferred_element_type=f32)
    out = out[0:16, :] + out[16:32, :] + fine * (1.0 / LOW_SCALE)
    field_ref[0] = out[0:8, 0:128] - out[8:16, 128:256]
    field_ref[1] = out[0:8, 128:256] + out[8:16, 0:128]


def exchange(array, axes):
    return lax.all_to_all(array, axes, split_axis=0, concat_axis=0, tiled=True)


def local(desired, spk_cells, pt_cells, eval_cells, wavenumber):
    send0 = call(
        prepare_kernel,
        shape(8, 8, 128),
        [vmem((2, 8, 256), f32), vmem((3, 256), f32), pltpu.SemaphoreType.DMA((2,))],
        WHOLE, "aa", "prepare", 1024,
    )(desired, pt_cells)
    got0 = exchange(send0, FLD)
    g, send1 = call(
        first_kernel,
        (shape(8, 2, 512, 128), shape(8, 8, 128)),
        [vmem((8, 64, 128), f32), vmem((8, 8, 128), f32), vmem((2, 512, 128), f32)],
        8, "sv", "first", 524288 * 48, 524288,
    )(wavenumber, got0)
    got1 = exchange(send1, NEAR)
    send2, g0 = call(
        image_kernel,
        (shape(8, 24, 128), shape(8, 128)),
        [vmem((2, 512, 128), f32), vmem((16, 128), f32)], 8, "vv", "image", 524288 * 8,
    )(g, got1)
    got2 = exchange(send2, BANKS)
    send3 = call(
        adjoint_kernel, shape(8, 32, 128), [vmem((2, 512, 128), f32)], 8, "vv", "adjoint", 524288 * 8,
    )(g, got2)
    got3 = exchange(send3, NEAR)
    send4, alpha = call(
        second_image_kernel,
        (shape(8, 24, 128), shape(2, 128)),
        [vmem((2, 512, 128), f32), vmem((16, 128), f32)], 8, "vvvv", "second_image", 524288 * 8,
    )(g, got3, got2, g0)
    got4 = exchange(send4, BANKS)
    send5, scalars = call(
        norm_kernel, (shape(8, 24, 128), shape(3, 128)), [], 8, "vvv", "norm", 81920,
    )(got4, got2, alpha)
    got5 = exchange(send5, NEAR)
    send6 = call(
        drive_kernel, shape(8, ROWS, 128), [], 8, "vvvvvv", "drive", 81920,
    )(got5, got3, got2, got4, alpha, scalars)
    got6 = exchange(send6, FLD)
    eval_cells, got5 = lax.optimization_barrier((eval_cells, got5))
    high, low = call(
        eval_green_kernel,
        (shape(256, 4096, dtype=bf16), shape(256, 4096, dtype=f8)),
        [], 8, "sv", "eval_green", 524288 * 40, 524288,
    )(wavenumber, eval_cells)
    return call(
        field_kernel,
        (shape(2, 8, 256), shape(2, 8, 256), shape(2, 8, 128)),
        [], 12, "vvvvv", "field", 524288 * 96,
    )(got6.reshape(8 * ROWS, 128), high, low, desired, spk_cells.reshape(32, 128))


def solution(mesh):
    split = Mesh(
        mesh.devices.reshape(2, 4, 2, 2, 4, 2, 2), ("ylo", "x", "core", "yhi", "za", "zb", "zc")
    )
    in_specs = (P(None, None, PTS), P(), P(None, PTS), P(None, SPK + PTS), P())
    out_specs = (P(None, None, SPK), P(None, None, PTS), P(None, None, SPK + PTS))
    return jax.shard_map(local, mesh=split, in_specs=in_specs, out_specs=out_specs, check_vma=False)
```

```python
import math

import jax
import jax.numpy as jnp
from jax import lax
from jax.experimental import pallas as pl
from jax.experimental.pallas import tpu as pltpu
from jax.sharding import Mesh
from jax.sharding import PartitionSpec as P

WALL = 64
SPK = ("ylo", "x", "core")
PTS = ("yhi", "za", "zb", "zc")
FLD = ("za", "zb")
BANKS = ("x", "core")
NEAR = ("ylo", "yhi", "zc")

wall_pitch = 0.05
front_gap = 0.5
depth_span = 3.15
side_span = 3.2
tikhonov = 0.1
centre = (WALL - 1) * 0.5

SIN = (4.442879676818848, -7.307816505432129, 3.5977742671966553, -0.7911993861198425)
COS = (-1.4142040014266968, 6.97763729095459, -5.715188026428223, 1.728213906288147)
ROUNDER = 12582912.0
LOW_SCALE = 4194304.0

f32 = jnp.float32
f8 = jnp.float8_e4m3fn
bf16 = jnp.bfloat16
vmem = pltpu.VMEM


def spec(space=pltpu.VMEM):
    return pl.BlockSpec(memory_space=space)


def shape(*dims, dtype=f32):
    return jax.ShapeDtypeStruct(dims, dtype)


WHOLE = 64
SPACES = {"s": pltpu.SMEM, "v": pltpu.VMEM, "a": pl.ANY, "h": pltpu.HBM}


def call(kernel, out_shapes, scratch, limit_mib, spaces, name, flops, trans=0, out_spaces=None):
    return pl.pallas_call(
        kernel,
        out_shape=out_shapes,
        in_specs=[spec(SPACES[c]) for c in spaces],
        out_specs=tuple(spec(SPACES[c]) for c in out_spaces)
        if out_spaces
        else jax.tree.map(lambda _: spec(), out_shapes),
        scratch_shapes=scratch,
        compiler_params=pltpu.CompilerParams(vmem_limit_bytes=min(int(limit_mib * (1 << 20)), 67043328)),
        cost_estimate=pl.CostEstimate(flops=flops, bytes_accessed=1 << 20, transcendentals=trans),
        name=name,
    )


def poly(coeffs, u):
    out = coeffs[-1]
    for c in coeffs[-2::-1]:
        out = out * u + c
    return out


def green(scaled, strength):
    inverse = lax.rsqrt(scaled)
    turns = scaled * inverse
    magnitude = inverse * strength
    whole = (turns + ROUNDER) - ROUNDER
    frac = turns - whole
    u = frac * frac
    s = poly(SIN, u) * frac
    c = poly(COS, u)
    ms = magnitude * s
    return magnitude - ms * s, ms * c


def column(row):
    return jnp.broadcast_to(row, (128, 128)).T


def total(x):
    return jnp.broadcast_to(jnp.sum(x, keepdims=True), (1, 128))


def fold(x):
    out = x[0]
    for i in range(1, x.shape[0]):
        out = out + x[i]
    return out


def split_bf16(x):
    high = x.astype(bf16)
    return high, (x - high.astype(f32)).astype(bf16)


def iota(dims, dim):
    return lax.broadcasted_iota(jnp.int32, dims, dim)


def prepare_kernel(desired_hbm, points_hbm, send_ref, desired_ref, points_ref, sems):
    copies = [
        pltpu.make_async_copy(desired_hbm, desired_ref, sems.at[0]),
        pltpu.make_async_copy(points_hbm, points_ref, sems.at[1]),
    ]
    for copy in copies:
        copy.start()
    lanes = pl.ds(pl.multiple_of(lax.axis_index("ylo") * 128, 128), 128)
    for copy in copies:
        copy.wait()
    points = points_ref[:, lanes]
    for f in range(8):
        send_ref[f, 0:1, :] = desired_ref[0, f : f + 1, lanes]
        send_ref[f, 1:2, :] = desired_ref[1, f : f + 1, lanes]
        send_ref[f, 2:5, :] = points


def eval_green_kernel(wave_ref, eval_ref, high_ref, low_ref):
    kappa = wave_ref[0] * (0.5 / math.pi)
    strength = kappa * (1.0 / WALL)
    ex = column((front_gap + eval_ref[0:1, :] * depth_span) * kappa)
    ey = column((eval_ref[1:2, :] * side_span - 0.5 * side_span) * kappa)
    ez = column((eval_ref[2:3, :] * side_span - 0.5 * side_span) * kappa)
    lane = iota((1, 128), 1)
    dz = ez - (jnp.bitwise_and(lane, WALL - 1).astype(f32) - centre) * (wall_pitch * kappa)
    base = ex * ex + dz * dz

    def step(i, carry):
        wall_row = i * 2 + jnp.right_shift(lane, 6)
        wy = (wall_row.astype(f32) - centre) * (wall_pitch * kappa)
        lanes = pl.ds(pl.multiple_of(i * 128, 128), 128)
        for start in range(0, 128, 64):
            rows = slice(start, start + 64)
            dy = ey[rows] - wy
            real, imag = green(base[rows] + dy * dy, strength)
            for first, value in ((start, real), (128 + start, imag)):
                high = value.astype(bf16)
                high_ref[first : first + 64, lanes] = high
                low_ref[first : first + 64, lanes] = ((value - high.astype(f32)) * LOW_SCALE).astype(f8)
        return carry

    lax.fori_loop(0, 32, step, 0)


def first_kernel(wave_ref, got_ref, g_ref, send_ref, dz2_ref, rest_ref, acc_ref):
    kappa = wave_ref[0] * (0.5 / math.pi)
    strength = kappa * (1.0 / WALL)
    wz = (iota((WALL, 128), 0).astype(f32) - centre) * (wall_pitch * kappa)
    wy = ((iota((8, 128), 0) + lax.axis_index(BANKS) * 8).astype(f32) - centre) * (wall_pitch * kappa)
    for j in range(8):
        px = (front_gap + got_ref[j, 2:3, :] * depth_span) * kappa
        py = (got_ref[j, 3:4, :] * side_span - 0.5 * side_span) * kappa
        pz = (got_ref[j, 4:5, :] * side_span - 0.5 * side_span) * kappa
        dz = pz - wz
        dz2_ref[j] = dz * dz
        dy = py - wy
        rest_ref[j] = px * px + dy * dy
    size = 32

    def wall_row(r, carry):
        for start in range(0, WALL, size):
            rows = pl.ds(pl.multiple_of(r * WALL + start, size), size)

            def block(j, sums):
                real_sum, imag_sum = sums
                vr = got_ref[j, 0:1, :]
                vi = got_ref[j, 1:2, :]
                real, imag = green(
                    dz2_ref[j, start : start + size, :] + rest_ref[j, pl.ds(r, 1), :], strength
                )
                g_ref[j, 0, rows, :] = real
                g_ref[j, 1, rows, :] = imag
                real_sum = real_sum + (real * vr + imag * vi)
                imag_sum = imag_sum + (real * vi - imag * vr)
                return real_sum, imag_sum

            zero = jnp.zeros((size, 128), f32)
            real_sum, imag_sum = lax.fori_loop(0, 8, block, (zero, zero), unroll=2)
            acc_ref[0, rows, :] = real_sum
            acc_ref[1, rows, :] = imag_sum
        return carry

    lax.fori_loop(0, 8, wall_row, 0)
    rows = rows_of(acc_ref)
    for i in range(8):
        send_ref[i] = rows


def rows_of(acc_ref):
    rows = []
    for part in range(2):
        for blk in range(4):
            block = acc_ref[part, blk * 128 : blk * 128 + 128, :]
            rows.append(jnp.sum(block.T, axis=0, keepdims=True))
    return jnp.concatenate(rows, axis=0)


def forward(g_ref, rows, col_ref, out_ref):
    for part in range(2):
        for blk in range(4):
            i = part * 4 + blk
            col_ref[part, blk * 128 : blk * 128 + 128, :] = column(rows[i : i + 1, :])
    size = 64

    def step(t, carry):
        real_sum = jnp.zeros((8, 128), f32)
        imag_sum = jnp.zeros((8, 128), f32)
        for k in range(512 // size):
            at = slice(k * size, k * size + size)
            gr = g_ref[t, 0, at, :]
            gi = g_ref[t, 1, at, :]
            qr = col_ref[0, at, :]
            qi = col_ref[1, at, :]
            real_sum = real_sum + (gr * qr - gi * qi).reshape(size // 8, 8, 128).sum(axis=0)
            imag_sum = imag_sum + (gi * qr + gr * qi).reshape(size // 8, 8, 128).sum(axis=0)
        out_ref[pl.ds(t, 1), :] = jnp.sum(real_sum, axis=0, keepdims=True)
        out_ref[pl.ds(t + 8, 1), :] = jnp.sum(imag_sum, axis=0, keepdims=True)
        return carry

    lax.fori_loop(0, 8, step, 0)


def adjoint(g_ref, im, acc_ref):
    size = 64

    def chunk(k, carry):
        rows = pl.ds(pl.multiple_of(k * size, size), size)
        real_sum = jnp.zeros((size, 128), f32)
        imag_sum = jnp.zeros((size, 128), f32)
        for t in range(8):
            vr = im[t : t + 1, :]
            vi = im[8 + t : 9 + t, :]
            gr = g_ref[t, 0, rows, :]
            gi = g_ref[t, 1, rows, :]
            real_sum = real_sum + (gr * vr + gi * vi)
            imag_sum = imag_sum + (gr * vi - gi * vr)
        acc_ref[0, rows, :] = real_sum
        acc_ref[1, rows, :] = imag_sum
        return carry

    lax.fori_loop(0, 512 // size, chunk, 0)
    return rows_of(acc_ref)


def image_kernel(g_ref, got_ref, send_ref, own_ref, col_ref, im_ref):
    g0 = fold(got_ref)
    own_ref[...] = g0
    forward(g_ref, g0, col_ref, im_ref)
    im = im_ref[...]
    for i in range(8):
        send_ref[i, 0:16, :] = im
        send_ref[i, 16:24, :] = g0


def adjoint_kernel(g_ref, got_ref, send_ref, acc_ref):
    im = fold(got_ref[:, 0:16, :])
    rows = adjoint(g_ref, im, acc_ref)
    norm = jnp.broadcast_to(total(im * im), (8, 128))
    for i in range(8):
        send_ref[i, 0:8, :] = rows
        send_ref[i, 8:24, :] = im
        send_ref[i, 24:32, :] = norm


def gathered_total(a, b):
    return total(fold(a * b))


def second_image_kernel(g_ref, got3_ref, got2_ref, g0_ref, send_ref, alpha_ref, col_ref, im_ref):
    all_g0 = got2_ref[:, 16:24, :]
    gamma = gathered_total(all_g0, all_g0)
    g0 = g0_ref[...]
    back = fold(got3_ref[:, 0:8, :])
    norm = fold(got3_ref[:, 24:25, :])
    alpha = gamma / (norm + tikhonov * gamma)
    alpha_ref[0:1, :] = alpha
    alpha_ref[1:2, :] = gamma
    g1 = g0 - alpha * (back + tikhonov * g0)
    forward(g_ref, g1, col_ref, im_ref)
    im = im_ref[...]
    for i in range(8):
        send_ref[i, 0:16, :] = im
        send_ref[i, 16:24, :] = g1


def norm_kernel(got4_ref, got2_ref, alpha_ref, send_ref, scalar_ref):
    all_g0 = got2_ref[:, 16:24, :]
    all_g1 = got4_ref[:, 16:24, :]
    gamma0 = alpha_ref[1:2, :]
    gamma1 = gathered_total(all_g1, all_g1)
    cross = gathered_total(all_g1, all_g0)
    beta = gamma1 / gamma0
    im1 = fold(got4_ref[:, 0:16, :]) + beta * fold(got2_ref[:, 0:16, :])
    scalar_ref[0:1, :] = beta
    scalar_ref[1:2, :] = gamma1
    scalar_ref[2:3, :] = gamma1 + (2.0 * cross + beta * gamma0) * beta
    square = jnp.broadcast_to(total(im1 * im1), (8, 128))
    for i in range(8):
        send_ref[i, 0:16, :] = im1
        send_ref[i, 16:24, :] = square


def drive_kernel(got5_ref, got3_ref, got2_ref, got4_ref, alpha_ref, scalar_ref, send_ref):
    alpha0 = alpha_ref[0:1, :]
    beta = scalar_ref[0:1, :]
    norm = fold(got5_ref[:, 16:17, :])
    alpha1 = scalar_ref[1:2, :] / (norm + tikhonov * scalar_ref[2:3, :])
    from_first = alpha0 + alpha1 * beta
    core = lax.axis_index("core")
    for k in range(4):
        bank = core * 4 + k
        rows = from_first * got2_ref[bank, 16:24, :] + alpha1 * got4_ref[bank, 16:24, :]
        for i in range(8):
            send_ref[i, 8 * k : 8 * k + 8, :] = rows
    for half in range(2):
        member = half * 4 + lax.axis_index(("yhi", "zc"))
        change = alpha0 * got3_ref[member, 8:24, :] + alpha1 * got5_ref[member, 0:16, :]
        for i in range(8):
            send_ref[i, 32 + half : 33 + half, :] = change[i : i + 1, :]
            send_ref[i, 34 + half : 35 + half, :] = change[8 + i : 9 + i, :]


ROWS = 40


def of_fields(got_ref, row):
    return got_ref[pl.ds(row, 8, stride=ROWS), :]


def field_part(got_ref, half, high_ref, low_ref, cells_ref):
    first_cell = lax.axis_index(SPK) * 2
    cells = jnp.concatenate([cells_ref[pl.ds(first_cell + blk, 1), :] for blk in range(2)], axis=1)
    pick = jnp.where(iota((128, 256), 0) == jnp.bitwise_and(cells, 127), 1.0, 0.0).astype(bf16)
    line = iota((32, 256), 0)
    place = half * 16 + jnp.right_shift(line, 3) * 4 + jnp.bitwise_and(line, 3)
    right = place == jnp.right_shift(cells, 7)
    is_real = jnp.bitwise_and(line, 4) == 0
    masks = [jnp.where(right & is_real, 1.0, 0.0), jnp.where(right & ~is_real, 1.0, 0.0)]
    drives = [[], []]
    for f in range(8):
        x = got_ref[f * ROWS : f * ROWS + 32, :]
        high = x.astype(bf16)
        middle, low = split_bf16(x - high.astype(f32))
        three = jnp.concatenate([high, middle, low], axis=0)
        picked = jnp.dot(three, pick, preferred_element_type=f32)
        picked = picked[0:32] + picked[32:64] + picked[64:96]
        for part in range(2):
            drives[part].append(jnp.sum(picked * masks[part], axis=0, keepdims=True))
    out = jnp.zeros((32, 256), f32)
    fine = jnp.zeros((16, 256), f32)
    dims = (((1,), (1,)), ((), ()))
    for k in range(4):
        for pair in range(2):
            parts = [
                jnp.concatenate(
                    [of_fields(got_ref, k * 8 + part * 4 + pair * 2 + i) for i in range(2)], axis=1
                )
                for part in range(2)
            ]
            high, low = split_bf16(jnp.concatenate(parts, axis=0))
            both = jnp.concatenate([high, low], axis=0)
            lanes = pl.ds(pl.multiple_of(half * 2048 + (k * 2 + pair) * 256, 256), 256)
            out = out + lax.dot_general(both, high_ref[:, lanes], dims, preferred_element_type=f32)
            rest = low_ref[:, lanes].astype(bf16)
            fine = fine + lax.dot_general(high, rest, dims, preferred_element_type=f32)
    out = out[0:16, :] + out[16:32, :] + fine * (1.0 / LOW_SCALE)
    return [jnp.concatenate(rows, axis=0) for rows in drives], out


def near_field_kernel(
    got_ref, high_ref, low_ref, desired_ref, cells_ref, residual_ref, drives_ref, product_ref
):
    for part in range(2):
        for half in range(2):
            lanes = slice(half * 128, half * 128 + 128)
            residual_ref[part, :, lanes] = desired_ref[part, :, lanes] - of_fields(
                got_ref, 32 + part * 2 + half
            )
    drives, out = field_part(got_ref, lax.axis_index("core"), high_ref, low_ref, cells_ref)
    drives_ref[0] = drives[0]
    drives_ref[1] = drives[1]
    product_ref[...] = out


def far_field_kernel(
    got_ref, high_ref, low_ref, cells_ref, near_drives_ref, near_product_ref, drives_ref, field_ref
):
    drives, out = field_part(got_ref, 1 - lax.axis_index("core"), high_ref, low_ref, cells_ref)
    drives_ref[0] = near_drives_ref[0] + drives[0]
    drives_ref[1] = near_drives_ref[1] + drives[1]
    out = near_product_ref[...] + out
    field_ref[0] = out[0:8, 0:128] - out[8:16, 128:256]
    field_ref[1] = out[0:8, 128:256] + out[8:16, 0:128]


def exchange(array, axes):
    return lax.all_to_all(array, axes, split_axis=0, concat_axis=0, tiled=True)


def local(desired, spk_cells, pt_cells, eval_cells, wavenumber):
    send0 = call(
        prepare_kernel,
        shape(8, 8, 128),
        [vmem((2, 8, 256), f32), vmem((3, 256), f32), pltpu.SemaphoreType.DMA((2,))],
        WHOLE, "aa", "prepare", 1024,
    )(desired, pt_cells)
    got0 = exchange(send0, FLD)
    g, send1 = call(
        first_kernel,
        (shape(8, 2, 512, 128), shape(8, 8, 128)),
        [vmem((8, 64, 128), f32), vmem((8, 8, 128), f32), vmem((2, 512, 128), f32)],
        8, "sv", "first", 524288 * 48, 524288,
    )(wavenumber, got0)
    got1 = exchange(send1, NEAR)
    send2, g0 = call(
        image_kernel,
        (shape(8, 24, 128), shape(8, 128)),
        [vmem((2, 512, 128), f32), vmem((16, 128), f32)], 8, "vv", "image", 524288 * 8,
    )(g, got1)
    got2 = exchange(send2, BANKS)
    send3 = call(
        adjoint_kernel, shape(8, 32, 128), [vmem((2, 512, 128), f32)], 8, "vv", "adjoint", 524288 * 8,
    )(g, got2)
    got3 = exchange(send3, NEAR)
    send4, alpha = call(
        second_image_kernel,
        (shape(8, 24, 128), shape(2, 128)),
        [vmem((2, 512, 128), f32), vmem((16, 128), f32)], 8, "vvvv", "second_image", 524288 * 8,
    )(g, got3, got2, g0)
    got4 = exchange(send4, BANKS)
    send5, scalars = call(
        norm_kernel, (shape(8, 24, 128), shape(3, 128)), [], 8, "vvv", "norm", 81920,
    )(got4, got2, alpha)
    got5 = exchange(send5, NEAR)
    send6 = call(
        drive_kernel, shape(8, ROWS, 128), [], 8, "vvvvvv", "drive", 81920,
    )(got5, got3, got2, got4, alpha, scalars)
    got6 = exchange(send6, FLD)
    eval_cells, got5 = lax.optimization_barrier((eval_cells, got5))
    high, low = call(
        eval_green_kernel,
        (shape(256, 4096, dtype=bf16), shape(256, 4096, dtype=f8)),
        [], 8, "sv", "eval_green", 524288 * 40, 524288,
    )(wavenumber, eval_cells)
    got6, high, low = lax.optimization_barrier((got6.reshape(8 * ROWS, 128), high, low))
    other = lax.ppermute(got6, "core", [(0, 1), (1, 0)])
    cells = spk_cells.reshape(32, 128)
    residual, near_drives, product = call(
        near_field_kernel,
        (shape(2, 8, 256), shape(2, 8, 256), shape(16, 256)),
        [], 8, "vvvvv", "near_field", 524288 * 48,
    )(got6, high, low, desired, cells)
    drives, field = call(
        far_field_kernel,
        (shape(2, 8, 256), shape(2, 8, 128)),
        [], 8, "vvvvvv", "far_field", 524288 * 48,
    )(other, high, low, cells, near_drives, product)
    return drives, residual, field


def solution(mesh):
    split = Mesh(
        mesh.devices.reshape(2, 4, 2, 2, 4, 2, 2), ("ylo", "x", "core", "yhi", "za", "zb", "zc")
    )
    in_specs = (P(None, None, PTS), P(), P(None, PTS), P(None, SPK + PTS), P())
    out_specs = (P(None, None, SPK), P(None, None, PTS), P(None, None, SPK + PTS))
    return jax.shard_map(local, mesh=split, in_specs=in_specs, out_specs=out_specs, check_vma=False)
```

```python
import math

import jax
import jax.numpy as jnp
from jax import lax
from jax.experimental import pallas as pl
from jax.experimental.pallas import tpu as pltpu
from jax.sharding import Mesh
from jax.sharding import PartitionSpec as P

WALL = 64
SPK = ("ylo", "x", "core")
PTS = ("yhi", "za", "zb", "zc")
FLD = ("za", "zb")
BANKS = ("x", "core")
NEAR = ("ylo", "yhi", "zc")

wall_pitch = 0.05
front_gap = 0.5
depth_span = 3.15
side_span = 3.2
tikhonov = 0.1
centre = (WALL - 1) * 0.5

SIN = (4.442879676818848, -7.307816505432129, 3.5977742671966553, -0.7911993861198425)
COS = (-1.4142040014266968, 6.97763729095459, -5.715188026428223, 1.728213906288147)
ROUNDER = 12582912.0
LOW_SCALE = 4194304.0

f32 = jnp.float32
f8 = jnp.float8_e4m3fn
bf16 = jnp.bfloat16
vmem = pltpu.VMEM


def spec(space=pltpu.VMEM):
    return pl.BlockSpec(memory_space=space)


def shape(*dims, dtype=f32):
    return jax.ShapeDtypeStruct(dims, dtype)


WHOLE = 64
SPACES = {"s": pltpu.SMEM, "v": pltpu.VMEM, "a": pl.ANY, "h": pltpu.HBM}


def call(kernel, out_shapes, scratch, limit_mib, spaces, name, flops, trans=0, out_spaces=None):
    return pl.pallas_call(
        kernel,
        out_shape=out_shapes,
        in_specs=[spec(SPACES[c]) for c in spaces],
        out_specs=tuple(spec(SPACES[c]) for c in out_spaces)
        if out_spaces
        else jax.tree.map(lambda _: spec(), out_shapes),
        scratch_shapes=scratch,
        compiler_params=pltpu.CompilerParams(vmem_limit_bytes=min(int(limit_mib * (1 << 20)), 67043328)),
        cost_estimate=pl.CostEstimate(flops=flops, bytes_accessed=1 << 20, transcendentals=trans),
        name=name,
    )


def poly(coeffs, u):
    out = coeffs[-1]
    for c in coeffs[-2::-1]:
        out = out * u + c
    return out


def green(scaled, strength):
    inverse = lax.rsqrt(scaled)
    turns = scaled * inverse
    magnitude = inverse * strength
    whole = (turns + ROUNDER) - ROUNDER
    frac = turns - whole
    u = frac * frac
    s = poly(SIN, u) * frac
    c = poly(COS, u)
    ms = magnitude * s
    return magnitude - ms * s, ms * c


def column(row):
    return jnp.broadcast_to(row, (128, 128)).T


def total(x):
    return jnp.broadcast_to(jnp.sum(x, keepdims=True), (1, 128))


def fold(x):
    out = x[0]
    for i in range(1, x.shape[0]):
        out = out + x[i]
    return out


def split_bf16(x):
    high = x.astype(bf16)
    return high, (x - high.astype(f32)).astype(bf16)


def iota(dims, dim):
    return lax.broadcasted_iota(jnp.int32, dims, dim)


def prepare_kernel(desired_hbm, points_hbm, send_ref, desired_ref, points_ref, sems):
    copies = [
        pltpu.make_async_copy(desired_hbm, desired_ref, sems.at[0]),
        pltpu.make_async_copy(points_hbm, points_ref, sems.at[1]),
    ]
    for copy in copies:
        copy.start()
    lanes = pl.ds(pl.multiple_of(lax.axis_index("ylo") * 128, 128), 128)
    for copy in copies:
        copy.wait()
    points = points_ref[:, lanes]
    for f in range(8):
        send_ref[f, 0:1, :] = desired_ref[0, f : f + 1, lanes]
        send_ref[f, 1:2, :] = desired_ref[1, f : f + 1, lanes]
        send_ref[f, 2:5, :] = points


def eval_green_kernel(wave_ref, eval_ref, high_ref, low_ref):
    kappa = wave_ref[0] * (0.5 / math.pi)
    strength = kappa * (1.0 / WALL)
    ex = column((front_gap + eval_ref[0:1, :] * depth_span) * kappa)
    ey = column((eval_ref[1:2, :] * side_span - 0.5 * side_span) * kappa)
    ez = column((eval_ref[2:3, :] * side_span - 0.5 * side_span) * kappa)
    lane = iota((1, 128), 1)
    dz = ez - (jnp.bitwise_and(lane, WALL - 1).astype(f32) - centre) * (wall_pitch * kappa)
    base = ex * ex + dz * dz

    def step(i, carry):
        wall_row = i * 2 + jnp.right_shift(lane, 6)
        wy = (wall_row.astype(f32) - centre) * (wall_pitch * kappa)
        lanes = pl.ds(pl.multiple_of(i * 128, 128), 128)
        for start in range(0, 128, 64):
            rows = slice(start, start + 64)
            dy = ey[rows] - wy
            real, imag = green(base[rows] + dy * dy, strength)
            for first, value in ((start, real), (128 + start, imag)):
                high = value.astype(bf16)
                high_ref[first : first + 64, lanes] = high
                low_ref[first : first + 64, lanes] = ((value - high.astype(f32)) * LOW_SCALE).astype(f8)
        return carry

    lax.fori_loop(0, 32, step, 0)


def first_kernel(wave_ref, got_ref, g_ref, send_ref, dz2_ref, rest_ref, acc_ref):
    kappa = wave_ref[0] * (0.5 / math.pi)
    strength = kappa * (1.0 / WALL)
    wz = (iota((WALL, 128), 0).astype(f32) - centre) * (wall_pitch * kappa)
    wy = ((iota((8, 128), 0) + lax.axis_index(BANKS) * 8).astype(f32) - centre) * (wall_pitch * kappa)
    for j in range(8):
        px = (front_gap + got_ref[j, 2:3, :] * depth_span) * kappa
        py = (got_ref[j, 3:4, :] * side_span - 0.5 * side_span) * kappa
        pz = (got_ref[j, 4:5, :] * side_span - 0.5 * side_span) * kappa
        dz = pz - wz
        dz2_ref[j] = dz * dz
        dy = py - wy
        rest_ref[j] = px * px + dy * dy
    size = 32

    def wall_row(r, carry):
        for start in range(0, WALL, size):
            rows = pl.ds(pl.multiple_of(r * WALL + start, size), size)

            def block(j, sums):
                real_sum, imag_sum = sums
                vr = got_ref[j, 0:1, :]
                vi = got_ref[j, 1:2, :]
                real, imag = green(
                    dz2_ref[j, start : start + size, :] + rest_ref[j, pl.ds(r, 1), :], strength
                )
                g_ref[j, 0, rows, :] = real
                g_ref[j, 1, rows, :] = imag
                real_sum = real_sum + (real * vr + imag * vi)
                imag_sum = imag_sum + (real * vi - imag * vr)
                return real_sum, imag_sum

            zero = jnp.zeros((size, 128), f32)
            real_sum, imag_sum = lax.fori_loop(0, 8, block, (zero, zero), unroll=8)
            acc_ref[0, rows, :] = real_sum
            acc_ref[1, rows, :] = imag_sum
        return carry

    lax.fori_loop(0, 8, wall_row, 0)
    rows = rows_of(acc_ref)
    for i in range(8):
        send_ref[i] = rows


def rows_of(acc_ref):
    rows = []
    for part in range(2):
        for blk in range(4):
            block = acc_ref[part, blk * 128 : blk * 128 + 128, :]
            rows.append(jnp.sum(block.T, axis=0, keepdims=True))
    return jnp.concatenate(rows, axis=0)


def forward(g_ref, rows, col_ref, out_ref):
    for part in range(2):
        for blk in range(4):
            i = part * 4 + blk
            col_ref[part, blk * 128 : blk * 128 + 128, :] = column(rows[i : i + 1, :])
    size = 64

    def step(t, carry):
        real_sum = jnp.zeros((8, 128), f32)
        imag_sum = jnp.zeros((8, 128), f32)
        for k in range(512 // size):
            at = slice(k * size, k * size + size)
            gr = g_ref[t, 0, at, :]
            gi = g_ref[t, 1, at, :]
            qr = col_ref[0, at, :]
            qi = col_ref[1, at, :]
            real_sum = real_sum + (gr * qr - gi * qi).reshape(size // 8, 8, 128).sum(axis=0)
            imag_sum = imag_sum + (gi * qr + gr * qi).reshape(size // 8, 8, 128).sum(axis=0)
        out_ref[pl.ds(t, 1), :] = jnp.sum(real_sum, axis=0, keepdims=True)
        out_ref[pl.ds(t + 8, 1), :] = jnp.sum(imag_sum, axis=0, keepdims=True)
        return carry

    lax.fori_loop(0, 8, step, 0)


def adjoint(g_ref, im, acc_ref):
    size = 128

    def chunk(k, carry):
        rows = pl.ds(pl.multiple_of(k * size, size), size)
        real_sum = jnp.zeros((size, 128), f32)
        imag_sum = jnp.zeros((size, 128), f32)
        for t in range(8):
            vr = im[t : t + 1, :]
            vi = im[8 + t : 9 + t, :]
            gr = g_ref[t, 0, rows, :]
            gi = g_ref[t, 1, rows, :]
            real_sum = real_sum + (gr * vr + gi * vi)
            imag_sum = imag_sum + (gr * vi - gi * vr)
        acc_ref[0, rows, :] = real_sum
        acc_ref[1, rows, :] = imag_sum
        return carry

    lax.fori_loop(0, 512 // size, chunk, 0)
    return rows_of(acc_ref)


def image_kernel(g_ref, got_ref, send_ref, own_ref, col_ref, im_ref):
    g0 = fold(got_ref)
    own_ref[...] = g0
    forward(g_ref, g0, col_ref, im_ref)
    im = im_ref[...]
    for i in range(8):
        send_ref[i, 0:16, :] = im
        send_ref[i, 16:24, :] = g0


def adjoint_kernel(g_ref, got_ref, send_ref, acc_ref):
    im = fold(got_ref[:, 0:16, :])
    rows = adjoint(g_ref, im, acc_ref)
    norm = jnp.broadcast_to(total(im * im), (8, 128))
    for i in range(8):
        send_ref[i, 0:8, :] = rows
        send_ref[i, 8:24, :] = im
        send_ref[i, 24:32, :] = norm


def gathered_total(a, b):
    return total(fold(a * b))


def second_image_kernel(g_ref, got3_ref, got2_ref, g0_ref, send_ref, alpha_ref, col_ref, im_ref):
    all_g0 = got2_ref[:, 16:24, :]
    gamma = gathered_total(all_g0, all_g0)
    g0 = g0_ref[...]
    back = fold(got3_ref[:, 0:8, :])
    norm = fold(got3_ref[:, 24:25, :])
    alpha = gamma / (norm + tikhonov * gamma)
    alpha_ref[0:1, :] = alpha
    alpha_ref[1:2, :] = gamma
    g1 = g0 - alpha * (back + tikhonov * g0)
    forward(g_ref, g1, col_ref, im_ref)
    im = im_ref[...]
    for i in range(8):
        send_ref[i, 0:16, :] = im
        send_ref[i, 16:24, :] = g1


def norm_kernel(got4_ref, got2_ref, alpha_ref, send_ref, scalar_ref):
    all_g0 = got2_ref[:, 16:24, :]
    all_g1 = got4_ref[:, 16:24, :]
    gamma0 = alpha_ref[1:2, :]
    gamma1 = gathered_total(all_g1, all_g1)
    cross = gathered_total(all_g1, all_g0)
    beta = gamma1 / gamma0
    im1 = fold(got4_ref[:, 0:16, :]) + beta * fold(got2_ref[:, 0:16, :])
    scalar_ref[0:1, :] = beta
    scalar_ref[1:2, :] = gamma1
    scalar_ref[2:3, :] = gamma1 + (2.0 * cross + beta * gamma0) * beta
    square = jnp.broadcast_to(total(im1 * im1), (8, 128))
    for i in range(8):
        send_ref[i, 0:16, :] = im1
        send_ref[i, 16:24, :] = square


def drive_kernel(got5_ref, got3_ref, got2_ref, got4_ref, alpha_ref, scalar_ref, send_ref):
    alpha0 = alpha_ref[0:1, :]
    beta = scalar_ref[0:1, :]
    norm = fold(got5_ref[:, 16:17, :])
    alpha1 = scalar_ref[1:2, :] / (norm + tikhonov * scalar_ref[2:3, :])
    from_first = alpha0 + alpha1 * beta
    core = lax.axis_index("core")
    for k in range(4):
        bank = core * 4 + k
        rows = from_first * got2_ref[bank, 16:24, :] + alpha1 * got4_ref[bank, 16:24, :]
        for i in range(8):
            send_ref[i, 8 * k : 8 * k + 8, :] = rows
    for half in range(2):
        member = half * 4 + lax.axis_index(("yhi", "zc"))
        change = alpha0 * got3_ref[member, 8:24, :] + alpha1 * got5_ref[member, 0:16, :]
        for i in range(8):
            send_ref[i, 32 + half : 33 + half, :] = change[i : i + 1, :]
            send_ref[i, 34 + half : 35 + half, :] = change[8 + i : 9 + i, :]


ROWS = 40


def of_fields(got_ref, row):
    return got_ref[pl.ds(row, 8, stride=ROWS), :]


def field_part(got_ref, half, high_ref, low_ref, cells_ref):
    first_cell = lax.axis_index(SPK) * 2
    cells = jnp.concatenate([cells_ref[pl.ds(first_cell + blk, 1), :] for blk in range(2)], axis=1)
    pick = jnp.where(iota((128, 256), 0) == jnp.bitwise_and(cells, 127), 1.0, 0.0).astype(bf16)
    line = iota((32, 256), 0)
    place = half * 16 + jnp.right_shift(line, 3) * 4 + jnp.bitwise_and(line, 3)
    right = place == jnp.right_shift(cells, 7)
    is_real = jnp.bitwise_and(line, 4) == 0
    masks = [jnp.where(right & is_real, 1.0, 0.0), jnp.where(right & ~is_real, 1.0, 0.0)]
    drives = [[], []]
    for f in range(8):
        x = got_ref[f * ROWS : f * ROWS + 32, :]
        high = x.astype(bf16)
        middle, low = split_bf16(x - high.astype(f32))
        three = jnp.concatenate([high, middle, low], axis=0)
        picked = jnp.dot(three, pick, preferred_element_type=f32)
        picked = picked[0:32] + picked[32:64] + picked[64:96]
        for part in range(2):
            drives[part].append(jnp.sum(picked * masks[part], axis=0, keepdims=True))
    out = jnp.zeros((32, 256), f32)
    fine = jnp.zeros((16, 256), f32)
    dims = (((1,), (1,)), ((), ()))
    for k in range(4):
        for pair in range(2):
            parts = [
                jnp.concatenate(
                    [of_fields(got_ref, k * 8 + part * 4 + pair * 2 + i) for i in range(2)], axis=1
                )
                for part in range(2)
            ]
            high, low = split_bf16(jnp.concatenate(parts, axis=0))
            both = jnp.concatenate([high, low], axis=0)
            lanes = pl.ds(pl.multiple_of(half * 2048 + (k * 2 + pair) * 256, 256), 256)
            out = out + lax.dot_general(both, high_ref[:, lanes], dims, preferred_element_type=f32)
            rest = low_ref[:, lanes].astype(bf16)
            fine = fine + lax.dot_general(high, rest, dims, preferred_element_type=f32)
    out = out[0:16, :] + out[16:32, :] + fine * (1.0 / LOW_SCALE)
    return [jnp.concatenate(rows, axis=0) for rows in drives], out


def near_field_kernel(got_ref, high_ref, low_ref, cells_ref, drives_ref, product_ref):
    drives, out = field_part(got_ref, lax.axis_index("core"), high_ref, low_ref, cells_ref)
    drives_ref[0] = drives[0]
    drives_ref[1] = drives[1]
    product_ref[...] = out


def far_field_kernel(
    got_ref, high_ref, low_ref, cells_ref, near_drives_ref, near_product_ref, desired_ref, near_ref,
    drives_ref, residual_ref, field_ref,
):
    for part in range(2):
        for half in range(2):
            lanes = slice(half * 128, half * 128 + 128)
            residual_ref[part, :, lanes] = desired_ref[part, :, lanes] - of_fields(
                near_ref, 32 + part * 2 + half
            )
    drives, out = field_part(got_ref, 1 - lax.axis_index("core"), high_ref, low_ref, cells_ref)
    drives_ref[0] = near_drives_ref[0] + drives[0]
    drives_ref[1] = near_drives_ref[1] + drives[1]
    out = near_product_ref[...] + out
    field_ref[0] = out[0:8, 0:128] - out[8:16, 128:256]
    field_ref[1] = out[0:8, 128:256] + out[8:16, 0:128]


def exchange(array, axes):
    return lax.all_to_all(array, axes, split_axis=0, concat_axis=0, tiled=True)


def local(desired, spk_cells, pt_cells, eval_cells, wavenumber):
    send0 = call(
        prepare_kernel,
        shape(8, 8, 128),
        [vmem((2, 8, 256), f32), vmem((3, 256), f32), pltpu.SemaphoreType.DMA((2,))],
        WHOLE, "aa", "prepare", 1024,
    )(desired, pt_cells)
    got0 = exchange(send0, FLD)
    g, send1 = call(
        first_kernel,
        (shape(8, 2, 512, 128), shape(8, 8, 128)),
        [vmem((8, 64, 128), f32), vmem((8, 8, 128), f32), vmem((2, 512, 128), f32)],
        8, "sv", "first", 524288 * 48, 524288,
    )(wavenumber, got0)
    got1 = exchange(send1, NEAR)
    send2, g0 = call(
        image_kernel,
        (shape(8, 24, 128), shape(8, 128)),
        [vmem((2, 512, 128), f32), vmem((16, 128), f32)], 8, "vv", "image", 524288 * 8,
    )(g, got1)
    got2 = exchange(send2, BANKS)
    send3 = call(
        adjoint_kernel, shape(8, 32, 128), [vmem((2, 512, 128), f32)], 8, "vv", "adjoint", 524288 * 8,
    )(g, got2)
    got3 = exchange(send3, NEAR)
    send4, alpha = call(
        second_image_kernel,
        (shape(8, 24, 128), shape(2, 128)),
        [vmem((2, 512, 128), f32), vmem((16, 128), f32)], 8, "vvvv", "second_image", 524288 * 8,
    )(g, got3, got2, g0)
    got4 = exchange(send4, BANKS)
    send5, scalars = call(
        norm_kernel, (shape(8, 24, 128), shape(3, 128)), [], 8, "vvv", "norm", 81920,
    )(got4, got2, alpha)
    got5 = exchange(send5, NEAR)
    send6 = call(
        drive_kernel, shape(8, ROWS, 128), [], 8, "vvvvvv", "drive", 81920,
    )(got5, got3, got2, got4, alpha, scalars)
    got6 = exchange(send6, FLD)
    eval_cells, got5 = lax.optimization_barrier((eval_cells, got5))
    high, low = call(
        eval_green_kernel,
        (shape(256, 4096, dtype=bf16), shape(256, 4096, dtype=f8)),
        [], 8, "sv", "eval_green", 524288 * 40, 524288,
    )(wavenumber, eval_cells)
    got6, high, low = lax.optimization_barrier((got6.reshape(8 * ROWS, 128), high, low))
    other = lax.ppermute(got6, "core", [(0, 1), (1, 0)])
    cells = spk_cells.reshape(32, 128)
    near_drives, product = call(
        near_field_kernel,
        (shape(2, 8, 256), shape(16, 256)),
        [], 8, "vvvv", "near_field", 524288 * 48,
    )(got6, high, low, cells)
    return call(
        far_field_kernel,
        (shape(2, 8, 256), shape(2, 8, 256), shape(2, 8, 128)),
        [], 8, "vvvvvvvv", "far_field", 524288 * 48,
    )(other, high, low, cells, near_drives, product, desired, got6)


def solution(mesh):
    split = Mesh(
        mesh.devices.reshape(2, 4, 2, 2, 4, 2, 2), ("ylo", "x", "core", "yhi", "za", "zb", "zc")
    )
    in_specs = (P(None, None, PTS), P(), P(None, PTS), P(None, SPK + PTS), P())
    out_specs = (P(None, None, SPK), P(None, None, PTS), P(None, None, SPK + PTS))
    return jax.shard_map(local, mesh=split, in_specs=in_specs, out_specs=out_specs, check_vma=False)
```

```python
import math

import jax
import jax.numpy as jnp
from jax import lax
from jax.experimental import pallas as pl
from jax.experimental.pallas import tpu as pltpu
from jax.sharding import Mesh
from jax.sharding import PartitionSpec as P

WALL = 64
SPK = ("ylo", "x", "core")
PTS = ("yhi", "za", "zb", "zc")
FLD = ("zb", "za")
SPREAD = ("za", "zb")
BANKS = ("core", "x")
NEAR = ("zc", "yhi", "ylo")

wall_pitch = 0.05
front_gap = 0.5
depth_span = 3.15
side_span = 3.2
tikhonov = 0.1
centre = (WALL - 1) * 0.5

SIN = (4.442879676818848, -7.307816505432129, 3.5977742671966553, -0.7911993861198425)
COS = (-1.4142040014266968, 6.97763729095459, -5.715188026428223, 1.728213906288147)
ROUNDER = 12582912.0
LOW_SCALE = 4194304.0

f32 = jnp.float32
f8 = jnp.float8_e4m3fn
bf16 = jnp.bfloat16
vmem = pltpu.VMEM


def spec(space=pltpu.VMEM):
    return pl.BlockSpec(memory_space=space)


def shape(*dims, dtype=f32):
    return jax.ShapeDtypeStruct(dims, dtype)


WHOLE = 64
SPACES = {"s": pltpu.SMEM, "v": pltpu.VMEM, "a": pl.ANY, "h": pltpu.HBM}


def call(kernel, out_shapes, scratch, limit_mib, spaces, name, flops, trans=0, out_spaces=None):
    return pl.pallas_call(
        kernel,
        out_shape=out_shapes,
        in_specs=[spec(SPACES[c]) for c in spaces],
        out_specs=tuple(spec(SPACES[c]) for c in out_spaces)
        if out_spaces
        else jax.tree.map(lambda _: spec(), out_shapes),
        scratch_shapes=scratch,
        compiler_params=pltpu.CompilerParams(vmem_limit_bytes=min(int(limit_mib * (1 << 20)), 67043328)),
        cost_estimate=pl.CostEstimate(flops=flops, bytes_accessed=1 << 20, transcendentals=trans),
        name=name,
    )


def poly(coeffs, u):
    out = coeffs[-1]
    for c in coeffs[-2::-1]:
        out = out * u + c
    return out


def green(scaled, strength):
    inverse = lax.rsqrt(scaled)
    turns = scaled * inverse
    magnitude = inverse * strength
    whole = (turns + ROUNDER) - ROUNDER
    frac = turns - whole
    u = frac * frac
    s = poly(SIN, u) * frac
    c = poly(COS, u)
    ms = magnitude * s
    return magnitude - ms * s, ms * c


def column(row):
    return jnp.broadcast_to(row, (128, 128)).T


def total(x):
    return jnp.broadcast_to(jnp.sum(x, keepdims=True), (1, 128))


def fold(x):
    out = x[0]
    for i in range(1, x.shape[0]):
        out = out + x[i]
    return out


def split_bf16(x):
    high = x.astype(bf16)
    return high, (x - high.astype(f32)).astype(bf16)


def iota(dims, dim):
    return lax.broadcasted_iota(jnp.int32, dims, dim)


def prepare_kernel(desired_hbm, points_hbm, send_ref, desired_ref, points_ref, sems):
    copies = [
        pltpu.make_async_copy(desired_hbm, desired_ref, sems.at[0]),
        pltpu.make_async_copy(points_hbm, points_ref, sems.at[1]),
    ]
    for copy in copies:
        copy.start()
    lanes = pl.ds(pl.multiple_of(lax.axis_index("ylo") * 128, 128), 128)
    for copy in copies:
        copy.wait()
    points = points_ref[:, lanes]
    for i in range(8):
        f = i % 2 * 4 + i // 2
        send_ref[i, 0:1, :] = desired_ref[0, f : f + 1, lanes]
        send_ref[i, 1:2, :] = desired_ref[1, f : f + 1, lanes]
        send_ref[i, 2:5, :] = points


def eval_green_kernel(wave_ref, eval_ref, high_ref, low_ref):
    kappa = wave_ref[0] * (0.5 / math.pi)
    strength = kappa * (1.0 / WALL)
    ex = column((front_gap + eval_ref[0:1, :] * depth_span) * kappa)
    ey = column((eval_ref[1:2, :] * side_span - 0.5 * side_span) * kappa)
    ez = column((eval_ref[2:3, :] * side_span - 0.5 * side_span) * kappa)
    lane = iota((1, 128), 1)
    dz = ez - (jnp.bitwise_and(lane, WALL - 1).astype(f32) - centre) * (wall_pitch * kappa)
    base = ex * ex + dz * dz

    def step(i, carry):
        wall_row = i * 2 + jnp.right_shift(lane, 6)
        wy = (wall_row.astype(f32) - centre) * (wall_pitch * kappa)
        lanes = pl.ds(pl.multiple_of(i * 128, 128), 128)
        for start in range(0, 128, 64):
            rows = slice(start, start + 64)
            dy = ey[rows] - wy
            real, imag = green(base[rows] + dy * dy, strength)
            for first, value in ((start, real), (128 + start, imag)):
                high = value.astype(bf16)
                high_ref[first : first + 64, lanes] = high
                low_ref[first : first + 64, lanes] = ((value - high.astype(f32)) * LOW_SCALE).astype(f8)
        return carry

    lax.fori_loop(0, 32, step, 0)


def first_kernel(wave_ref, got_ref, g_ref, send_ref, dz2_ref, rest_ref, acc_ref):
    kappa = wave_ref[0] * (0.5 / math.pi)
    strength = kappa * (1.0 / WALL)
    wz = (iota((WALL, 128), 0).astype(f32) - centre) * (wall_pitch * kappa)
    wy = ((iota((8, 128), 0) + lax.axis_index(BANKS) * 8).astype(f32) - centre) * (wall_pitch * kappa)
    for j in range(8):
        i = j % 4 * 2 + j // 4
        px = (front_gap + got_ref[i, 2:3, :] * depth_span) * kappa
        py = (got_ref[i, 3:4, :] * side_span - 0.5 * side_span) * kappa
        pz = (got_ref[i, 4:5, :] * side_span - 0.5 * side_span) * kappa
        dz = pz - wz
        dz2_ref[j] = dz * dz
        dy = py - wy
        rest_ref[j] = px * px + dy * dy
    size = 32

    def wall_row(r, carry):
        for start in range(0, WALL, size):
            rows = pl.ds(pl.multiple_of(r * WALL + start, size), size)

            def block(j, sums):
                real_sum, imag_sum = sums
                i = jnp.bitwise_and(j, 3) * 2 + jnp.right_shift(j, 2)
                vr = got_ref[i, 0:1, :]
                vi = got_ref[i, 1:2, :]
                real, imag = green(
                    dz2_ref[j, start : start + size, :] + rest_ref[j, pl.ds(r, 1), :], strength
                )
                g_ref[j, 0, rows, :] = real
                g_ref[j, 1, rows, :] = imag
                real_sum = real_sum + (real * vr + imag * vi)
                imag_sum = imag_sum + (real * vi - imag * vr)
                return real_sum, imag_sum

            zero = jnp.zeros((size, 128), f32)
            real_sum, imag_sum = lax.fori_loop(0, 8, block, (zero, zero), unroll=8)
            acc_ref[0, rows, :] = real_sum
            acc_ref[1, rows, :] = imag_sum
        return carry

    lax.fori_loop(0, 8, wall_row, 0)
    rows = rows_of(acc_ref)
    for i in range(8):
        send_ref[i] = rows


def rows_of(acc_ref):
    rows = []
    for part in range(2):
        for blk in range(4):
            block = acc_ref[part, blk * 128 : blk * 128 + 128, :]
            rows.append(jnp.sum(block.T, axis=0, keepdims=True))
    return jnp.concatenate(rows, axis=0)


def forward(g_ref, rows, col_ref, out_ref):
    for part in range(2):
        for blk in range(4):
            i = part * 4 + blk
            col_ref[part, blk * 128 : blk * 128 + 128, :] = column(rows[i : i + 1, :])
    size = 64

    def step(t, carry):
        real_sum = jnp.zeros((8, 128), f32)
        imag_sum = jnp.zeros((8, 128), f32)
        for k in range(512 // size):
            at = slice(k * size, k * size + size)
            gr = g_ref[t, 0, at, :]
            gi = g_ref[t, 1, at, :]
            qr = col_ref[0, at, :]
            qi = col_ref[1, at, :]
            real_sum = real_sum + (gr * qr - gi * qi).reshape(size // 8, 8, 128).sum(axis=0)
            imag_sum = imag_sum + (gi * qr + gr * qi).reshape(size // 8, 8, 128).sum(axis=0)
        out_ref[pl.ds(t, 1), :] = jnp.sum(real_sum, axis=0, keepdims=True)
        out_ref[pl.ds(t + 8, 1), :] = jnp.sum(imag_sum, axis=0, keepdims=True)
        return carry

    lax.fori_loop(0, 8, step, 0)


def adjoint(g_ref, im, acc_ref):
    size = 128

    def chunk(k, carry):
        rows = pl.ds(pl.multiple_of(k * size, size), size)
        real_sum = jnp.zeros((size, 128), f32)
        imag_sum = jnp.zeros((size, 128), f32)
        for t in range(8):
            vr = im[t : t + 1, :]
            vi = im[8 + t : 9 + t, :]
            gr = g_ref[t, 0, rows, :]
            gi = g_ref[t, 1, rows, :]
            real_sum = real_sum + (gr * vr + gi * vi)
            imag_sum = imag_sum + (gr * vi - gi * vr)
        acc_ref[0, rows, :] = real_sum
        acc_ref[1, rows, :] = imag_sum
        return carry

    lax.fori_loop(0, 512 // size, chunk, 0)
    return rows_of(acc_ref)


def image_kernel(g_ref, got_ref, send_ref, own_ref, col_ref, im_ref):
    g0 = fold(got_ref)
    own_ref[...] = g0
    forward(g_ref, g0, col_ref, im_ref)
    im = im_ref[...]
    for i in range(8):
        send_ref[i, 0:16, :] = im
        send_ref[i, 16:24, :] = g0


def adjoint_kernel(g_ref, got_ref, send_ref, acc_ref):
    im = fold(got_ref[:, 0:16, :])
    rows = adjoint(g_ref, im, acc_ref)
    norm = jnp.broadcast_to(total(im * im), (8, 128))
    for i in range(8):
        send_ref[i, 0:8, :] = rows
        send_ref[i, 8:24, :] = im
        send_ref[i, 24:32, :] = norm


def gathered_total(a, b):
    return total(fold(a * b))


def second_image_kernel(g_ref, got3_ref, got2_ref, g0_ref, send_ref, alpha_ref, col_ref, im_ref):
    all_g0 = got2_ref[:, 16:24, :]
    gamma = gathered_total(all_g0, all_g0)
    g0 = g0_ref[...]
    back = fold(got3_ref[:, 0:8, :])
    norm = fold(got3_ref[:, 24:25, :])
    alpha = gamma / (norm + tikhonov * gamma)
    alpha_ref[0:1, :] = alpha
    alpha_ref[1:2, :] = gamma
    g1 = g0 - alpha * (back + tikhonov * g0)
    forward(g_ref, g1, col_ref, im_ref)
    im = im_ref[...]
    for i in range(8):
        send_ref[i, 0:16, :] = im
        send_ref[i, 16:24, :] = g1


def norm_kernel(got4_ref, got2_ref, alpha_ref, send_ref, scalar_ref):
    all_g0 = got2_ref[:, 16:24, :]
    all_g1 = got4_ref[:, 16:24, :]
    gamma0 = alpha_ref[1:2, :]
    gamma1 = gathered_total(all_g1, all_g1)
    cross = gathered_total(all_g1, all_g0)
    beta = gamma1 / gamma0
    im1 = fold(got4_ref[:, 0:16, :]) + beta * fold(got2_ref[:, 0:16, :])
    scalar_ref[0:1, :] = beta
    scalar_ref[1:2, :] = gamma1
    scalar_ref[2:3, :] = gamma1 + (2.0 * cross + beta * gamma0) * beta
    square = jnp.broadcast_to(total(im1 * im1), (8, 128))
    for i in range(8):
        send_ref[i, 0:16, :] = im1
        send_ref[i, 16:24, :] = square


def drive_kernel(got5_ref, got3_ref, got2_ref, got4_ref, alpha_ref, scalar_ref, send_ref):
    alpha0 = alpha_ref[0:1, :]
    beta = scalar_ref[0:1, :]
    norm = fold(got5_ref[:, 16:17, :])
    alpha1 = scalar_ref[1:2, :] / (norm + tikhonov * scalar_ref[2:3, :])
    from_first = alpha0 + alpha1 * beta
    core = lax.axis_index("core")
    for k in range(4):
        bank = core * 4 + k
        rows = from_first * got2_ref[bank, 16:24, :] + alpha1 * got4_ref[bank, 16:24, :]
        for i in range(8):
            send_ref[i, 8 * k : 8 * k + 8, :] = rows
    for half in range(2):
        member = lax.axis_index(("zc", "yhi")) * 2 + half
        change = alpha0 * got3_ref[member, 8:24, :] + alpha1 * got5_ref[member, 0:16, :]
        for i in range(8):
            send_ref[i, 32 + half : 33 + half, :] = change[i : i + 1, :]
            send_ref[i, 34 + half : 35 + half, :] = change[8 + i : 9 + i, :]


ROWS = 40


def of_fields(got_ref, row):
    return got_ref[pl.ds(row, 8, stride=ROWS), :]


def field_part(got_ref, half, high_ref, low_ref, cells_ref):
    first_cell = lax.axis_index(SPK) * 2
    cells = jnp.concatenate([cells_ref[pl.ds(first_cell + blk, 1), :] for blk in range(2)], axis=1)
    pick = jnp.where(iota((128, 256), 0) == jnp.bitwise_and(cells, 127), 1.0, 0.0).astype(bf16)
    line = iota((32, 256), 0)
    place = half * 16 + jnp.right_shift(line, 3) * 4 + jnp.bitwise_and(line, 3)
    right = place == jnp.right_shift(cells, 7)
    is_real = jnp.bitwise_and(line, 4) == 0
    masks = [jnp.where(right & is_real, 1.0, 0.0), jnp.where(right & ~is_real, 1.0, 0.0)]
    drives = [[], []]
    for f in range(8):
        x = got_ref[f * ROWS : f * ROWS + 32, :]
        high = x.astype(bf16)
        middle, low = split_bf16(x - high.astype(f32))
        three = jnp.concatenate([high, middle, low], axis=0)
        picked = jnp.dot(three, pick, preferred_element_type=f32)
        picked = picked[0:32] + picked[32:64] + picked[64:96]
        for part in range(2):
            drives[part].append(jnp.sum(picked * masks[part], axis=0, keepdims=True))
    out = jnp.zeros((32, 256), f32)
    fine = jnp.zeros((16, 256), f32)
    dims = (((1,), (1,)), ((), ()))
    for k in range(4):
        for pair in range(2):
            parts = [
                jnp.concatenate(
                    [of_fields(got_ref, k * 8 + part * 4 + pair * 2 + i) for i in range(2)], axis=1
                )
                for part in range(2)
            ]
            high, low = split_bf16(jnp.concatenate(parts, axis=0))
            both = jnp.concatenate([high, low], axis=0)
            lanes = pl.ds(pl.multiple_of(half * 2048 + (k * 2 + pair) * 256, 256), 256)
            out = out + lax.dot_general(both, high_ref[:, lanes], dims, preferred_element_type=f32)
            rest = low_ref[:, lanes].astype(bf16)
            fine = fine + lax.dot_general(high, rest, dims, preferred_element_type=f32)
    out = out[0:16, :] + out[16:32, :] + fine * (1.0 / LOW_SCALE)
    return [jnp.concatenate(rows, axis=0) for rows in drives], out


def near_field_kernel(got_ref, high_ref, low_ref, cells_ref, drives_ref, product_ref):
    drives, out = field_part(got_ref, lax.axis_index("core"), high_ref, low_ref, cells_ref)
    drives_ref[0] = drives[0]
    drives_ref[1] = drives[1]
    product_ref[...] = out


def far_field_kernel(
    got_ref, high_ref, low_ref, cells_ref, near_drives_ref, near_product_ref, desired_ref, near_ref,
    drives_ref, residual_ref, field_ref,
):
    for part in range(2):
        for half in range(2):
            lanes = slice(half * 128, half * 128 + 128)
            residual_ref[part, :, lanes] = desired_ref[part, :, lanes] - of_fields(
                near_ref, 32 + part * 2 + half
            )
    drives, out = field_part(got_ref, 1 - lax.axis_index("core"), high_ref, low_ref, cells_ref)
    drives_ref[0] = near_drives_ref[0] + drives[0]
    drives_ref[1] = near_drives_ref[1] + drives[1]
    out = near_product_ref[...] + out
    field_ref[0] = out[0:8, 0:128] - out[8:16, 128:256]
    field_ref[1] = out[0:8, 128:256] + out[8:16, 0:128]


def exchange(array, axes):
    return lax.all_to_all(array, axes, split_axis=0, concat_axis=0, tiled=True)


def local(desired, spk_cells, pt_cells, eval_cells, wavenumber):
    send0 = call(
        prepare_kernel,
        shape(8, 8, 128),
        [vmem((2, 8, 256), f32), vmem((3, 256), f32), pltpu.SemaphoreType.DMA((2,))],
        WHOLE, "aa", "prepare", 1024,
    )(desired, pt_cells)
    got0 = exchange(send0, SPREAD)
    g, send1 = call(
        first_kernel,
        (shape(8, 2, 512, 128), shape(8, 8, 128)),
        [vmem((8, 64, 128), f32), vmem((8, 8, 128), f32), vmem((2, 512, 128), f32)],
        8, "sv", "first", 524288 * 48, 524288,
    )(wavenumber, got0)
    got1 = exchange(send1, NEAR)
    send2, g0 = call(
        image_kernel,
        (shape(8, 24, 128), shape(8, 128)),
        [vmem((2, 512, 128), f32), vmem((16, 128), f32)], 8, "vv", "image", 524288 * 8,
    )(g, got1)
    got2 = exchange(send2, BANKS)
    send3 = call(
        adjoint_kernel, shape(8, 32, 128), [vmem((2, 512, 128), f32)], 8, "vv", "adjoint", 524288 * 8,
    )(g, got2)
    got3 = exchange(send3, NEAR)
    send4, alpha = call(
        second_image_kernel,
        (shape(8, 24, 128), shape(2, 128)),
        [vmem((2, 512, 128), f32), vmem((16, 128), f32)], 8, "vvvv", "second_image", 524288 * 8,
    )(g, got3, got2, g0)
    got4 = exchange(send4, BANKS)
    send5, scalars = call(
        norm_kernel, (shape(8, 24, 128), shape(3, 128)), [], 8, "vvv", "norm", 81920,
    )(got4, got2, alpha)
    got5 = exchange(send5, NEAR)
    send6 = call(
        drive_kernel, shape(8, ROWS, 128), [], 8, "vvvvvv", "drive", 81920,
    )(got5, got3, got2, got4, alpha, scalars)
    got6 = exchange(send6, FLD)
    eval_cells, got5 = lax.optimization_barrier((eval_cells, got5))
    high, low = call(
        eval_green_kernel,
        (shape(256, 4096, dtype=bf16), shape(256, 4096, dtype=f8)),
        [], 8, "sv", "eval_green", 524288 * 40, 524288,
    )(wavenumber, eval_cells)
    got6, high, low = lax.optimization_barrier((got6.reshape(8 * ROWS, 128), high, low))
    other = lax.ppermute(got6, "core", [(0, 1), (1, 0)])
    cells = spk_cells.reshape(32, 128)
    near_drives, product = call(
        near_field_kernel,
        (shape(2, 8, 256), shape(16, 256)),
        [], 8, "vvvv", "near_field", 524288 * 48,
    )(got6, high, low, cells)
    return call(
        far_field_kernel,
        (shape(2, 8, 256), shape(2, 8, 256), shape(2, 8, 128)),
        [], 8, "vvvvvvvv", "far_field", 524288 * 48,
    )(other, high, low, cells, near_drives, product, desired, got6)


def solution(mesh):
    split = Mesh(
        mesh.devices.reshape(2, 4, 2, 2, 4, 2, 2), ("ylo", "x", "core", "yhi", "za", "zb", "zc")
    )
    in_specs = (P(None, None, PTS), P(), P(None, PTS), P(None, SPK + PTS), P())
    out_specs = (P(None, None, SPK), P(None, None, PTS), P(None, None, SPK + PTS))
    return jax.shard_map(local, mesh=split, in_specs=in_specs, out_specs=out_specs, check_vma=False)
```

```python
import math

import jax
import jax.numpy as jnp
from jax import lax
from jax.experimental import pallas as pl
from jax.experimental.pallas import tpu as pltpu
from jax.sharding import Mesh
from jax.sharding import PartitionSpec as P

WALL = 64
SPK = ("ylo", "x", "core")
PTS = ("yhi", "za", "zb", "zc")
FLD = ("zb", "za")
SPREAD = ("za", "zb")
BANKS = ("core", "x")
NEAR = ("zc", "yhi", "ylo")

wall_pitch = 0.05
front_gap = 0.5
depth_span = 3.15
side_span = 3.2
tikhonov = 0.1
centre = (WALL - 1) * 0.5

SIN = (4.442879676818848, -7.307816505432129, 3.5977742671966553, -0.7911993861198425)
COS = (-1.4142040014266968, 6.97763729095459, -5.715188026428223, 1.728213906288147)
ROUNDER = 12582912.0
LOW_SCALE = 4194304.0

f32 = jnp.float32
f8 = jnp.float8_e4m3fn
bf16 = jnp.bfloat16
vmem = pltpu.VMEM


def spec(space=pltpu.VMEM):
    return pl.BlockSpec(memory_space=space)


def shape(*dims, dtype=f32):
    return jax.ShapeDtypeStruct(dims, dtype)


WHOLE = 64
SPACES = {"s": pltpu.SMEM, "v": pltpu.VMEM, "a": pl.ANY, "h": pltpu.HBM}


def call(kernel, out_shapes, scratch, limit_mib, spaces, name, flops, trans=0, out_spaces=None):
    return pl.pallas_call(
        kernel,
        out_shape=out_shapes,
        in_specs=[spec(SPACES[c]) for c in spaces],
        out_specs=tuple(spec(SPACES[c]) for c in out_spaces)
        if out_spaces
        else jax.tree.map(lambda _: spec(), out_shapes),
        scratch_shapes=scratch,
        compiler_params=pltpu.CompilerParams(vmem_limit_bytes=min(int(limit_mib * (1 << 20)), 67043328)),
        cost_estimate=pl.CostEstimate(flops=flops, bytes_accessed=1 << 20, transcendentals=trans),
        name=name,
    )


def poly(coeffs, u):
    out = coeffs[-1]
    for c in coeffs[-2::-1]:
        out = out * u + c
    return out


def green(scaled, strength):
    inverse = lax.rsqrt(scaled)
    turns = scaled * inverse
    magnitude = inverse * strength
    whole = (turns + ROUNDER) - ROUNDER
    frac = turns - whole
    u = frac * frac
    s = poly(SIN, u) * frac
    c = poly(COS, u)
    ms = magnitude * s
    return magnitude - ms * s, ms * c


def column(row):
    return jnp.broadcast_to(row, (128, 128)).T


def total(x):
    return jnp.broadcast_to(jnp.sum(x, keepdims=True), (1, 128))


def fold(x):
    out = x[0]
    for i in range(1, x.shape[0]):
        out = out + x[i]
    return out


def split_bf16(x):
    high = x.astype(bf16)
    return high, (x - high.astype(f32)).astype(bf16)


def iota(dims, dim):
    return lax.broadcasted_iota(jnp.int32, dims, dim)


def prepare_kernel(desired_hbm, points_hbm, send_ref, desired_ref, points_ref, sems):
    copies = [
        pltpu.make_async_copy(desired_hbm, desired_ref, sems.at[0]),
        pltpu.make_async_copy(points_hbm, points_ref, sems.at[1]),
    ]
    for copy in copies:
        copy.start()
    lanes = pl.ds(pl.multiple_of(lax.axis_index("ylo") * 128, 128), 128)
    for copy in copies:
        copy.wait()
    points = points_ref[:, lanes]
    for i in range(8):
        f = i % 2 * 4 + i // 2
        send_ref[i, 0:1, :] = desired_ref[0, f : f + 1, lanes]
        send_ref[i, 1:2, :] = desired_ref[1, f : f + 1, lanes]
        send_ref[i, 2:5, :] = points


def eval_green_kernel(wave_ref, eval_ref, high_ref, low_ref):
    kappa = wave_ref[0] * (0.5 / math.pi)
    strength = kappa * (1.0 / WALL)
    ex = column((front_gap + eval_ref[0:1, :] * depth_span) * kappa)
    ey = column((eval_ref[1:2, :] * side_span - 0.5 * side_span) * kappa)
    ez = column((eval_ref[2:3, :] * side_span - 0.5 * side_span) * kappa)
    lane = iota((1, 128), 1)
    dz = ez - (jnp.bitwise_and(lane, WALL - 1).astype(f32) - centre) * (wall_pitch * kappa)
    base = ex * ex + dz * dz

    def step(i, carry):
        wall_row = i * 2 + jnp.right_shift(lane, 6)
        wy = (wall_row.astype(f32) - centre) * (wall_pitch * kappa)
        lanes = pl.ds(pl.multiple_of(i * 128, 128), 128)
        for start in range(0, 128, 64):
            rows = slice(start, start + 64)
            dy = ey[rows] - wy
            real, imag = green(base[rows] + dy * dy, strength)
            for first, value in ((start, real), (128 + start, imag)):
                high = value.astype(bf16)
                high_ref[first : first + 64, lanes] = high
                low_ref[first : first + 64, lanes] = ((value - high.astype(f32)) * LOW_SCALE).astype(f8)
        return carry

    lax.fori_loop(0, 32, step, 0)


def first_kernel(wave_ref, got_ref, g_ref, send_ref, dz2_ref, rest_ref, acc_ref):
    kappa = wave_ref[0] * (0.5 / math.pi)
    strength = kappa * (1.0 / WALL)
    wz = (iota((WALL, 128), 0).astype(f32) - centre) * (wall_pitch * kappa)
    wy = ((iota((8, 128), 0) + lax.axis_index(BANKS) * 8).astype(f32) - centre) * (wall_pitch * kappa)
    for j in range(8):
        i = j % 4 * 2 + j // 4
        px = (front_gap + got_ref[i, 2:3, :] * depth_span) * kappa
        py = (got_ref[i, 3:4, :] * side_span - 0.5 * side_span) * kappa
        pz = (got_ref[i, 4:5, :] * side_span - 0.5 * side_span) * kappa
        dz = pz - wz
        dz2_ref[j] = dz * dz
        dy = py - wy
        rest_ref[j] = px * px + dy * dy
    size = 32

    def wall_row(r, carry):
        for start in range(0, WALL, size):
            rows = pl.ds(pl.multiple_of(r * WALL + start, size), size)

            def block(j, sums):
                real_sum, imag_sum = sums
                i = jnp.bitwise_and(j, 3) * 2 + jnp.right_shift(j, 2)
                vr = got_ref[i, 0:1, :]
                vi = got_ref[i, 1:2, :]
                real, imag = green(
                    dz2_ref[j, start : start + size, :] + rest_ref[j, pl.ds(r, 1), :], strength
                )
                g_ref[j, 0, rows, :] = real
                g_ref[j, 1, rows, :] = imag
                real_sum = real_sum + (real * vr + imag * vi)
                imag_sum = imag_sum + (real * vi - imag * vr)
                return real_sum, imag_sum

            zero = jnp.zeros((size, 128), f32)
            real_sum, imag_sum = lax.fori_loop(0, 8, block, (zero, zero), unroll=8)
            acc_ref[0, rows, :] = real_sum
            acc_ref[1, rows, :] = imag_sum
        return carry

    lax.fori_loop(0, 8, wall_row, 0)
    rows = rows_of(acc_ref)
    for i in range(8):
        send_ref[i] = rows


def rows_of(acc_ref):
    rows = []
    for part in range(2):
        for blk in range(4):
            block = acc_ref[part, blk * 128 : blk * 128 + 128, :]
            rows.append(jnp.sum(block.T, axis=0, keepdims=True))
    return jnp.concatenate(rows, axis=0)


def forward(g_ref, rows, col_ref, out_ref):
    for part in range(2):
        for blk in range(4):
            i = part * 4 + blk
            col_ref[part, blk * 128 : blk * 128 + 128, :] = column(rows[i : i + 1, :])
    size = 64

    def step(t, carry):
        real_sum = jnp.zeros((8, 128), f32)
        imag_sum = jnp.zeros((8, 128), f32)
        for k in range(512 // size):
            at = slice(k * size, k * size + size)
            gr = g_ref[t, 0, at, :]
            gi = g_ref[t, 1, at, :]
            qr = col_ref[0, at, :]
            qi = col_ref[1, at, :]
            real_sum = real_sum + (gr * qr - gi * qi).reshape(size // 8, 8, 128).sum(axis=0)
            imag_sum = imag_sum + (gi * qr + gr * qi).reshape(size // 8, 8, 128).sum(axis=0)
        out_ref[pl.ds(t, 1), :] = jnp.sum(real_sum, axis=0, keepdims=True)
        out_ref[pl.ds(t + 8, 1), :] = jnp.sum(imag_sum, axis=0, keepdims=True)
        return carry

    lax.fori_loop(0, 8, step, 0)


def adjoint(g_ref, im, acc_ref):
    size = 128

    def chunk(k, carry):
        rows = pl.ds(pl.multiple_of(k * size, size), size)
        real_sum = jnp.zeros((size, 128), f32)
        imag_sum = jnp.zeros((size, 128), f32)
        for t in range(8):
            vr = im[t : t + 1, :]
            vi = im[8 + t : 9 + t, :]
            gr = g_ref[t, 0, rows, :]
            gi = g_ref[t, 1, rows, :]
            real_sum = real_sum + (gr * vr + gi * vi)
            imag_sum = imag_sum + (gr * vi - gi * vr)
        acc_ref[0, rows, :] = real_sum
        acc_ref[1, rows, :] = imag_sum
        return carry

    lax.fori_loop(0, 512 // size, chunk, 0)
    return rows_of(acc_ref)


def image_kernel(g_ref, got_ref, send_ref, own_ref, col_ref, im_ref):
    g0 = fold(got_ref)
    own_ref[...] = g0
    forward(g_ref, g0, col_ref, im_ref)
    im = im_ref[...]
    for i in range(8):
        send_ref[i, 0:16, :] = im
        send_ref[i, 16:24, :] = g0


def adjoint_kernel(g_ref, got_ref, send_ref, acc_ref):
    im = fold(got_ref[:, 0:16, :])
    rows = adjoint(g_ref, im, acc_ref)
    for i in range(8):
        send_ref[i, 0:8, :] = rows
        send_ref[i, 8:24, :] = im


def gathered_total(a, b):
    return total(fold(a * b))


def second_image_kernel(g_ref, got3_ref, got2_ref, g0_ref, send_ref, alpha_ref, col_ref, im_ref):
    all_g0 = got2_ref[:, 16:24, :]
    gamma = gathered_total(all_g0, all_g0)
    g0 = g0_ref[...]
    back = fold(got3_ref[:, 0:8, :])
    all_im0 = got3_ref[:, 8:24, :]
    norm = gathered_total(all_im0, all_im0)
    alpha = gamma / (norm + tikhonov * gamma)
    alpha_ref[0:1, :] = alpha
    alpha_ref[1:2, :] = gamma
    g1 = g0 - alpha * (back + tikhonov * g0)
    forward(g_ref, g1, col_ref, im_ref)
    im = im_ref[...]
    for i in range(8):
        send_ref[i, 0:16, :] = im
        send_ref[i, 16:24, :] = g1


def norm_kernel(got4_ref, got2_ref, alpha_ref, send_ref, scalar_ref):
    all_g0 = got2_ref[:, 16:24, :]
    all_g1 = got4_ref[:, 16:24, :]
    gamma0 = alpha_ref[1:2, :]
    gamma1 = gathered_total(all_g1, all_g1)
    cross = gathered_total(all_g1, all_g0)
    beta = gamma1 / gamma0
    im1 = fold(got4_ref[:, 0:16, :]) + beta * fold(got2_ref[:, 0:16, :])
    scalar_ref[0:1, :] = beta
    scalar_ref[1:2, :] = gamma1
    scalar_ref[2:3, :] = gamma1 + (2.0 * cross + beta * gamma0) * beta
    for i in range(8):
        send_ref[i] = im1


def drive_kernel(got5_ref, got3_ref, got2_ref, got4_ref, alpha_ref, scalar_ref, send_ref):
    alpha0 = alpha_ref[0:1, :]
    beta = scalar_ref[0:1, :]
    all_im1 = got5_ref[...]
    norm = gathered_total(all_im1, all_im1)
    alpha1 = scalar_ref[1:2, :] / (norm + tikhonov * scalar_ref[2:3, :])
    from_first = alpha0 + alpha1 * beta
    core = lax.axis_index("core")
    for k in range(4):
        bank = core * 4 + k
        rows = from_first * got2_ref[bank, 16:24, :] + alpha1 * got4_ref[bank, 16:24, :]
        for i in range(8):
            send_ref[i, 8 * k : 8 * k + 8, :] = rows
    for half in range(2):
        member = lax.axis_index(("zc", "yhi")) * 2 + half
        change = alpha0 * got3_ref[member, 8:24, :] + alpha1 * got5_ref[member]
        for i in range(8):
            send_ref[i, 32 + half : 33 + half, :] = change[i : i + 1, :]
            send_ref[i, 34 + half : 35 + half, :] = change[8 + i : 9 + i, :]


ROWS = 40


def of_fields(got_ref, row):
    return got_ref[pl.ds(row, 8, stride=ROWS), :]


def field_part(got_ref, half, high_ref, low_ref, cells_ref):
    first_cell = lax.axis_index(SPK) * 2
    cells = jnp.concatenate([cells_ref[pl.ds(first_cell + blk, 1), :] for blk in range(2)], axis=1)
    pick = jnp.where(iota((128, 256), 0) == jnp.bitwise_and(cells, 127), 1.0, 0.0).astype(bf16)
    line = iota((32, 256), 0)
    place = half * 16 + jnp.right_shift(line, 3) * 4 + jnp.bitwise_and(line, 3)
    right = place == jnp.right_shift(cells, 7)
    is_real = jnp.bitwise_and(line, 4) == 0
    masks = [jnp.where(right & is_real, 1.0, 0.0), jnp.where(right & ~is_real, 1.0, 0.0)]
    drives = [[], []]
    for f in range(8):
        x = got_ref[f * ROWS : f * ROWS + 32, :]
        high = x.astype(bf16)
        middle, low = split_bf16(x - high.astype(f32))
        three = jnp.concatenate([high, middle, low], axis=0)
        picked = jnp.dot(three, pick, preferred_element_type=f32)
        picked = picked[0:32] + picked[32:64] + picked[64:96]
        for part in range(2):
            drives[part].append(jnp.sum(picked * masks[part], axis=0, keepdims=True))
    out = jnp.zeros((32, 256), f32)
    fine = jnp.zeros((16, 256), f32)
    dims = (((1,), (1,)), ((), ()))
    for k in range(4):
        for pair in range(2):
            parts = [
                jnp.concatenate(
                    [of_fields(got_ref, k * 8 + part * 4 + pair * 2 + i) for i in range(2)], axis=1
                )
                for part in range(2)
            ]
            high, low = split_bf16(jnp.concatenate(parts, axis=0))
            both = jnp.concatenate([high, low], axis=0)
            lanes = pl.ds(pl.multiple_of(half * 2048 + (k * 2 + pair) * 256, 256), 256)
            out = out + lax.dot_general(both, high_ref[:, lanes], dims, preferred_element_type=f32)
            rest = low_ref[:, lanes].astype(bf16)
            fine = fine + lax.dot_general(high, rest, dims, preferred_element_type=f32)
    out = out[0:16, :] + out[16:32, :] + fine * (1.0 / LOW_SCALE)
    return [jnp.concatenate(rows, axis=0) for rows in drives], out


def near_field_kernel(got_ref, high_ref, low_ref, cells_ref, drives_ref, product_ref):
    drives, out = field_part(got_ref, lax.axis_index("core"), high_ref, low_ref, cells_ref)
    drives_ref[0] = drives[0]
    drives_ref[1] = drives[1]
    product_ref[...] = out


def far_field_kernel(
    got_ref, high_ref, low_ref, cells_ref, near_drives_ref, near_product_ref, desired_ref, near_ref,
    drives_ref, residual_ref, field_ref,
):
    for part in range(2):
        for half in range(2):
            lanes = slice(half * 128, half * 128 + 128)
            residual_ref[part, :, lanes] = desired_ref[part, :, lanes] - of_fields(
                near_ref, 32 + part * 2 + half
            )
    drives, out = field_part(got_ref, 1 - lax.axis_index("core"), high_ref, low_ref, cells_ref)
    drives_ref[0] = near_drives_ref[0] + drives[0]
    drives_ref[1] = near_drives_ref[1] + drives[1]
    out = near_product_ref[...] + out
    field_ref[0] = out[0:8, 0:128] - out[8:16, 128:256]
    field_ref[1] = out[0:8, 128:256] + out[8:16, 0:128]


def exchange(array, axes):
    return lax.all_to_all(array, axes, split_axis=0, concat_axis=0, tiled=True)


def local(desired, spk_cells, pt_cells, eval_cells, wavenumber):
    send0 = call(
        prepare_kernel,
        shape(8, 8, 128),
        [vmem((2, 8, 256), f32), vmem((3, 256), f32), pltpu.SemaphoreType.DMA((2,))],
        WHOLE, "aa", "prepare", 1024,
    )(desired, pt_cells)
    got0 = exchange(send0, SPREAD)
    g, send1 = call(
        first_kernel,
        (shape(8, 2, 512, 128), shape(8, 8, 128)),
        [vmem((8, 64, 128), f32), vmem((8, 8, 128), f32), vmem((2, 512, 128), f32)],
        8, "sv", "first", 524288 * 48, 524288,
    )(wavenumber, got0)
    got1 = exchange(send1, NEAR)
    send2, g0 = call(
        image_kernel,
        (shape(8, 24, 128), shape(8, 128)),
        [vmem((2, 512, 128), f32), vmem((16, 128), f32)], 8, "vv", "image", 524288 * 8,
    )(g, got1)
    got2 = exchange(send2, BANKS)
    send3 = call(
        adjoint_kernel, shape(8, 24, 128), [vmem((2, 512, 128), f32)], 8, "vv", "adjoint", 524288 * 8,
    )(g, got2)
    got3 = exchange(send3, NEAR)
    send4, alpha = call(
        second_image_kernel,
        (shape(8, 24, 128), shape(2, 128)),
        [vmem((2, 512, 128), f32), vmem((16, 128), f32)], 8, "vvvv", "second_image", 524288 * 8,
    )(g, got3, got2, g0)
    got4 = exchange(send4, BANKS)
    send5, scalars = call(
        norm_kernel, (shape(8, 16, 128), shape(3, 128)), [], 8, "vvv", "norm", 81920,
    )(got4, got2, alpha)
    got5 = exchange(send5, NEAR)
    send6 = call(
        drive_kernel, shape(8, ROWS, 128), [], 8, "vvvvvv", "drive", 81920,
    )(got5, got3, got2, got4, alpha, scalars)
    got6 = exchange(send6, FLD)
    eval_cells, got5 = lax.optimization_barrier((eval_cells, got5))
    high, low = call(
        eval_green_kernel,
        (shape(256, 4096, dtype=bf16), shape(256, 4096, dtype=f8)),
        [], 8, "sv", "eval_green", 524288 * 40, 524288,
    )(wavenumber, eval_cells)
    got6, high, low = lax.optimization_barrier((got6.reshape(8 * ROWS, 128), high, low))
    other = lax.ppermute(got6, "core", [(0, 1), (1, 0)])
    cells = spk_cells.reshape(32, 128)
    near_drives, product = call(
        near_field_kernel,
        (shape(2, 8, 256), shape(16, 256)),
        [], 8, "vvvv", "near_field", 524288 * 48,
    )(got6, high, low, cells)
    return call(
        far_field_kernel,
        (shape(2, 8, 256), shape(2, 8, 256), shape(2, 8, 128)),
        [], 8, "vvvvvvvv", "far_field", 524288 * 48,
    )(other, high, low, cells, near_drives, product, desired, got6)


def solution(mesh):
    split = Mesh(
        mesh.devices.reshape(2, 4, 2, 2, 4, 2, 2), ("ylo", "x", "core", "yhi", "za", "zb", "zc")
    )
    in_specs = (P(None, None, PTS), P(), P(None, PTS), P(None, SPK + PTS), P())
    out_specs = (P(None, None, SPK), P(None, None, PTS), P(None, None, SPK + PTS))
    return jax.shard_map(local, mesh=split, in_specs=in_specs, out_specs=out_specs, check_vma=False)
```

```python
import math

import jax
import jax.numpy as jnp
from jax import lax
from jax.experimental import pallas as pl
from jax.experimental.pallas import tpu as pltpu
from jax.sharding import Mesh
from jax.sharding import PartitionSpec as P

WALL = 64
SPK = ("ylo", "x", "core")
PTS = ("yhi", "za", "zb", "zc")
FLD = ("zb", "za")
BANKS = ("core", "x")
NEAR = ("zc", "yhi", "ylo")

wall_pitch = 0.05
front_gap = 0.5
depth_span = 3.15
side_span = 3.2
tikhonov = 0.1
centre = (WALL - 1) * 0.5

SIN = (4.442879676818848, -7.307816505432129, 3.5977742671966553, -0.7911993861198425)
COS = (-1.4142040014266968, 6.97763729095459, -5.715188026428223, 1.728213906288147)
ROUNDER = 12582912.0
LOW_SCALE = 4194304.0

f32 = jnp.float32
f8 = jnp.float8_e4m3fn
bf16 = jnp.bfloat16
vmem = pltpu.VMEM


def spec(space=pltpu.VMEM):
    return pl.BlockSpec(memory_space=space)


def shape(*dims, dtype=f32):
    return jax.ShapeDtypeStruct(dims, dtype)


WHOLE = 64
SPACES = {"s": pltpu.SMEM, "v": pltpu.VMEM, "a": pl.ANY, "h": pltpu.HBM}


def call(kernel, out_shapes, scratch, limit_mib, spaces, name, flops, trans=0, out_spaces=None):
    return pl.pallas_call(
        kernel,
        out_shape=out_shapes,
        in_specs=[spec(SPACES[c]) for c in spaces],
        out_specs=tuple(spec(SPACES[c]) for c in out_spaces)
        if out_spaces
        else jax.tree.map(lambda _: spec(), out_shapes),
        scratch_shapes=scratch,
        compiler_params=pltpu.CompilerParams(vmem_limit_bytes=min(int(limit_mib * (1 << 20)), 67043328)),
        cost_estimate=pl.CostEstimate(flops=flops, bytes_accessed=1 << 20, transcendentals=trans),
        name=name,
    )


def poly(coeffs, u):
    out = coeffs[-1]
    for c in coeffs[-2::-1]:
        out = out * u + c
    return out


def green(scaled, strength):
    inverse = lax.rsqrt(scaled)
    turns = scaled * inverse
    magnitude = inverse * strength
    whole = (turns + ROUNDER) - ROUNDER
    frac = turns - whole
    u = frac * frac
    s = poly(SIN, u) * frac
    c = poly(COS, u)
    ms = magnitude * s
    return magnitude - ms * s, ms * c


def column(row):
    return jnp.broadcast_to(row, (128, 128)).T


def total(x):
    return jnp.broadcast_to(jnp.sum(x, keepdims=True), (1, 128))


def fold(x):
    out = x[0]
    for i in range(1, x.shape[0]):
        out = out + x[i]
    return out


def split_bf16(x):
    high = x.astype(bf16)
    return high, (x - high.astype(f32)).astype(bf16)


def iota(dims, dim):
    return lax.broadcasted_iota(jnp.int32, dims, dim)


def prepare_kernel(desired_hbm, points_hbm, send_ref, desired_ref, points_ref, sems):
    copies = [
        pltpu.make_async_copy(desired_hbm, desired_ref, sems.at[0]),
        pltpu.make_async_copy(points_hbm, points_ref, sems.at[1]),
    ]
    for copy in copies:
        copy.start()
    lanes = pl.ds(pl.multiple_of(lax.axis_index("ylo") * 128, 128), 128)
    for copy in copies:
        copy.wait()
    points = points_ref[:, lanes]
    for f in range(8):
        send_ref[f, 0:1, :] = desired_ref[0, f : f + 1, lanes]
        send_ref[f, 1:2, :] = desired_ref[1, f : f + 1, lanes]
        send_ref[f, 2:5, :] = points


def eval_green_kernel(wave_ref, eval_ref, high_ref, low_ref):
    kappa = wave_ref[0] * (0.5 / math.pi)
    strength = kappa * (1.0 / WALL)
    ex = column((front_gap + eval_ref[0:1, :] * depth_span) * kappa)
    ey = column((eval_ref[1:2, :] * side_span - 0.5 * side_span) * kappa)
    ez = column((eval_ref[2:3, :] * side_span - 0.5 * side_span) * kappa)
    lane = iota((1, 128), 1)
    dz = ez - (jnp.bitwise_and(lane, WALL - 1).astype(f32) - centre) * (wall_pitch * kappa)
    base = ex * ex + dz * dz

    def step(i, carry):
        wall_row = i * 2 + jnp.right_shift(lane, 6)
        wy = (wall_row.astype(f32) - centre) * (wall_pitch * kappa)
        lanes = pl.ds(pl.multiple_of(i * 128, 128), 128)
        for start in range(0, 128, 64):
            rows = slice(start, start + 64)
            dy = ey[rows] - wy
            real, imag = green(base[rows] + dy * dy, strength)
            for first, value in ((start, real), (128 + start, imag)):
                high = value.astype(bf16)
                high_ref[first : first + 64, lanes] = high
                low_ref[first : first + 64, lanes] = ((value - high.astype(f32)) * LOW_SCALE).astype(f8)
        return carry

    lax.fori_loop(0, 32, step, 0)


def first_kernel(wave_ref, got_ref, g_ref, send_ref, dz2_ref, rest_ref, acc_ref):
    kappa = wave_ref[0] * (0.5 / math.pi)
    strength = kappa * (1.0 / WALL)
    wz = (iota((WALL, 128), 0).astype(f32) - centre) * (wall_pitch * kappa)
    wy = ((iota((8, 128), 0) + lax.axis_index(BANKS) * 8).astype(f32) - centre) * (wall_pitch * kappa)
    for j in range(8):
        px = (front_gap + got_ref[j, 2:3, :] * depth_span) * kappa
        py = (got_ref[j, 3:4, :] * side_span - 0.5 * side_span) * kappa
        pz = (got_ref[j, 4:5, :] * side_span - 0.5 * side_span) * kappa
        dz = pz - wz
        dz2_ref[j] = dz * dz
        dy = py - wy
        rest_ref[j] = px * px + dy * dy
    size = 64

    def wall_row(r, carry):
        for start in range(0, WALL, size):
            rows = pl.ds(pl.multiple_of(r * WALL + start, size), size)

            def block(j, sums):
                real_sum, imag_sum = sums
                vr = got_ref[j, 0:1, :]
                vi = got_ref[j, 1:2, :]
                real, imag = green(
                    dz2_ref[j, start : start + size, :] + rest_ref[j, pl.ds(r, 1), :], strength
                )
                g_ref[j, 0, rows, :] = real
                g_ref[j, 1, rows, :] = imag
                real_sum = real_sum + (real * vr + imag * vi)
                imag_sum = imag_sum + (real * vi - imag * vr)
                return real_sum, imag_sum

            zero = jnp.zeros((size, 128), f32)
            real_sum, imag_sum = lax.fori_loop(0, 8, block, (zero, zero), unroll=8)
            acc_ref[0, rows, :] = real_sum
            acc_ref[1, rows, :] = imag_sum
        return carry

    lax.fori_loop(0, 8, wall_row, 0)
    rows = rows_of(acc_ref)
    for i in range(8):
        send_ref[i] = rows


def rows_of(acc_ref):
    rows = []
    for part in range(2):
        for blk in range(4):
            block = acc_ref[part, blk * 128 : blk * 128 + 128, :]
            rows.append(jnp.sum(block.T, axis=0, keepdims=True))
    return jnp.concatenate(rows, axis=0)


def forward(g_ref, rows, col_ref, out_ref):
    for part in range(2):
        for blk in range(4):
            i = part * 4 + blk
            col_ref[part, blk * 128 : blk * 128 + 128, :] = column(rows[i : i + 1, :])
    size = 64

    def step(t, carry):
        real_sum = jnp.zeros((8, 128), f32)
        imag_sum = jnp.zeros((8, 128), f32)
        for k in range(512 // size):
            at = slice(k * size, k * size + size)
            gr = g_ref[t, 0, at, :]
            gi = g_ref[t, 1, at, :]
            qr = col_ref[0, at, :]
            qi = col_ref[1, at, :]
            real_sum = real_sum + (gr * qr - gi * qi).reshape(size // 8, 8, 128).sum(axis=0)
            imag_sum = imag_sum + (gi * qr + gr * qi).reshape(size // 8, 8, 128).sum(axis=0)
        out_ref[pl.ds(t, 1), :] = jnp.sum(real_sum, axis=0, keepdims=True)
        out_ref[pl.ds(t + 8, 1), :] = jnp.sum(imag_sum, axis=0, keepdims=True)
        return carry

    lax.fori_loop(0, 8, step, 0)


def adjoint(g_ref, im, acc_ref):
    size = 128

    def chunk(k, carry):
        rows = pl.ds(pl.multiple_of(k * size, size), size)
        real_sum = jnp.zeros((size, 128), f32)
        imag_sum = jnp.zeros((size, 128), f32)
        for t in range(8):
            vr = im[t : t + 1, :]
            vi = im[8 + t : 9 + t, :]
            gr = g_ref[t, 0, rows, :]
            gi = g_ref[t, 1, rows, :]
            real_sum = real_sum + (gr * vr + gi * vi)
            imag_sum = imag_sum + (gr * vi - gi * vr)
        acc_ref[0, rows, :] = real_sum
        acc_ref[1, rows, :] = imag_sum
        return carry

    lax.fori_loop(0, 512 // size, chunk, 0)
    return rows_of(acc_ref)


def image_kernel(g_ref, got_ref, send_ref, own_ref, col_ref, im_ref):
    g0 = fold(got_ref)
    own_ref[...] = g0
    forward(g_ref, g0, col_ref, im_ref)
    im = im_ref[...]
    for i in range(8):
        send_ref[i, 0:16, :] = im
        send_ref[i, 16:24, :] = g0


def adjoint_kernel(g_ref, got_ref, send_ref, acc_ref):
    im = fold(got_ref[:, 0:16, :])
    rows = adjoint(g_ref, im, acc_ref)
    for i in range(8):
        send_ref[i, 0:8, :] = rows
        send_ref[i, 8:24, :] = im


def gathered_total(a, b):
    return total(fold(a * b))


def second_image_kernel(g_ref, got3_ref, got2_ref, g0_ref, send_ref, alpha_ref, col_ref, im_ref):
    all_g0 = got2_ref[:, 16:24, :]
    gamma = gathered_total(all_g0, all_g0)
    g0 = g0_ref[...]
    back = fold(got3_ref[:, 0:8, :])
    all_im0 = got3_ref[:, 8:24, :]
    norm = gathered_total(all_im0, all_im0)
    alpha = gamma / (norm + tikhonov * gamma)
    alpha_ref[0:1, :] = alpha
    alpha_ref[1:2, :] = gamma
    g1 = g0 - alpha * (back + tikhonov * g0)
    forward(g_ref, g1, col_ref, im_ref)
    im = im_ref[...]
    for i in range(8):
        send_ref[i, 0:16, :] = im
        send_ref[i, 16:24, :] = g1


def norm_kernel(got4_ref, got2_ref, alpha_ref, send_ref, scalar_ref):
    all_g0 = got2_ref[:, 16:24, :]
    all_g1 = got4_ref[:, 16:24, :]
    gamma0 = alpha_ref[1:2, :]
    gamma1 = gathered_total(all_g1, all_g1)
    cross = gathered_total(all_g1, all_g0)
    beta = gamma1 / gamma0
    im1 = fold(got4_ref[:, 0:16, :]) + beta * fold(got2_ref[:, 0:16, :])
    scalar_ref[0:1, :] = beta
    scalar_ref[1:2, :] = gamma1
    scalar_ref[2:3, :] = gamma1 + (2.0 * cross + beta * gamma0) * beta
    for i in range(8):
        send_ref[i] = im1


def drive_kernel(got5_ref, got3_ref, got2_ref, got4_ref, alpha_ref, scalar_ref, send_ref):
    alpha0 = alpha_ref[0:1, :]
    beta = scalar_ref[0:1, :]
    all_im1 = got5_ref[...]
    norm = gathered_total(all_im1, all_im1)
    alpha1 = scalar_ref[1:2, :] / (norm + tikhonov * scalar_ref[2:3, :])
    from_first = alpha0 + alpha1 * beta
    core = lax.axis_index("core")
    for k in range(4):
        bank = core * 4 + k
        rows = from_first * got2_ref[bank, 16:24, :] + alpha1 * got4_ref[bank, 16:24, :]
        for i in range(8):
            send_ref[i, 8 * k : 8 * k + 8, :] = rows
    for half in range(2):
        member = lax.axis_index(("zc", "yhi")) * 2 + half
        change = alpha0 * got3_ref[member, 8:24, :] + alpha1 * got5_ref[member]
        for i in range(8):
            send_ref[i, 32 + half : 33 + half, :] = change[i : i + 1, :]
            send_ref[i, 34 + half : 35 + half, :] = change[8 + i : 9 + i, :]


ROWS = 40


def of_fields(got_ref, row):
    return got_ref[pl.ds(row, 8, stride=ROWS), :]


def field_part(got_ref, half, high_ref, low_ref, cells_ref):
    first_cell = lax.axis_index(SPK) * 2
    cells = jnp.concatenate([cells_ref[pl.ds(first_cell + blk, 1), :] for blk in range(2)], axis=1)
    pick = jnp.where(iota((128, 256), 0) == jnp.bitwise_and(cells, 127), 1.0, 0.0).astype(bf16)
    line = iota((32, 256), 0)
    place = half * 16 + jnp.right_shift(line, 3) * 4 + jnp.bitwise_and(line, 3)
    right = place == jnp.right_shift(cells, 7)
    is_real = jnp.bitwise_and(line, 4) == 0
    masks = [jnp.where(right & is_real, 1.0, 0.0), jnp.where(right & ~is_real, 1.0, 0.0)]
    drives = [[], []]
    for f in range(8):
        x = got_ref[f * ROWS : f * ROWS + 32, :]
        high = x.astype(bf16)
        middle, low = split_bf16(x - high.astype(f32))
        three = jnp.concatenate([high, middle, low], axis=0)
        picked = jnp.dot(three, pick, preferred_element_type=f32)
        picked = picked[0:32] + picked[32:64] + picked[64:96]
        for part in range(2):
            drives[part].append(jnp.sum(picked * masks[part], axis=0, keepdims=True))
    out = jnp.zeros((32, 256), f32)
    fine = jnp.zeros((16, 256), f32)
    dims = (((1,), (1,)), ((), ()))
    for k in range(4):
        for pair in range(2):
            parts = [
                jnp.concatenate(
                    [of_fields(got_ref, k * 8 + part * 4 + pair * 2 + i) for i in range(2)], axis=1
                )
                for part in range(2)
            ]
            high, low = split_bf16(jnp.concatenate(parts, axis=0))
            both = jnp.concatenate([high, low], axis=0)
            lanes = pl.ds(pl.multiple_of(half * 2048 + (k * 2 + pair) * 256, 256), 256)
            out = out + lax.dot_general(both, high_ref[:, lanes], dims, preferred_element_type=f32)
            rest = low_ref[:, lanes].astype(bf16)
            fine = fine + lax.dot_general(high, rest, dims, preferred_element_type=f32)
    out = out[0:16, :] + out[16:32, :] + fine * (1.0 / LOW_SCALE)
    return [jnp.concatenate(rows, axis=0) for rows in drives], out


def near_field_kernel(got_ref, high_ref, low_ref, cells_ref, drives_ref, product_ref):
    drives, out = field_part(got_ref, lax.axis_index("core"), high_ref, low_ref, cells_ref)
    drives_ref[0] = drives[0]
    drives_ref[1] = drives[1]
    product_ref[...] = out


def far_field_kernel(
    got_ref, high_ref, low_ref, cells_ref, near_drives_ref, near_product_ref, desired_ref, near_ref,
    drives_ref, residual_ref, field_ref,
):
    for part in range(2):
        for half in range(2):
            lanes = slice(half * 128, half * 128 + 128)
            residual_ref[part, :, lanes] = desired_ref[part, :, lanes] - of_fields(
                near_ref, 32 + part * 2 + half
            )
    drives, out = field_part(got_ref, 1 - lax.axis_index("core"), high_ref, low_ref, cells_ref)
    drives_ref[0] = near_drives_ref[0] + drives[0]
    drives_ref[1] = near_drives_ref[1] + drives[1]
    out = near_product_ref[...] + out
    field_ref[0] = out[0:8, 0:128] - out[8:16, 128:256]
    field_ref[1] = out[0:8, 128:256] + out[8:16, 0:128]


def exchange(array, axes):
    return lax.all_to_all(array, axes, split_axis=0, concat_axis=0, tiled=True)


def local(desired, spk_cells, pt_cells, eval_cells, wavenumber):
    send0 = call(
        prepare_kernel,
        shape(8, 8, 128),
        [vmem((2, 8, 256), f32), vmem((3, 256), f32), pltpu.SemaphoreType.DMA((2,))],
        WHOLE, "aa", "prepare", 1024,
    )(desired, pt_cells)
    got0 = exchange(send0, FLD)
    g, send1 = call(
        first_kernel,
        (shape(8, 2, 512, 128), shape(8, 8, 128)),
        [vmem((8, 64, 128), f32), vmem((8, 8, 128), f32), vmem((2, 512, 128), f32)],
        8, "sv", "first", 524288 * 48, 524288,
    )(wavenumber, got0)
    got1 = exchange(send1, NEAR)
    send2, g0 = call(
        image_kernel,
        (shape(8, 24, 128), shape(8, 128)),
        [vmem((2, 512, 128), f32), vmem((16, 128), f32)], 8, "vv", "image", 524288 * 8,
    )(g, got1)
    got2 = exchange(send2, BANKS)
    send3 = call(
        adjoint_kernel, shape(8, 24, 128), [vmem((2, 512, 128), f32)], 8, "vv", "adjoint", 524288 * 8,
    )(g, got2)
    got3 = exchange(send3, NEAR)
    send4, alpha = call(
        second_image_kernel,
        (shape(8, 24, 128), shape(2, 128)),
        [vmem((2, 512, 128), f32), vmem((16, 128), f32)], 8, "vvvv", "second_image", 524288 * 8,
    )(g, got3, got2, g0)
    got4 = exchange(send4, BANKS)
    send5, scalars = call(
        norm_kernel, (shape(8, 16, 128), shape(3, 128)), [], 8, "vvv", "norm", 81920,
    )(got4, got2, alpha)
    got5 = exchange(send5, NEAR)
    send6 = call(
        drive_kernel, shape(8, ROWS, 128), [], 8, "vvvvvv", "drive", 81920,
    )(got5, got3, got2, got4, alpha, scalars)
    got6 = exchange(send6, FLD)
    eval_cells, got5 = lax.optimization_barrier((eval_cells, got5))
    high, low = call(
        eval_green_kernel,
        (shape(256, 4096, dtype=bf16), shape(256, 4096, dtype=f8)),
        [], 8, "sv", "eval_green", 524288 * 40, 524288,
    )(wavenumber, eval_cells)
    got6, high, low = lax.optimization_barrier((got6.reshape(8 * ROWS, 128), high, low))
    other = lax.ppermute(got6, "core", [(0, 1), (1, 0)])
    cells = spk_cells.reshape(32, 128)
    near_drives, product = call(
        near_field_kernel,
        (shape(2, 8, 256), shape(16, 256)),
        [], 8, "vvvv", "near_field", 524288 * 48,
    )(got6, high, low, cells)
    return call(
        far_field_kernel,
        (shape(2, 8, 256), shape(2, 8, 256), shape(2, 8, 128)),
        [], 8, "vvvvvvvv", "far_field", 524288 * 48,
    )(other, high, low, cells, near_drives, product, desired, got6)


def solution(mesh):
    split = Mesh(
        mesh.devices.reshape(2, 4, 2, 2, 4, 2, 2), ("ylo", "x", "core", "yhi", "za", "zb", "zc")
    )
    in_specs = (P(None, None, PTS), P(), P(None, PTS), P(None, SPK + PTS), P())
    out_specs = (P(None, None, SPK), P(None, None, PTS), P(None, None, SPK + PTS))
    return jax.shard_map(local, mesh=split, in_specs=in_specs, out_specs=out_specs, check_vma=False)
```

```python
import math

import jax
import jax.numpy as jnp
from jax import lax
from jax.experimental import pallas as pl
from jax.experimental.pallas import tpu as pltpu
from jax.sharding import Mesh
from jax.sharding import PartitionSpec as P

WALL = 64
SPK = ("ylo", "xhi", "xlo", "core")
PTS = ("yhi", "zhi", "zlo", "zb", "zc")
FLD = ("zb", "zlo", "zhi")
BANKS = ("core", "xlo", "xhi")
NEAR = ("zc", "yhi", "ylo")

wall_pitch = 0.05
front_gap = 0.5
depth_span = 3.15
side_span = 3.2
tikhonov = 0.1
centre = (WALL - 1) * 0.5

SIN = (4.442879676818848, -7.307816505432129, 3.5977742671966553, -0.7911993861198425)
COS = (-1.4142040014266968, 6.97763729095459, -5.715188026428223, 1.728213906288147)
ROUNDER = 12582912.0
LOW_SCALE = 4194304.0

f32 = jnp.float32
f8 = jnp.float8_e4m3fn
bf16 = jnp.bfloat16
vmem = pltpu.VMEM


def spec(space=pltpu.VMEM):
    return pl.BlockSpec(memory_space=space)


def shape(*dims, dtype=f32):
    return jax.ShapeDtypeStruct(dims, dtype)


WHOLE = 64
SPACES = {"s": pltpu.SMEM, "v": pltpu.VMEM, "a": pl.ANY, "h": pltpu.HBM}


def call(kernel, out_shapes, scratch, limit_mib, spaces, name, flops, trans=0, out_spaces=None):
    return pl.pallas_call(
        kernel,
        out_shape=out_shapes,
        in_specs=[spec(SPACES[c]) for c in spaces],
        out_specs=tuple(spec(SPACES[c]) for c in out_spaces)
        if out_spaces
        else jax.tree.map(lambda _: spec(), out_shapes),
        scratch_shapes=scratch,
        compiler_params=pltpu.CompilerParams(vmem_limit_bytes=min(int(limit_mib * (1 << 20)), 67043328)),
        cost_estimate=pl.CostEstimate(flops=flops, bytes_accessed=1 << 20, transcendentals=trans),
        name=name,
    )


def poly(coeffs, u):
    out = coeffs[-1]
    for c in coeffs[-2::-1]:
        out = out * u + c
    return out


def green(scaled, strength):
    inverse = lax.rsqrt(scaled)
    turns = scaled * inverse
    magnitude = inverse * strength
    whole = (turns + ROUNDER) - ROUNDER
    frac = turns - whole
    u = frac * frac
    s = poly(SIN, u) * frac
    c = poly(COS, u)
    ms = magnitude * s
    return magnitude - ms * s, ms * c


def column(row):
    return jnp.broadcast_to(row, (128, 128)).T


def total(x):
    return jnp.broadcast_to(jnp.sum(x, keepdims=True), (1, 128))


def fold(x):
    out = x[0]
    for i in range(1, x.shape[0]):
        out = out + x[i]
    return out


def split_bf16(x):
    high = x.astype(bf16)
    return high, (x - high.astype(f32)).astype(bf16)


def iota(dims, dim):
    return lax.broadcasted_iota(jnp.int32, dims, dim)


def prepare_kernel(desired_hbm, points_hbm, send_ref, desired_ref, points_ref, sems):
    copies = [
        pltpu.make_async_copy(desired_hbm, desired_ref, sems.at[0]),
        pltpu.make_async_copy(points_hbm, points_ref, sems.at[1]),
    ]
    for copy in copies:
        copy.start()
    lanes = pl.ds(pl.multiple_of(lax.axis_index("ylo") * 128, 128), 128)
    for copy in copies:
        copy.wait()
    points = points_ref[:, lanes]
    for f in range(8):
        send_ref[f, 0:1, :] = desired_ref[0, f : f + 1, lanes]
        send_ref[f, 1:2, :] = desired_ref[1, f : f + 1, lanes]
        send_ref[f, 2:5, :] = points


def eval_green_kernel(wave_ref, eval_ref, high_ref, low_ref):
    kappa = wave_ref[0] * (0.5 / math.pi)
    strength = kappa * (1.0 / WALL)
    ex = column((front_gap + eval_ref[0:1, :] * depth_span) * kappa)
    ey = column((eval_ref[1:2, :] * side_span - 0.5 * side_span) * kappa)
    ez = column((eval_ref[2:3, :] * side_span - 0.5 * side_span) * kappa)
    lane = iota((1, 128), 1)
    dz = ez - (jnp.bitwise_and(lane, WALL - 1).astype(f32) - centre) * (wall_pitch * kappa)
    base = ex * ex + dz * dz

    def step(i, carry):
        wall_row = i * 2 + jnp.right_shift(lane, 6)
        wy = (wall_row.astype(f32) - centre) * (wall_pitch * kappa)
        lanes = pl.ds(pl.multiple_of(i * 128, 128), 128)
        for start in range(0, 128, 64):
            rows = slice(start, start + 64)
            dy = ey[rows] - wy
            real, imag = green(base[rows] + dy * dy, strength)
            for first, value in ((start, real), (128 + start, imag)):
                high = value.astype(bf16)
                high_ref[first : first + 64, lanes] = high
                low_ref[first : first + 64, lanes] = ((value - high.astype(f32)) * LOW_SCALE).astype(f8)
        return carry

    lax.fori_loop(0, 32, step, 0)


def first_kernel(wave_ref, got_ref, g_ref, send_ref, dz2_ref, rest_ref, acc_ref):
    kappa = wave_ref[0] * (0.5 / math.pi)
    strength = kappa * (1.0 / WALL)
    wz = (iota((WALL, 128), 0).astype(f32) - centre) * (wall_pitch * kappa)
    wy = ((iota((8, 128), 0) + lax.axis_index(BANKS) * 8).astype(f32) - centre) * (wall_pitch * kappa)
    for j in range(8):
        px = (front_gap + got_ref[j, 2:3, :] * depth_span) * kappa
        py = (got_ref[j, 3:4, :] * side_span - 0.5 * side_span) * kappa
        pz = (got_ref[j, 4:5, :] * side_span - 0.5 * side_span) * kappa
        dz = pz - wz
        dz2_ref[j] = dz * dz
        dy = py - wy
        rest_ref[j] = px * px + dy * dy
    size = 64

    def wall_row(r, carry):
        for start in range(0, WALL, size):
            rows = pl.ds(pl.multiple_of(r * WALL + start, size), size)

            def block(j, sums):
                real_sum, imag_sum = sums
                vr = got_ref[j, 0:1, :]
                vi = got_ref[j, 1:2, :]
                real, imag = green(
                    dz2_ref[j, start : start + size, :] + rest_ref[j, pl.ds(r, 1), :], strength
                )
                g_ref[j, 0, rows, :] = real
                g_ref[j, 1, rows, :] = imag
                real_sum = real_sum + (real * vr + imag * vi)
                imag_sum = imag_sum + (real * vi - imag * vr)
                return real_sum, imag_sum

            zero = jnp.zeros((size, 128), f32)
            real_sum, imag_sum = lax.fori_loop(0, 8, block, (zero, zero), unroll=8)
            acc_ref[0, rows, :] = real_sum
            acc_ref[1, rows, :] = imag_sum
        return carry

    lax.fori_loop(0, 8, wall_row, 0)
    rows = rows_of(acc_ref)
    for i in range(8):
        send_ref[i] = rows


def rows_of(acc_ref):
    rows = []
    for part in range(2):
        for blk in range(4):
            block = acc_ref[part, blk * 128 : blk * 128 + 128, :]
            rows.append(jnp.sum(block.T, axis=0, keepdims=True))
    return jnp.concatenate(rows, axis=0)


def forward(g_ref, rows, col_ref, out_ref):
    for part in range(2):
        for blk in range(4):
            i = part * 4 + blk
            col_ref[part, blk * 128 : blk * 128 + 128, :] = column(rows[i : i + 1, :])
    size = 64

    def step(t, carry):
        real_sum = jnp.zeros((8, 128), f32)
        imag_sum = jnp.zeros((8, 128), f32)
        for k in range(512 // size):
            at = slice(k * size, k * size + size)
            gr = g_ref[t, 0, at, :]
            gi = g_ref[t, 1, at, :]
            qr = col_ref[0, at, :]
            qi = col_ref[1, at, :]
            real_sum = real_sum + (gr * qr - gi * qi).reshape(size // 8, 8, 128).sum(axis=0)
            imag_sum = imag_sum + (gi * qr + gr * qi).reshape(size // 8, 8, 128).sum(axis=0)
        out_ref[pl.ds(t, 1), :] = jnp.sum(real_sum, axis=0, keepdims=True)
        out_ref[pl.ds(t + 8, 1), :] = jnp.sum(imag_sum, axis=0, keepdims=True)
        return carry

    lax.fori_loop(0, 8, step, 0)


def adjoint(g_ref, im, acc_ref):
    size = 128

    def chunk(k, carry):
        rows = pl.ds(pl.multiple_of(k * size, size), size)
        real_sum = jnp.zeros((size, 128), f32)
        imag_sum = jnp.zeros((size, 128), f32)
        for t in range(8):
            vr = im[t : t + 1, :]
            vi = im[8 + t : 9 + t, :]
            gr = g_ref[t, 0, rows, :]
            gi = g_ref[t, 1, rows, :]
            real_sum = real_sum + (gr * vr + gi * vi)
            imag_sum = imag_sum + (gr * vi - gi * vr)
        acc_ref[0, rows, :] = real_sum
        acc_ref[1, rows, :] = imag_sum
        return carry

    lax.fori_loop(0, 512 // size, chunk, 0)
    return rows_of(acc_ref)


def image_kernel(g_ref, got_ref, send_ref, own_ref, col_ref, im_ref):
    g0 = fold(got_ref)
    own_ref[...] = g0
    forward(g_ref, g0, col_ref, im_ref)
    im = im_ref[...]
    for i in range(8):
        send_ref[i, 0:16, :] = im
        send_ref[i, 16:24, :] = g0


def adjoint_kernel(g_ref, got_ref, send_ref, acc_ref):
    im = fold(got_ref[:, 0:16, :])
    rows = adjoint(g_ref, im, acc_ref)
    for i in range(8):
        send_ref[i, 0:8, :] = rows
        send_ref[i, 8:24, :] = im


def gathered_total(a, b):
    return total(fold(a * b))


def second_image_kernel(g_ref, got3_ref, got2_ref, g0_ref, send_ref, alpha_ref, col_ref, im_ref):
    all_g0 = got2_ref[:, 16:24, :]
    gamma = gathered_total(all_g0, all_g0)
    g0 = g0_ref[...]
    back = fold(got3_ref[:, 0:8, :])
    all_im0 = got3_ref[:, 8:24, :]
    norm = gathered_total(all_im0, all_im0)
    alpha = gamma / (norm + tikhonov * gamma)
    alpha_ref[0:1, :] = alpha
    alpha_ref[1:2, :] = gamma
    g1 = g0 - alpha * (back + tikhonov * g0)
    forward(g_ref, g1, col_ref, im_ref)
    im = im_ref[...]
    for i in range(8):
        send_ref[i, 0:16, :] = im
        send_ref[i, 16:24, :] = g1


def norm_kernel(got4_ref, got2_ref, alpha_ref, send_ref, scalar_ref):
    all_g0 = got2_ref[:, 16:24, :]
    all_g1 = got4_ref[:, 16:24, :]
    gamma0 = alpha_ref[1:2, :]
    gamma1 = gathered_total(all_g1, all_g1)
    cross = gathered_total(all_g1, all_g0)
    beta = gamma1 / gamma0
    im1 = fold(got4_ref[:, 0:16, :]) + beta * fold(got2_ref[:, 0:16, :])
    scalar_ref[0:1, :] = beta
    scalar_ref[1:2, :] = gamma1
    scalar_ref[2:3, :] = gamma1 + (2.0 * cross + beta * gamma0) * beta
    for i in range(8):
        send_ref[i] = im1


def drive_kernel(got5_ref, got3_ref, got2_ref, got4_ref, alpha_ref, scalar_ref, send_ref):
    alpha0 = alpha_ref[0:1, :]
    beta = scalar_ref[0:1, :]
    all_im1 = got5_ref[...]
    norm = gathered_total(all_im1, all_im1)
    alpha1 = scalar_ref[1:2, :] / (norm + tikhonov * scalar_ref[2:3, :])
    from_first = alpha0 + alpha1 * beta
    core = lax.axis_index("core")
    for k in range(4):
        bank = core * 4 + k
        rows = from_first * got2_ref[bank, 16:24, :] + alpha1 * got4_ref[bank, 16:24, :]
        for i in range(8):
            send_ref[i, 8 * k : 8 * k + 8, :] = rows
    for half in range(2):
        member = lax.axis_index(("zc", "yhi")) * 2 + half
        change = alpha0 * got3_ref[member, 8:24, :] + alpha1 * got5_ref[member]
        for i in range(8):
            send_ref[i, 32 + half : 33 + half, :] = change[i : i + 1, :]
            send_ref[i, 34 + half : 35 + half, :] = change[8 + i : 9 + i, :]


ROWS = 40


def of_fields(got_ref, row):
    return got_ref[pl.ds(row, 8, stride=ROWS), :]


def field_part(got_ref, half, high_ref, low_ref, cells_ref):
    first_cell = lax.axis_index(SPK) * 2
    cells = jnp.concatenate([cells_ref[pl.ds(first_cell + blk, 1), :] for blk in range(2)], axis=1)
    pick = jnp.where(iota((128, 256), 0) == jnp.bitwise_and(cells, 127), 1.0, 0.0).astype(bf16)
    line = iota((32, 256), 0)
    place = half * 16 + jnp.right_shift(line, 3) * 4 + jnp.bitwise_and(line, 3)
    right = place == jnp.right_shift(cells, 7)
    is_real = jnp.bitwise_and(line, 4) == 0
    masks = [jnp.where(right & is_real, 1.0, 0.0), jnp.where(right & ~is_real, 1.0, 0.0)]
    drives = [[], []]
    for f in range(8):
        x = got_ref[f * ROWS : f * ROWS + 32, :]
        high = x.astype(bf16)
        middle, low = split_bf16(x - high.astype(f32))
        three = jnp.concatenate([high, middle, low], axis=0)
        picked = jnp.dot(three, pick, preferred_element_type=f32)
        picked = picked[0:32] + picked[32:64] + picked[64:96]
        for part in range(2):
            drives[part].append(jnp.sum(picked * masks[part], axis=0, keepdims=True))
    out = jnp.zeros((32, 256), f32)
    fine = jnp.zeros((16, 256), f32)
    dims = (((1,), (1,)), ((), ()))
    for k in range(4):
        for pair in range(2):
            parts = [
                jnp.concatenate(
                    [of_fields(got_ref, k * 8 + part * 4 + pair * 2 + i) for i in range(2)], axis=1
                )
                for part in range(2)
            ]
            high, low = split_bf16(jnp.concatenate(parts, axis=0))
            both = jnp.concatenate([high, low], axis=0)
            lanes = pl.ds(pl.multiple_of(half * 2048 + (k * 2 + pair) * 256, 256), 256)
            out = out + lax.dot_general(both, high_ref[:, lanes], dims, preferred_element_type=f32)
            rest = low_ref[:, lanes].astype(bf16)
            fine = fine + lax.dot_general(high, rest, dims, preferred_element_type=f32)
    out = out[0:16, :] + out[16:32, :] + fine * (1.0 / LOW_SCALE)
    return [jnp.concatenate(rows, axis=0) for rows in drives], out


def near_field_kernel(got_ref, high_ref, low_ref, cells_ref, drives_ref, product_ref):
    drives, out = field_part(got_ref, lax.axis_index("core"), high_ref, low_ref, cells_ref)
    drives_ref[0] = drives[0]
    drives_ref[1] = drives[1]
    product_ref[...] = out


def far_field_kernel(
    got_ref, high_ref, low_ref, cells_ref, near_drives_ref, near_product_ref, desired_ref, near_ref,
    drives_ref, residual_ref, field_ref,
):
    for part in range(2):
        for half in range(2):
            lanes = slice(half * 128, half * 128 + 128)
            residual_ref[part, :, lanes] = desired_ref[part, :, lanes] - of_fields(
                near_ref, 32 + part * 2 + half
            )
    drives, out = field_part(got_ref, 1 - lax.axis_index("core"), high_ref, low_ref, cells_ref)
    drives_ref[0] = near_drives_ref[0] + drives[0]
    drives_ref[1] = near_drives_ref[1] + drives[1]
    out = near_product_ref[...] + out
    field_ref[0] = out[0:8, 0:128] - out[8:16, 128:256]
    field_ref[1] = out[0:8, 128:256] + out[8:16, 0:128]


def exchange(array, axes):
    return lax.all_to_all(array, axes, split_axis=0, concat_axis=0, tiled=True)


def local(desired, spk_cells, pt_cells, eval_cells, wavenumber):
    send0 = call(
        prepare_kernel,
        shape(8, 8, 128),
        [vmem((2, 8, 256), f32), vmem((3, 256), f32), pltpu.SemaphoreType.DMA((2,))],
        WHOLE, "aa", "prepare", 1024,
    )(desired, pt_cells)
    got0 = exchange(send0, FLD)
    g, send1 = call(
        first_kernel,
        (shape(8, 2, 512, 128), shape(8, 8, 128)),
        [vmem((8, 64, 128), f32), vmem((8, 8, 128), f32), vmem((2, 512, 128), f32)],
        8, "sv", "first", 524288 * 48, 524288,
    )(wavenumber, got0)
    got1 = exchange(send1, NEAR)
    send2, g0 = call(
        image_kernel,
        (shape(8, 24, 128), shape(8, 128)),
        [vmem((2, 512, 128), f32), vmem((16, 128), f32)], 8, "vv", "image", 524288 * 8,
    )(g, got1)
    got2 = exchange(send2, BANKS)
    send3 = call(
        adjoint_kernel, shape(8, 24, 128), [vmem((2, 512, 128), f32)], 8, "vv", "adjoint", 524288 * 8,
    )(g, got2)
    got3 = exchange(send3, NEAR)
    send4, alpha = call(
        second_image_kernel,
        (shape(8, 24, 128), shape(2, 128)),
        [vmem((2, 512, 128), f32), vmem((16, 128), f32)], 8, "vvvv", "second_image", 524288 * 8,
    )(g, got3, got2, g0)
    got4 = exchange(send4, BANKS)
    send5, scalars = call(
        norm_kernel, (shape(8, 16, 128), shape(3, 128)), [], 8, "vvv", "norm", 81920,
    )(got4, got2, alpha)
    got5 = exchange(send5, NEAR)
    send6 = call(
        drive_kernel, shape(8, ROWS, 128), [], 8, "vvvvvv", "drive", 81920,
    )(got5, got3, got2, got4, alpha, scalars)
    got6 = exchange(send6, FLD)
    eval_cells, got5 = lax.optimization_barrier((eval_cells, got5))
    high, low = call(
        eval_green_kernel,
        (shape(256, 4096, dtype=bf16), shape(256, 4096, dtype=f8)),
        [], 8, "sv", "eval_green", 524288 * 40, 524288,
    )(wavenumber, eval_cells)
    got6, high, low = lax.optimization_barrier((got6.reshape(8 * ROWS, 128), high, low))
    other = lax.ppermute(got6, "core", [(0, 1), (1, 0)])
    cells = spk_cells.reshape(32, 128)
    near_drives, product = call(
        near_field_kernel,
        (shape(2, 8, 256), shape(16, 256)),
        [], 8, "vvvv", "near_field", 524288 * 48,
    )(got6, high, low, cells)
    return call(
        far_field_kernel,
        (shape(2, 8, 256), shape(2, 8, 256), shape(2, 8, 128)),
        [], 8, "vvvvvvvv", "far_field", 524288 * 48,
    )(other, high, low, cells, near_drives, product, desired, got6)


def solution(mesh):
    split = Mesh(mesh.devices.reshape((2,) * 9), SPK + PTS)
    in_specs = (P(None, None, PTS), P(), P(None, PTS), P(None, SPK + PTS), P())
    out_specs = (P(None, None, SPK), P(None, None, PTS), P(None, None, SPK + PTS))
    return jax.shard_map(local, mesh=split, in_specs=in_specs, out_specs=out_specs, check_vma=False)
```

```python
import math

import jax
import jax.numpy as jnp
from jax import lax
from jax.experimental import pallas as pl
from jax.experimental.pallas import tpu as pltpu
from jax.sharding import Mesh
from jax.sharding import PartitionSpec as P

WALL = 64
SPK = ("ylo", "xhi", "xlo", "core")
PTS = ("yhi", "zhi", "zlo", "zb", "zc")
FLD = ("zb", "zlo", "zhi")
BANKS = ("core", "xlo", "xhi")
NEAR = ("ylo", "zc", "yhi")

wall_pitch = 0.05
front_gap = 0.5
depth_span = 3.15
side_span = 3.2
tikhonov = 0.1
centre = (WALL - 1) * 0.5

SIN = (4.442879676818848, -7.307816505432129, 3.5977742671966553, -0.7911993861198425)
COS = (-1.4142040014266968, 6.97763729095459, -5.715188026428223, 1.728213906288147)
ROUNDER = 12582912.0
LOW_SCALE = 4194304.0

f32 = jnp.float32
f8 = jnp.float8_e4m3fn
bf16 = jnp.bfloat16
vmem = pltpu.VMEM


def spec(space=pltpu.VMEM):
    return pl.BlockSpec(memory_space=space)


def shape(*dims, dtype=f32):
    return jax.ShapeDtypeStruct(dims, dtype)


WHOLE = 64
SPACES = {"s": pltpu.SMEM, "v": pltpu.VMEM, "a": pl.ANY, "h": pltpu.HBM}


def call(kernel, out_shapes, scratch, limit_mib, spaces, name, flops, trans=0, out_spaces=None):
    return pl.pallas_call(
        kernel,
        out_shape=out_shapes,
        in_specs=[spec(SPACES[c]) for c in spaces],
        out_specs=tuple(spec(SPACES[c]) for c in out_spaces)
        if out_spaces
        else jax.tree.map(lambda _: spec(), out_shapes),
        scratch_shapes=scratch,
        compiler_params=pltpu.CompilerParams(vmem_limit_bytes=min(int(limit_mib * (1 << 20)), 67043328)),
        cost_estimate=pl.CostEstimate(flops=flops, bytes_accessed=1 << 20, transcendentals=trans),
        name=name,
    )


def poly(coeffs, u):
    out = coeffs[-1]
    for c in coeffs[-2::-1]:
        out = out * u + c
    return out


def green(scaled, strength):
    inverse = lax.rsqrt(scaled)
    turns = scaled * inverse
    magnitude = inverse * strength
    whole = (turns + ROUNDER) - ROUNDER
    frac = turns - whole
    u = frac * frac
    s = poly(SIN, u) * frac
    c = poly(COS, u)
    ms = magnitude * s
    return magnitude - ms * s, ms * c


def column(row):
    return jnp.broadcast_to(row, (128, 128)).T


def total(x):
    return jnp.broadcast_to(jnp.sum(x, keepdims=True), (1, 128))


def fold(x):
    out = x[0]
    for i in range(1, x.shape[0]):
        out = out + x[i]
    return out


def split_bf16(x):
    high = x.astype(bf16)
    return high, (x - high.astype(f32)).astype(bf16)


def iota(dims, dim):
    return lax.broadcasted_iota(jnp.int32, dims, dim)


def prepare_kernel(desired_hbm, points_hbm, send_ref, desired_ref, points_ref, sems):
    copies = [
        pltpu.make_async_copy(desired_hbm, desired_ref, sems.at[0]),
        pltpu.make_async_copy(points_hbm, points_ref, sems.at[1]),
    ]
    for copy in copies:
        copy.start()
    lanes = pl.ds(pl.multiple_of(lax.axis_index("ylo") * 128, 128), 128)
    for copy in copies:
        copy.wait()
    points = points_ref[:, lanes]
    for f in range(8):
        send_ref[f, 0:1, :] = desired_ref[0, f : f + 1, lanes]
        send_ref[f, 1:2, :] = desired_ref[1, f : f + 1, lanes]
        send_ref[f, 2:5, :] = points


def eval_green_kernel(wave_ref, eval_ref, high_ref, low_ref):
    kappa = wave_ref[0] * (0.5 / math.pi)
    strength = kappa * (1.0 / WALL)
    ex = column((front_gap + eval_ref[0:1, :] * depth_span) * kappa)
    ey = column((eval_ref[1:2, :] * side_span - 0.5 * side_span) * kappa)
    ez = column((eval_ref[2:3, :] * side_span - 0.5 * side_span) * kappa)
    lane = iota((1, 128), 1)
    dz = ez - (jnp.bitwise_and(lane, WALL - 1).astype(f32) - centre) * (wall_pitch * kappa)
    base = ex * ex + dz * dz

    def step(i, carry):
        wall_row = i * 2 + jnp.right_shift(lane, 6)
        wy = (wall_row.astype(f32) - centre) * (wall_pitch * kappa)
        lanes = pl.ds(pl.multiple_of(i * 128, 128), 128)
        for start in range(0, 128, 64):
            rows = slice(start, start + 64)
            dy = ey[rows] - wy
            real, imag = green(base[rows] + dy * dy, strength)
            for first, value in ((start, real), (128 + start, imag)):
                high = value.astype(bf16)
                high_ref[first : first + 64, lanes] = high
                low_ref[first : first + 64, lanes] = ((value - high.astype(f32)) * LOW_SCALE).astype(f8)
        return carry

    lax.fori_loop(0, 32, step, 0)


def first_kernel(wave_ref, got_ref, g_ref, send_ref, dz2_ref, rest_ref, acc_ref):
    kappa = wave_ref[0] * (0.5 / math.pi)
    strength = kappa * (1.0 / WALL)
    wz = (iota((WALL, 128), 0).astype(f32) - centre) * (wall_pitch * kappa)
    wy = ((iota((8, 128), 0) + lax.axis_index(BANKS) * 8).astype(f32) - centre) * (wall_pitch * kappa)
    for j in range(8):
        px = (front_gap + got_ref[j, 2:3, :] * depth_span) * kappa
        py = (got_ref[j, 3:4, :] * side_span - 0.5 * side_span) * kappa
        pz = (got_ref[j, 4:5, :] * side_span - 0.5 * side_span) * kappa
        dz = pz - wz
        dz2_ref[j] = dz * dz
        dy = py - wy
        rest_ref[j] = px * px + dy * dy
    size = 64

    def wall_row(r, carry):
        for start in range(0, WALL, size):
            rows = pl.ds(pl.multiple_of(r * WALL + start, size), size)

            def block(j, sums):
                real_sum, imag_sum = sums
                vr = got_ref[j, 0:1, :]
                vi = got_ref[j, 1:2, :]
                real, imag = green(
                    dz2_ref[j, start : start + size, :] + rest_ref[j, pl.ds(r, 1), :], strength
                )
                g_ref[j, 0, rows, :] = real
                g_ref[j, 1, rows, :] = imag
                real_sum = real_sum + (real * vr + imag * vi)
                imag_sum = imag_sum + (real * vi - imag * vr)
                return real_sum, imag_sum

            zero = jnp.zeros((size, 128), f32)
            real_sum, imag_sum = lax.fori_loop(0, 8, block, (zero, zero), unroll=8)
            acc_ref[0, rows, :] = real_sum
            acc_ref[1, rows, :] = imag_sum
        return carry

    lax.fori_loop(0, 8, wall_row, 0)
    rows = rows_of(acc_ref)
    for i in range(8):
        send_ref[i] = rows


def rows_of(acc_ref):
    rows = []
    for part in range(2):
        for blk in range(4):
            block = acc_ref[part, blk * 128 : blk * 128 + 128, :]
            rows.append(jnp.sum(block.T, axis=0, keepdims=True))
    return jnp.concatenate(rows, axis=0)


def forward(g_ref, rows, col_ref, out_ref):
    for part in range(2):
        for blk in range(4):
            i = part * 4 + blk
            col_ref[part, blk * 128 : blk * 128 + 128, :] = column(rows[i : i + 1, :])
    size = 64

    def step(t, carry):
        real_sum = jnp.zeros((8, 128), f32)
        imag_sum = jnp.zeros((8, 128), f32)
        for k in range(512 // size):
            at = slice(k * size, k * size + size)
            gr = g_ref[t, 0, at, :]
            gi = g_ref[t, 1, at, :]
            qr = col_ref[0, at, :]
            qi = col_ref[1, at, :]
            real_sum = real_sum + (gr * qr - gi * qi).reshape(size // 8, 8, 128).sum(axis=0)
            imag_sum = imag_sum + (gi * qr + gr * qi).reshape(size // 8, 8, 128).sum(axis=0)
        out_ref[pl.ds(t, 1), :] = jnp.sum(real_sum, axis=0, keepdims=True)
        out_ref[pl.ds(t + 8, 1), :] = jnp.sum(imag_sum, axis=0, keepdims=True)
        return carry

    lax.fori_loop(0, 8, step, 0)


def adjoint(g_ref, im, acc_ref):
    size = 128

    def chunk(k, carry):
        rows = pl.ds(pl.multiple_of(k * size, size), size)
        real_sum = jnp.zeros((size, 128), f32)
        imag_sum = jnp.zeros((size, 128), f32)
        for t in range(8):
            vr = im[t : t + 1, :]
            vi = im[8 + t : 9 + t, :]
            gr = g_ref[t, 0, rows, :]
            gi = g_ref[t, 1, rows, :]
            real_sum = real_sum + (gr * vr + gi * vi)
            imag_sum = imag_sum + (gr * vi - gi * vr)
        acc_ref[0, rows, :] = real_sum
        acc_ref[1, rows, :] = imag_sum
        return carry

    lax.fori_loop(0, 512 // size, chunk, 0)
    return rows_of(acc_ref)


def image_kernel(g_ref, got_ref, send_ref, own_ref, col_ref, im_ref):
    g0 = fold(got_ref)
    own_ref[...] = g0
    forward(g_ref, g0, col_ref, im_ref)
    im = im_ref[...]
    for i in range(8):
        send_ref[i, 0:16, :] = im
        send_ref[i, 16:24, :] = g0


def adjoint_kernel(g_ref, got_ref, send_ref, acc_ref):
    im = fold(got_ref[:, 0:16, :])
    rows = adjoint(g_ref, im, acc_ref)
    for i in range(8):
        send_ref[i, 0:8, :] = rows
        send_ref[i, 8:24, :] = im


def gathered_total(a, b):
    return total(fold(a * b))


def second_image_kernel(g_ref, got3_ref, got2_ref, g0_ref, send_ref, alpha_ref, col_ref, im_ref):
    all_g0 = got2_ref[:, 16:24, :]
    gamma = gathered_total(all_g0, all_g0)
    g0 = g0_ref[...]
    back = fold(got3_ref[:, 0:8, :])
    all_im0 = got3_ref[:, 8:24, :]
    norm = gathered_total(all_im0, all_im0)
    alpha = gamma / (norm + tikhonov * gamma)
    alpha_ref[0:1, :] = alpha
    alpha_ref[1:2, :] = gamma
    g1 = g0 - alpha * (back + tikhonov * g0)
    forward(g_ref, g1, col_ref, im_ref)
    im = im_ref[...]
    for i in range(8):
        send_ref[i, 0:16, :] = im
        send_ref[i, 16:24, :] = g1


def norm_kernel(got4_ref, got2_ref, alpha_ref, send_ref, scalar_ref):
    all_g0 = got2_ref[:, 16:24, :]
    all_g1 = got4_ref[:, 16:24, :]
    gamma0 = alpha_ref[1:2, :]
    gamma1 = gathered_total(all_g1, all_g1)
    cross = gathered_total(all_g1, all_g0)
    beta = gamma1 / gamma0
    im1 = fold(got4_ref[:, 0:16, :]) + beta * fold(got2_ref[:, 0:16, :])
    scalar_ref[0:1, :] = beta
    scalar_ref[1:2, :] = gamma1
    scalar_ref[2:3, :] = gamma1 + (2.0 * cross + beta * gamma0) * beta
    for i in range(8):
        send_ref[i] = im1


def drive_kernel(got5_ref, got3_ref, got2_ref, got4_ref, alpha_ref, scalar_ref, send_ref):
    alpha0 = alpha_ref[0:1, :]
    beta = scalar_ref[0:1, :]
    all_im1 = got5_ref[...]
    norm = gathered_total(all_im1, all_im1)
    alpha1 = scalar_ref[1:2, :] / (norm + tikhonov * scalar_ref[2:3, :])
    from_first = alpha0 + alpha1 * beta
    core = lax.axis_index("core")
    for k in range(4):
        bank = core * 4 + k
        rows = from_first * got2_ref[bank, 16:24, :] + alpha1 * got4_ref[bank, 16:24, :]
        for i in range(8):
            send_ref[i, 8 * k : 8 * k + 8, :] = rows
    for half in range(2):
        member = half * 4 + lax.axis_index(("zc", "yhi"))
        change = alpha0 * got3_ref[member, 8:24, :] + alpha1 * got5_ref[member]
        for i in range(8):
            send_ref[i, 32 + half : 33 + half, :] = change[i : i + 1, :]
            send_ref[i, 34 + half : 35 + half, :] = change[8 + i : 9 + i, :]


ROWS = 40


def of_fields(got_ref, row):
    return got_ref[pl.ds(row, 8, stride=ROWS), :]


def field_part(got_ref, half, high_ref, low_ref, cells_ref):
    first_cell = lax.axis_index(SPK) * 2
    cells = jnp.concatenate([cells_ref[pl.ds(first_cell + blk, 1), :] for blk in range(2)], axis=1)
    pick = jnp.where(iota((128, 256), 0) == jnp.bitwise_and(cells, 127), 1.0, 0.0).astype(bf16)
    line = iota((32, 256), 0)
    place = half * 16 + jnp.right_shift(line, 3) * 4 + jnp.bitwise_and(line, 3)
    right = place == jnp.right_shift(cells, 7)
    is_real = jnp.bitwise_and(line, 4) == 0
    masks = [jnp.where(right & is_real, 1.0, 0.0), jnp.where(right & ~is_real, 1.0, 0.0)]
    drives = [[], []]
    for f in range(8):
        x = got_ref[f * ROWS : f * ROWS + 32, :]
        high = x.astype(bf16)
        middle, low = split_bf16(x - high.astype(f32))
        three = jnp.concatenate([high, middle, low], axis=0)
        picked = jnp.dot(three, pick, preferred_element_type=f32)
        picked = picked[0:32] + picked[32:64] + picked[64:96]
        for part in range(2):
            drives[part].append(jnp.sum(picked * masks[part], axis=0, keepdims=True))
    out = jnp.zeros((32, 256), f32)
    fine = jnp.zeros((16, 256), f32)
    dims = (((1,), (1,)), ((), ()))
    for k in range(4):
        for pair in range(2):
            parts = [
                jnp.concatenate(
                    [of_fields(got_ref, k * 8 + part * 4 + pair * 2 + i) for i in range(2)], axis=1
                )
                for part in range(2)
            ]
            high, low = split_bf16(jnp.concatenate(parts, axis=0))
            both = jnp.concatenate([high, low], axis=0)
            lanes = pl.ds(pl.multiple_of(half * 2048 + (k * 2 + pair) * 256, 256), 256)
            out = out + lax.dot_general(both, high_ref[:, lanes], dims, preferred_element_type=f32)
            rest = low_ref[:, lanes].astype(bf16)
            fine = fine + lax.dot_general(high, rest, dims, preferred_element_type=f32)
    out = out[0:16, :] + out[16:32, :] + fine * (1.0 / LOW_SCALE)
    return [jnp.concatenate(rows, axis=0) for rows in drives], out


def near_field_kernel(got_ref, high_ref, low_ref, cells_ref, drives_ref, product_ref):
    drives, out = field_part(got_ref, lax.axis_index("core"), high_ref, low_ref, cells_ref)
    drives_ref[0] = drives[0]
    drives_ref[1] = drives[1]
    product_ref[...] = out


def far_field_kernel(
    got_ref, high_ref, low_ref, cells_ref, near_drives_ref, near_product_ref, desired_ref, near_ref,
    drives_ref, residual_ref, field_ref,
):
    for part in range(2):
        for half in range(2):
            lanes = slice(half * 128, half * 128 + 128)
            residual_ref[part, :, lanes] = desired_ref[part, :, lanes] - of_fields(
                near_ref, 32 + part * 2 + half
            )
    drives, out = field_part(got_ref, 1 - lax.axis_index("core"), high_ref, low_ref, cells_ref)
    drives_ref[0] = near_drives_ref[0] + drives[0]
    drives_ref[1] = near_drives_ref[1] + drives[1]
    out = near_product_ref[...] + out
    field_ref[0] = out[0:8, 0:128] - out[8:16, 128:256]
    field_ref[1] = out[0:8, 128:256] + out[8:16, 0:128]


def exchange(array, axes):
    return lax.all_to_all(array, axes, split_axis=0, concat_axis=0, tiled=True)


def local(desired, spk_cells, pt_cells, eval_cells, wavenumber):
    send0 = call(
        prepare_kernel,
        shape(8, 8, 128),
        [vmem((2, 8, 256), f32), vmem((3, 256), f32), pltpu.SemaphoreType.DMA((2,))],
        WHOLE, "aa", "prepare", 1024,
    )(desired, pt_cells)
    got0 = exchange(send0, FLD)
    g, send1 = call(
        first_kernel,
        (shape(8, 2, 512, 128), shape(8, 8, 128)),
        [vmem((8, 64, 128), f32), vmem((8, 8, 128), f32), vmem((2, 512, 128), f32)],
        8, "sv", "first", 524288 * 48, 524288,
    )(wavenumber, got0)
    got1 = exchange(send1, NEAR)
    send2, g0 = call(
        image_kernel,
        (shape(8, 24, 128), shape(8, 128)),
        [vmem((2, 512, 128), f32), vmem((16, 128), f32)], 8, "vv", "image", 524288 * 8,
    )(g, got1)
    got2 = exchange(send2, BANKS)
    send3 = call(
        adjoint_kernel, shape(8, 24, 128), [vmem((2, 512, 128), f32)], 8, "vv", "adjoint", 524288 * 8,
    )(g, got2)
    got3 = exchange(send3, NEAR)
    send4, alpha = call(
        second_image_kernel,
        (shape(8, 24, 128), shape(2, 128)),
        [vmem((2, 512, 128), f32), vmem((16, 128), f32)], 8, "vvvv", "second_image", 524288 * 8,
    )(g, got3, got2, g0)
    got4 = exchange(send4, BANKS)
    send5, scalars = call(
        norm_kernel, (shape(8, 16, 128), shape(3, 128)), [], 8, "vvv", "norm", 81920,
    )(got4, got2, alpha)
    got5 = exchange(send5, NEAR)
    send6 = call(
        drive_kernel, shape(8, ROWS, 128), [], 8, "vvvvvv", "drive", 81920,
    )(got5, got3, got2, got4, alpha, scalars)
    got6 = exchange(send6, FLD)
    eval_cells, got5 = lax.optimization_barrier((eval_cells, got5))
    high, low = call(
        eval_green_kernel,
        (shape(256, 4096, dtype=bf16), shape(256, 4096, dtype=f8)),
        [], 8, "sv", "eval_green", 524288 * 40, 524288,
    )(wavenumber, eval_cells)
    got6, high, low = lax.optimization_barrier((got6.reshape(8 * ROWS, 128), high, low))
    other = lax.ppermute(got6, "core", [(0, 1), (1, 0)])
    cells = spk_cells.reshape(32, 128)
    near_drives, product = call(
        near_field_kernel,
        (shape(2, 8, 256), shape(16, 256)),
        [], 8, "vvvv", "near_field", 524288 * 48,
    )(got6, high, low, cells)
    return call(
        far_field_kernel,
        (shape(2, 8, 256), shape(2, 8, 256), shape(2, 8, 128)),
        [], 8, "vvvvvvvv", "far_field", 524288 * 48,
    )(other, high, low, cells, near_drives, product, desired, got6)


def solution(mesh):
    split = Mesh(mesh.devices.reshape((2,) * 9), SPK + PTS)
    in_specs = (P(None, None, PTS), P(), P(None, PTS), P(None, SPK + PTS), P())
    out_specs = (P(None, None, SPK), P(None, None, PTS), P(None, None, SPK + PTS))
    return jax.shard_map(local, mesh=split, in_specs=in_specs, out_specs=out_specs, check_vma=False)
```
